512 devices in a mesh: tm: 16 (over y, core), lat: 4 (over x), lon: 8 (over z).
Axes of the slice: x: 4, y: 8, z: 8, core: 2. Of those that a mesh axis runs over, the one named last changes fastest.
Arguments:
- residuals: bfloat16 [1024, 180, 1024], P('tm', 'lat', 'lon'), may hold values from -10 to 10
- diffusivity: float32 [180, 1024], P('lat', 'lon'), may hold values from 0.03 to 0.24
Outputs:
- projected: bfloat16 [1024, 180, 1024], P('tm', 'lat', 'lon')
The draws below stay inside these ranges and needn't reach their ends.
All inputs are finite; a program needn't handle non-finite values.
Results may differ from the reference program's by a relative error of at most 0.019.
Values may be sent and summed in bfloat16 or wider, within the bound.
A program may use at most 64 MiB of HBM per device.

```python
import math
import jax
import jax.numpy as jnp
from jax import lax

SNAP_DEV = 64
RANK = 32
PASSES = 4
POWER = 3
SNAPS = 1024
NLAT = 180
NLON = 1024
LEVELS = 4
N_TM = 16


def draw_residuals(key, part):
    keys = jax.random.split(jax.random.fold_in(key, 11), 4)
    count = 2 * RANK
    amplitude = jnp.exp(jax.random.uniform(keys[0], (count,), jnp.float32, 0.0, math.log(2.0)))
    coefs = jax.random.normal(keys[1], (SNAPS, count), jnp.float32)
    patterns = jax.random.normal(keys[2], (count, NLAT, NLON), jnp.float32)
    noise = jax.random.normal(keys[3], (SNAPS, NLAT * NLON), jnp.float32)
    rise = math.log(4.0)
    rows = (jnp.arange(NLAT).astype(jnp.float32) + 0.5) / NLAT
    centers = (jnp.arange(count).astype(jnp.float32) + 0.5) / count
    envelope = jnp.exp(-((rows[None, :] - centers[:, None]) / 0.15) ** 2)
    gain = jnp.exp(rise * rows)
    shaped = patterns * (envelope * gain[None, :])[:, :, None]
    signal = jnp.dot(coefs * amplitude[None, :] / math.sqrt(0.3 * count), shaped.reshape(count, NLAT * NLON), precision=lax.Precision.HIGHEST)
    values = jnp.clip(signal + 0.18 * noise, -10.0, 10.0)
    return values.reshape(SNAPS, NLAT, NLON).astype(jnp.bfloat16)


def block_scale(own_key, shape, shards, smallest, high):
    level, own = 1.0, jax.random.fold_in(own_key, 6)
    for axis_at, shards_of in shards:
        draws = jnp.exp(jax.random.uniform(jax.random.fold_in(own, axis_at), (shards_of,), jnp.float32, smallest / len(shards), high / len(shards)))
        level = level * jnp.repeat(draws, shape[axis_at] // shards_of).reshape([-1 if axis == axis_at else 1 for axis in range(len(shape))])
    return level


def setup_inputs(seed: int = 0) -> dict:
    key_of = jax.random.split(jax.random.key(seed), 3)
    return {
        "residuals": draw_residuals(jax.random.fold_in(key_of[2], 71), 0),
        "diffusivity": jnp.clip(jnp.exp(math.log(0.24) - 2.0794415 * jax.random.uniform(key_of[1], (NLAT, NLON), jnp.float32) ** block_scale(key_of[1], (NLAT, NLON), ((0, 4), (1, 8)), -0.2, 0.2)), 0.03, 0.24),
    }


exact_precision = lax.Precision.HIGHEST

def extend_grid(values):
    wrapped = jnp.concatenate([values[:, :, -1:], values, values[:, :, :1]], axis=2)
    border = jnp.zeros((wrapped.shape[0], 1, wrapped.shape[2]), jnp.float32)
    return jnp.concatenate([border, wrapped, border], axis=1)

def stencil(current, coeffs):
    center = current[:, 1:-1, 1:-1]
    middle = coeffs[:, 1:-1, 1:-1]
    northward = 0.5 * (middle + coeffs[:, :-2, 1:-1]) * (current[:, :-2, 1:-1] - center)
    southward = 0.5 * (middle + coeffs[:, 2:, 1:-1]) * (current[:, 2:, 1:-1] - center)
    westward = 0.5 * (middle + coeffs[:, 1:-1, :-2]) * (current[:, 1:-1, :-2] - center)
    eastward = 0.5 * (middle + coeffs[:, 1:-1, 2:]) * (current[:, 1:-1, 2:] - center)
    return center + (northward + southward + westward + eastward)

def orthonormal(block):
    inner = jnp.dot(block.T, block, precision=exact_precision)
    lower = jnp.linalg.cholesky(inner)
    return jax.scipy.linalg.solve_triangular(lower, block.T, lower=True).T

def top_space(gram):
    basis = orthonormal(gram[:, :RANK])
    for step_index in range(POWER):
        basis = orthonormal(jnp.dot(gram, basis, precision=exact_precision))
    return basis

def mode_block(stacked, gram):
    basis = top_space(gram).astype(jnp.bfloat16)
    modes = jnp.dot(basis.T.astype(jnp.float32), stacked.astype(jnp.float32), preferred_element_type=jnp.float32).astype(jnp.bfloat16)
    return (basis, modes)

def reference(residuals, diffusivity):
    coeffs = extend_grid(diffusivity[None])
    rows = jnp.arange(NLAT).astype(jnp.float32)
    latitude = (rows + 0.5) * math.pi / NLAT - math.pi / 2
    scale = jnp.sqrt(jnp.cos(latitude))

    def one_group(block):
        current = block.astype(jnp.float32)
        for pass_index in range(PASSES):
            current = stencil(extend_grid(current), coeffs)
        weighted = (current * scale[None, :, None]).astype(jnp.bfloat16).reshape(SNAP_DEV, NLAT * NLON)
        gram = jnp.dot(weighted.astype(jnp.float32), weighted.T.astype(jnp.float32), preferred_element_type=jnp.float32)
        basis, modes = mode_block(weighted, gram)
        return (weighted, modes)
    weighted_all, blocks = lax.map(one_group, residuals.reshape(N_TM, SNAP_DEV, NLAT, NLON))

    def merge_pair(stacked):
        gram = jnp.dot(stacked.astype(jnp.float32), stacked.T.astype(jnp.float32), preferred_element_type=jnp.float32)
        basis, modes = mode_block(stacked, gram)
        return (basis, modes, gram)
    for level_index in range(LEVELS):
        count = blocks.shape[0] // 2
        basis_all, blocks, gram_all = lax.map(merge_pair, blocks.reshape(count, 2 * RANK, NLAT * NLON))
    final = blocks[0]
    basis_f = basis_all[0].astype(jnp.float32)
    curvature = jnp.dot(basis_f.T, jnp.dot(gram_all[0], basis_f, precision=exact_precision), precision=exact_precision)
    factor = jnp.linalg.cholesky(curvature)

    def project(weighted):
        coef = jnp.dot(weighted.astype(jnp.float32), final.T.astype(jnp.float32), preferred_element_type=jnp.float32)
        solved = jax.scipy.linalg.cho_solve((factor, True), coef.T).T.astype(jnp.bfloat16)
        return jnp.dot(solved.astype(jnp.float32), final.astype(jnp.float32), preferred_element_type=jnp.float32).astype(jnp.bfloat16)
    projected = lax.map(project, weighted_all)
    return projected.reshape(SNAPS, NLAT, NLON)
```

```python
import functools
import math

import jax
import jax.numpy as jnp
from jax import lax
from jax.experimental import pallas as pl
from jax.experimental.pallas import tpu as pltpu
from jax.sharding import PartitionSpec as P

RANK = 32
PASSES = 4
POWER = 3
LANES = 128
HIGHEST = lax.Precision.HIGHEST
MESH = pl.DeviceIdType.MESH


def dot(a, b, dims, precision=None):
    return lax.dot_general(
        a, b, (dims, ((), ())), precision=precision, preferred_element_type=jnp.float32
    )


def matmul(a, b):
    return dot(a, b, ((1,), (0,)), HIGHEST)


def matmul_t(a, b):
    return dot(a, b, ((1,), (1,)), HIGHEST)


def rounded(a):
    return a.astype(jnp.bfloat16).astype(jnp.float32)


def factor_rows(m, start, block=8):
    count = RANK // 8
    v = [m[8 * i : 8 * i + 8] for i in range(count)]
    sub = lax.broadcasted_iota(jnp.int32, (8, LANES), 0)
    lane = lax.broadcasted_iota(jnp.int32, (8, LANES), 1)

    def column(x, j):
        return jnp.broadcast_to(x[:, start + j : start + j + 1], (8, LANES))

    for k in range(0, RANK, block):
        b, s = k // 8, k % 8
        row = [jnp.broadcast_to(v[b][s + j : s + j + 1, :], (8, LANES)) for j in range(block)]
        diag = {(i, j): column(row[i], k + j) for i in range(block) for j in range(i, block)}
        cols = [[column(v[i], k + j) for j in range(block)] for i in range(b, count)]
        inverse = []
        for i in range(block):
            inverse.append(1.0 / diag[i, i])
            ratio = {j: diag[i, j] * inverse[i] for j in range(i + 1, block)}
            for j in range(i + 1, block):
                for n in range(j, block):
                    diag[j, n] = diag[j, n] - ratio[j] * diag[i, n]
                row[j] = row[j] - ratio[j] * row[i]
                for c in cols:
                    c[j] = c[j] - c[i] * ratio[j]
        scaled = [row[i] * inverse[i] for i in range(block)]
        for i in range(b, count):
            total = None
            for j in range(block):
                if i == b and s + j == 7:
                    continue
                c = cols[i - b][j]
                if i == b:
                    c = jnp.where(sub > s + j, c, 0.0)
                term = c * scaled[j]
                total = term if total is None else total + term
            if total is not None:
                v[i] = v[i] - total
    out = []
    for i in range(count):
        pivot = jnp.sum(
            jnp.where(lane == sub + (start + 8 * i), v[i], 0.0), axis=1, keepdims=True
        )
        out.append(v[i] * lax.rsqrt(pivot))
    return jnp.concatenate(out, axis=0)


def half_mask(rows, side):
    lane = lax.broadcasted_iota(jnp.int32, (rows, LANES), 1)
    return (lane < 64) if side == 0 else (lane >= 64)


def inner_beside(p, side):
    start = 64 * (1 - side)
    parts = []
    if start:
        parts.append(jnp.zeros((start, LANES), jnp.float32))
    parts.append(p)
    parts.append(jnp.zeros((LANES - start - RANK, LANES), jnp.float32))
    return p + matmul_t(p, jnp.concatenate(parts, axis=0))


def top_rows(problems):
    row = lax.broadcasted_iota(jnp.int32, (RANK, LANES), 0)
    lane = lax.broadcasted_iota(jnp.int32, (RANK, LANES), 1)
    starts = tuple(
        jnp.where(lane == row + 64 * side, 1.0, 0.0).astype(jnp.float32) for _, side in problems
    )

    def body(_, bases):
        out = []
        for (gram, side), p in zip(problems, bases):
            keep = half_mask(RANK, side)
            p = jnp.where(keep, matmul(p, gram), 0.0)
            out.append((inner_beside(p, side), side, keep))
        return tuple(
            jnp.where(keep, factor_rows(m, 64 * (1 - side)), 0.0) for m, side, keep in out
        )

    return lax.fori_loop(0, POWER + 1, body, starts)


def merge_pairs(grams):
    problems = [(g, side) for g in grams for side in (0, 1)]
    tops = top_rows(problems)
    zeros = jnp.zeros((64, LANES), jnp.float32)
    joined = [
        jnp.concatenate([rounded(tops[2 * i]), rounded(tops[2 * i + 1]), zeros], axis=0)
        for i in range(len(grams))
    ]
    merged = [matmul_t(matmul(j, g), j) for j, g in zip(joined, grams)]
    second = top_rows([(m, 0) for m in merged])
    return [matmul(rounded(p), j) for p, j in zip(second, joined)]


def order_of(n):
    return sorted(range(1, n), key=lambda d: -min(d, n - d))


def merge_kernel(
    ny, nx, nz, y_ref, out_ref,
    pair, gram_part, gram_rs, gram_z, gram_ag,
    a_own, a_all, g2_part, g2_rs, g2_y, g2_z, g2_ag,
    f_all, coef_x, coef_z,
    send, recv,
):
    t, x, z = lax.axis_index("tm"), lax.axis_index("lat"), lax.axis_index("lon")
    y, c = t // 2, lax.rem(t, 2)
    nxc = 2 * nx
    p = x * 2 + c
    half = y_ref.shape[0] // 2
    per = half // ny

    def dev_xc(q):
        return (y * 2 + lax.rem(q, 2), q // 2, z)

    def dev_x(q):
        return (t, q, z)

    def dev_z(q):
        return (t, x, q)

    def dev_y(q):
        return (q * 2 + c, x, z)

    partner = (y * 2 + (1 - c), x, z)
    barrier = pltpu.get_barrier_semaphore()
    groups = ((nxc, p, dev_xc), (nz, z, dev_z), (ny, y, dev_y))
    for n, me, dev in groups:
        for d in range(1, n):
            pl.semaphore_signal(
                barrier, inc=1, device_id=dev(lax.rem(me + d, n)), device_id_type=MESH
            )
    pl.semaphore_wait(barrier, sum(n - 1 for n, _, _ in groups))

    pending = []
    stage_count = [0]

    def exchange(n, me, dev, source, target):
        stage = stage_count[0]
        stage_count[0] += 1
        copies = {}
        for d in order_of(n):
            q = lax.rem(me + d, n)
            copy = pltpu.make_async_remote_copy(
                src_ref=source(q), dst_ref=target,
                send_sem=send.at[stage, d], recv_sem=recv.at[stage, d],
                device_id=dev(q), device_id_type=MESH,
            )
            copy.start()
            copies[d] = copy
            pending.append(copy)
        return copies

    def arrive(copies):
        for d in sorted(copies, key=lambda d: min(d, len(copies) + 1 - d)):
            copies[d].wait_recv()

    stage = stage_count[0]
    stage_count[0] += 1
    swap = pltpu.make_async_remote_copy(
        src_ref=y_ref.at[pl.ds(half * (1 - c), half)], dst_ref=pair.at[c],
        send_sem=send.at[stage, 0], recv_sem=recv.at[stage, 0],
        device_id=partner, device_id_type=MESH,
    )
    swap.start()
    pending.append(swap)
    pair[c] = y_ref[pl.ds(half * c, half)]
    swap.wait_recv()

    def rows_of(r):
        return jnp.concatenate([pair[0, r], pair[1, r]], axis=0)

    total = jnp.zeros((LANES, LANES), jnp.float32)
    for r in range(0, half, 2):
        wide = jnp.concatenate([rows_of(r), rows_of(r + 1)], axis=1)
        total = total + dot(wide, wide, ((1,), (1,)))
    piece = LANES // nxc
    gram_part[...] = total.reshape(nxc, piece, LANES)
    copies = exchange(nxc, p, dev_xc, lambda q: gram_part.at[q], gram_rs.at[p])
    gram_rs[p] = gram_part[p]
    arrive(copies)
    gram_z[z] = jnp.sum(gram_rs[...], axis=0)
    copies = exchange(nz, z, dev_z, lambda q: gram_z.at[z], gram_z.at[z])
    arrive(copies)
    gram_ag[p] = jnp.sum(gram_z[...], axis=0)
    copies = exchange(nxc, p, dev_xc, lambda q: gram_ag.at[p], gram_ag.at[p])
    arrive(copies)
    gram = gram_ag[...].reshape(LANES, LANES)

    basis = merge_pairs([gram])[0].astype(jnp.bfloat16)

    for r in range(0, half, 2):
        wide = jnp.concatenate([rows_of(r), rows_of(r + 1)], axis=1)
        modes = dot(basis, wide, ((1,), (0,))).astype(jnp.bfloat16)
        a_own[r] = modes[:, :LANES]
        a_own[r + 1] = modes[:, LANES:]
    copies = exchange(ny, y, dev_y, lambda q: a_own.at[pl.ds(per * q, per)], a_all.at[y])
    a_all[y] = a_own[pl.ds(per * y, per)]
    arrive(copies)

    stacked = jnp.concatenate(
        [
            jnp.concatenate([a_all[b, r] for b in range(ny)], axis=0)
            for r in range(per)
        ],
        axis=1,
    )
    big = ny * RANK
    full = dot(stacked, stacked, ((1,), (1,)))
    width = full.shape[1]
    near = ny // 2
    if width % LANES:
        full = jnp.concatenate(
            [full, jnp.zeros((big, LANES - width % LANES), jnp.float32)], axis=1
        )
    tiles = full.shape[1] // LANES
    lane = lax.broadcasted_iota(jnp.int32, (RANK, LANES), 1)

    def lane_window(block, shift):
        if width < LANES:
            rolled = block if shift == 0 else jnp.where(
                lane < width - shift, pltpu.roll(block, LANES - shift, 1),
                pltpu.roll(block, (width - shift) % LANES, 1),
            )
            return rolled
        first, inner = shift // LANES, shift % LANES
        a = block[:, LANES * first : LANES * first + LANES]
        if inner == 0:
            return a
        nxt = (first + 1) % tiles
        bb = block[:, LANES * nxt : LANES * nxt + LANES]
        return jnp.where(
            lane < LANES - inner, pltpu.roll(a, LANES - inner, 1), pltpu.roll(bb, LANES - inner, 1)
        )

    pieces = []
    for b in range(ny):
        window = lane_window(full[RANK * b : RANK * b + RANK], RANK * b)
        pieces.append(jnp.where(lane < RANK * near, window, 0.0))
    extra = jnp.zeros((RANK, LANES), jnp.float32)
    for q in range(near):
        col = RANK * (q + near)
        tile, inner = col // LANES, col % LANES
        block = full[RANK * q : RANK * q + RANK, LANES * tile : LANES * tile + LANES]
        shift = (RANK * q - inner) % LANES
        if shift:
            block = pltpu.roll(block, shift, 1)
        extra = jnp.where((lane >= RANK * q) & (lane < RANK * q + RANK), block, extra)
    pieces.append(extra)
    tall = g2_part.shape[0] * g2_part.shape[1] - RANK * (ny + 1)
    if tall:
        pieces.append(jnp.zeros((tall, LANES), jnp.float32))
    g2_part[...] = jnp.concatenate(pieces, axis=0).reshape(g2_part.shape)
    copies = exchange(nxc, p, dev_xc, lambda q: g2_part.at[q], g2_rs.at[p])
    g2_rs[p] = g2_part[p]
    arrive(copies)
    g2_y[y] = jnp.sum(g2_rs[...], axis=0)
    copies = exchange(ny, y, dev_y, lambda q: g2_y.at[y], g2_y.at[y])
    arrive(copies)
    g2_z[z] = jnp.sum(g2_y[...], axis=0)
    copies = exchange(nz, z, dev_z, lambda q: g2_z.at[z], g2_z.at[z])
    arrive(copies)
    g2_ag[p] = jnp.sum(g2_z[...], axis=0)
    copies = exchange(nxc, p, dev_xc, lambda q: g2_ag.at[p], g2_ag.at[p])
    arrive(copies)
    flat = g2_ag[...].reshape(g2_ag.shape[0] * g2_ag.shape[1], LANES)

    zero = jnp.zeros((RANK, LANES), jnp.float32)
    upper = [[None] * tiles for _ in range(ny)]
    extra = flat[RANK * ny : RANK * ny + RANK]
    for b in range(ny):
        block = flat[RANK * b : RANK * b + RANK]
        block = jnp.where(lane < RANK, 0.5 * block, block)
        for tile in range(tiles):
            got = zero
            for off in range(near):
                col = (RANK * (b + off)) % width
                if col // LANES != tile:
                    continue
                inner = col % LANES
                shift = (inner - RANK * off) % LANES
                moved = pltpu.roll(block, shift, 1) if shift else block
                got = jnp.where((lane >= inner) & (lane < inner + RANK), moved, got)
            if b < near:
                col = RANK * (b + near)
                if col // LANES == tile:
                    inner = col % LANES
                    shift = (inner - RANK * b) % LANES
                    moved = pltpu.roll(extra, shift, 1) if shift else extra
                    got = jnp.where((lane >= inner) & (lane < inner + RANK), moved, got)
            upper[b][tile] = got
    per_tile = LANES // RANK

    def tile_value(i, j):
        rows = [upper[b][j] for b in range(per_tile * i, min(per_tile * i + per_tile, ny))]
        rows += [zero] * (per_tile - len(rows))
        return jnp.concatenate(rows, axis=0)

    up = [[tile_value(i, j) for j in range(tiles)] for i in range(tiles)]
    sym = [[up[i][j] + up[j][i].T for j in range(tiles)] for i in range(tiles)]

    if tiles == 2:
        halves = merge_pairs([sym[0][0], sym[1][1]])
        halves = [rounded(h) for h in halves]
        crossed = matmul_t(matmul(halves[0], sym[0][1]), halves[1])
        zeros64 = jnp.zeros((64, LANES), jnp.float32)

        def spread(a, b):
            return jnp.concatenate([a, b, zeros64], axis=0)

        pad = jnp.zeros((RANK, LANES), jnp.float32)
        first = spread(halves[0], pad)
        second = spread(pad, halves[1])
        upper_part = matmul_t(matmul(first, sym[0][1]), second)
        last = (
            matmul_t(matmul(first, sym[0][0]), first)
            + matmul_t(matmul(second, sym[1][1]), second)
            + upper_part
            + upper_part.T
        )
        sources = [first, second]
    elif ny == 4:
        tops = top_rows([(sym[0][0], 0), (sym[0][0], 1)])
        joined = jnp.concatenate(
            [rounded(tops[0]), rounded(tops[1]), jnp.zeros((64, LANES), jnp.float32)], axis=0
        )
        last = matmul_t(matmul(joined, sym[0][0]), joined)
        sources = [joined]
    else:
        last = sym[0][0]
        row = lax.broadcasted_iota(jnp.int32, (LANES, LANES), 0)
        col = lax.broadcasted_iota(jnp.int32, (LANES, LANES), 1)
        sources = [jnp.where(row == col, 1.0, 0.0).astype(jnp.float32)]
    top = rounded(top_rows([(last, 0)])[0])
    bent = matmul(top, last)
    place = jnp.concatenate(
        [jnp.zeros((64, LANES), jnp.float32), top, jnp.zeros((32, LANES), jnp.float32)], axis=0
    )
    final = factor_rows(top + matmul_t(bent, place), 64)
    final = jnp.where(half_mask(RANK, 0), final, 0.0)
    weights = jnp.concatenate([matmul(final, s) for s in sources], axis=1)[:, :big]
    weights = weights.astype(jnp.bfloat16)

    mine = half * c + per * y
    for r in range(per):
        tall_rows = jnp.concatenate([a_all[b, r] for b in range(ny)], axis=0)
        f_all[mine + r] = dot(weights, tall_rows, ((1,), (0,))).astype(jnp.bfloat16)
    here = f_all.at[pl.ds(mine, per)]
    copies = exchange(ny, y, dev_y, lambda q: here, here)
    stage = stage_count[0]
    stage_count[0] += 1

    def hand_over(d):
        owner = lax.rem(y + ny - d, ny)
        block = f_all.at[pl.ds(half * c + per * owner, per)]
        copy = pltpu.make_async_remote_copy(
            src_ref=block, dst_ref=block,
            send_sem=send.at[stage, d], recv_sem=recv.at[stage, d],
            device_id=partner, device_id_type=MESH,
        )
        copy.start()
        pending.append(copy)
        return copy

    handed = [hand_over(0)]
    for d in sorted(copies, key=lambda d: min(d, ny - d)):
        copies[d].wait_recv()
        handed.append(hand_over(d))
    for copy in handed:
        copy.wait_recv()

    coef = jnp.zeros((RANK, 64), jnp.float32)
    for r in range(0, 2 * half, 2):
        a = jnp.concatenate([f_all[r], f_all[r + 1]], axis=1)
        b = jnp.concatenate([y_ref[r], y_ref[r + 1]], axis=1)
        coef = coef + dot(a, b, ((1,), (1,)))
    coef_x[x] = jnp.concatenate([coef[:16], coef[16:]], axis=1)
    copies = exchange(nx, x, dev_x, lambda q: coef_x.at[x], coef_x.at[x])
    arrive(copies)
    coef_z[z] = jnp.sum(coef_x[...], axis=0)
    copies = exchange(nz, z, dev_z, lambda q: coef_z.at[z], coef_z.at[z])
    arrive(copies)
    packed = jnp.sum(coef_z[...], axis=0)
    solved = jnp.concatenate([packed[:, :64], packed[:, 64:]], axis=0).astype(jnp.bfloat16)

    solved_t = solved.T
    for r in range(0, out_ref.shape[0]):
        out_ref[r] = dot(solved_t, f_all[r], ((1,), (0,))).astype(jnp.bfloat16)
    for copy in pending:
        copy.wait_send()


def merge_call(rows, ny, nx, nz, height):
    nxc = 2 * nx
    half = rows.shape[0] // 2
    per = half // ny
    tall = RANK * (ny + 1)
    piece2 = -(-tall // (8 * nxc)) * 8
    f32, bf16 = jnp.float32, jnp.bfloat16
    vm = pltpu.VMEM
    return pl.pallas_call(
        functools.partial(merge_kernel, ny, nx, nz),
        out_shape=jax.ShapeDtypeStruct((height, 64, LANES), bf16),
        in_specs=[pl.BlockSpec(memory_space=pltpu.VMEM)],
        out_specs=pl.BlockSpec(memory_space=pltpu.VMEM),
        scratch_shapes=[
            vm((2, half, 64, LANES), bf16),
            vm((nxc, LANES // nxc, LANES), f32),
            vm((nxc, LANES // nxc, LANES), f32),
            vm((nz, LANES // nxc, LANES), f32),
            vm((nxc, LANES // nxc, LANES), f32),
            vm((half, RANK, LANES), bf16),
            vm((ny, per, RANK, LANES), bf16),
            vm((nxc, piece2, LANES), f32),
            vm((nxc, piece2, LANES), f32),
            vm((ny, piece2, LANES), f32),
            vm((nz, piece2, LANES), f32),
            vm((nxc, piece2, LANES), f32),
            vm((2 * half, RANK, LANES), bf16),
            vm((nx, 16, LANES), f32),
            vm((nz, 16, LANES), f32),
            pltpu.SemaphoreType.DMA((13, max(8, nxc, ny, nz))),
            pltpu.SemaphoreType.DMA((13, max(8, nxc, ny, nz))),
        ],
        compiler_params=pltpu.CompilerParams(collective_id=0, has_side_effects=True),
        name="merge",
    )(rows)


def with_halo(block, sides, width, periodic):
    for axis, dim in sides:
        count = lax.axis_size(axis)
        forward = [(i, i + 1) for i in range(count - 1)]
        if periodic:
            forward.append((count - 1, 0))
        backward = [(target, source) for source, target in forward]
        low = lax.ppermute(
            lax.slice_in_dim(block, block.shape[dim] - width, None, axis=dim), axis, forward
        )
        high = lax.ppermute(lax.slice_in_dim(block, 0, width, axis=dim), axis, backward)
        block = jnp.concatenate([low, block, high], axis=dim)
    return block


def stencil(current, coeffs):
    center = current[:, 1:-1, 1:-1]
    middle = coeffs[:, 1:-1, 1:-1]
    northward = 0.5 * (middle + coeffs[:, :-2, 1:-1]) * (current[:, :-2, 1:-1] - center)
    southward = 0.5 * (middle + coeffs[:, 2:, 1:-1]) * (current[:, 2:, 1:-1] - center)
    westward = 0.5 * (middle + coeffs[:, 1:-1, :-2]) * (current[:, 1:-1, :-2] - center)
    eastward = 0.5 * (middle + coeffs[:, 1:-1, 2:]) * (current[:, 1:-1, 2:] - center)
    return center + (northward + southward + westward + eastward)


def shards(residuals, diffusivity):
    snap_count, height, width = residuals.shape
    current = residuals.astype(jnp.float32)
    coeffs = diffusivity[None]
    for pass_index in range(PASSES):
        field_ext, coeff_ext = (
            with_halo(current.astype(jnp.bfloat16), (("lon", 2),), 1, True).astype(current.dtype),
            with_halo(coeffs.astype(jnp.bfloat16), (("lon", 2),), 1, True).astype(coeffs.dtype),
        )
        field_ext, coeff_ext = (
            with_halo(field_ext.astype(jnp.bfloat16), (("lat", 1),), 1, False).astype(
                field_ext.dtype
            ),
            with_halo(coeff_ext.astype(jnp.bfloat16), (("lat", 1),), 1, False).astype(
                coeff_ext.dtype
            ),
        )
        current = stencil(field_ext, coeff_ext)
    rows = (lax.axis_index("lat") * height + jnp.arange(height)).astype(jnp.float32)
    latitude = (rows + 0.5) * math.pi / (height * lax.axis_size("lat")) - math.pi / 2
    scale = jnp.sqrt(jnp.cos(latitude))
    weighted = (current * scale[None, :, None]).astype(jnp.bfloat16)

    ny, nx, nz = lax.axis_size("tm") // 2, lax.axis_size("lat"), lax.axis_size("lon")
    unit = 2 * ny
    padded = -(-height // unit) * unit
    while (padded // 2) % 2:
        padded += unit
    rows = jnp.pad(weighted.transpose(1, 0, 2), ((0, padded - height), (0, 0), (0, 0)))
    projected = merge_call(rows, ny, nx, nz, height)
    return projected.transpose(1, 0, 2)


def solution(mesh):
    return jax.shard_map(
        shards,
        mesh=mesh,
        in_specs=(P("tm", "lat", "lon"), P("lat", "lon")),
        out_specs=P("tm", "lat", "lon"),
        check_vma=False,
    )
```

```python
import functools
import math

import jax
import jax.numpy as jnp
from jax import lax
from jax.experimental import pallas as pl
from jax.experimental.pallas import tpu as pltpu
from jax.sharding import PartitionSpec as P

RANK = 32
PASSES = 4
POWER = 3
LANES = 128
ROW_BASE = 11
HIGHEST = lax.Precision.HIGHEST
MESH = pl.DeviceIdType.MESH


def dot(a, b, dims, precision=None):
    return lax.dot_general(
        a, b, (dims, ((), ())), precision=precision, preferred_element_type=jnp.float32
    )


def matmul(a, b):
    return dot(a, b, ((1,), (0,)), HIGHEST)


def matmul_t(a, b):
    return dot(a, b, ((1,), (1,)), HIGHEST)


def rounded(a):
    return a.astype(jnp.bfloat16).astype(jnp.float32)


def factor_rows(m, start, block=8):
    count = RANK // 8
    v = [m[8 * i : 8 * i + 8] for i in range(count)]
    sub = lax.broadcasted_iota(jnp.int32, (8, LANES), 0)
    lane = lax.broadcasted_iota(jnp.int32, (8, LANES), 1)

    def column(x, j):
        return jnp.broadcast_to(x[:, start + j : start + j + 1], (8, LANES))

    for k in range(0, RANK, block):
        b, s = k // 8, k % 8
        row = [jnp.broadcast_to(v[b][s + j : s + j + 1, :], (8, LANES)) for j in range(block)]
        diag = {(i, j): column(row[i], k + j) for i in range(block) for j in range(i, block)}
        cols = [[column(v[i], k + j) for j in range(block)] for i in range(b, count)]
        inverse = []
        for i in range(block):
            inverse.append(1.0 / diag[i, i])
            ratio = {j: diag[i, j] * inverse[i] for j in range(i + 1, block)}
            for j in range(i + 1, block):
                for n in range(j, block):
                    diag[j, n] = diag[j, n] - ratio[j] * diag[i, n]
                row[j] = row[j] - ratio[j] * row[i]
                for c in cols:
                    c[j] = c[j] - c[i] * ratio[j]
        scaled = [row[i] * inverse[i] for i in range(block)]
        for i in range(b, count):
            total = None
            for j in range(block):
                if i == b and s + j == 7:
                    continue
                c = cols[i - b][j]
                if i == b:
                    c = jnp.where(sub > s + j, c, 0.0)
                term = c * scaled[j]
                total = term if total is None else total + term
            if total is not None:
                v[i] = v[i] - total
    out = []
    for i in range(count):
        pivot = jnp.sum(
            jnp.where(lane == sub + (start + 8 * i), v[i], 0.0), axis=1, keepdims=True
        )
        out.append(v[i] * lax.rsqrt(pivot))
    return jnp.concatenate(out, axis=0)


def half_mask(rows, side):
    lane = lax.broadcasted_iota(jnp.int32, (rows, LANES), 1)
    return (lane < 64) if side == 0 else (lane >= 64)


def inner_beside(p, side):
    start = 64 * (1 - side)
    parts = []
    if start:
        parts.append(jnp.zeros((start, LANES), jnp.float32))
    parts.append(p)
    parts.append(jnp.zeros((LANES - start - RANK, LANES), jnp.float32))
    return p + matmul_t(p, jnp.concatenate(parts, axis=0))


def top_rows(problems):
    row = lax.broadcasted_iota(jnp.int32, (RANK, LANES), 0)
    lane = lax.broadcasted_iota(jnp.int32, (RANK, LANES), 1)
    starts = tuple(
        jnp.where(lane == row + 64 * side, 1.0, 0.0).astype(jnp.float32) for _, side in problems
    )

    def body(_, bases):
        out = []
        for (gram, side), p in zip(problems, bases):
            keep = half_mask(RANK, side)
            p = jnp.where(keep, matmul(p, gram), 0.0)
            out.append((inner_beside(p, side), side, keep))
        return tuple(
            jnp.where(keep, factor_rows(m, 64 * (1 - side)), 0.0) for m, side, keep in out
        )

    return lax.fori_loop(0, POWER + 1, body, starts)


def merge_pairs(grams):
    problems = [(g, side) for g in grams for side in (0, 1)]
    tops = top_rows(problems)
    zeros = jnp.zeros((64, LANES), jnp.float32)
    joined = [
        jnp.concatenate([rounded(tops[2 * i]), rounded(tops[2 * i + 1]), zeros], axis=0)
        for i in range(len(grams))
    ]
    merged = [matmul_t(matmul(j, g), j) for j, g in zip(joined, grams)]
    second = top_rows([(m, 0) for m in merged])
    return [matmul(rounded(p), j) for p, j in zip(second, joined)]


def order_of(n):
    return sorted(range(1, n), key=lambda d: -min(d, n - d))


def merge_kernel(
    ny, nx, nz, res_hbm, dif_ref, out_ref,
    res_ref, field, west, east, coef_m, coef_s, grid, y_ref, pack, pack_edge, edge_rows, dif_edge,
    got_rows, got_pack, got_edge, got_dif, got_dif_edge,
    pair, gram_part, gram_rs, gram_z, gram_ag,
    a_own, a_all, g2_part, g2_rs, g2_y, g2_z, g2_ag,
    f_all, coef_x, coef_z,
    send, recv, load_sem,
):
    t, x, z = lax.axis_index("tm"), lax.axis_index("lat"), lax.axis_index("lon")
    y, c = t // 2, lax.rem(t, 2)
    nxc = 2 * nx
    p = x * 2 + c
    half = y_ref.shape[0] // 2
    per = half // ny

    def dev_xc(q):
        return (y * 2 + lax.rem(q, 2), q // 2, z)

    def dev_x(q):
        return (t, q, z)

    def dev_z(q):
        return (t, x, q)

    def dev_y(q):
        return (q * 2 + c, x, z)

    partner = (y * 2 + (1 - c), x, z)
    def dev_around(dx, dz):
        return (t, lax.rem(x + dx + nx, nx), lax.rem(z + dz + nz, nz))

    load = pltpu.make_async_copy(res_hbm, res_ref, load_sem)
    load.start()
    corners = [(dx, dz) for dx in (-1, 1) for dz in (-1, 1)]
    barrier = pltpu.get_barrier_semaphore()
    groups = ((nxc, p, dev_xc), (nz, z, dev_z), (ny, y, dev_y))
    for n, me, dev in groups:
        for d in range(1, n):
            pl.semaphore_signal(
                barrier, inc=1, device_id=dev(lax.rem(me + d, n)), device_id_type=MESH
            )
    for dx, dz in corners:
        pl.semaphore_signal(barrier, inc=1, device_id=dev_around(dx, dz), device_id_type=MESH)

    pending = []
    stage_count = [0]

    def exchange(n, me, dev, source, target):
        stage = stage_count[0]
        stage_count[0] += 1
        copies = {}
        for d in order_of(n):
            q = lax.rem(me + d, n)
            copy = pltpu.make_async_remote_copy(
                src_ref=source(q), dst_ref=target,
                send_sem=send.at[stage, d], recv_sem=recv.at[stage, d],
                device_id=dev(q), device_id_type=MESH,
            )
            copy.start()
            copies[d] = copy
            pending.append(copy)
        return copies

    def arrive(copies):
        for d in sorted(copies, key=lambda d: min(d, len(copies) + 1 - d)):
            copies[d].wait_recv()

    height = res_ref.shape[1]
    base, edge = ROW_BASE, PASSES
    lane8 = lax.broadcasted_iota(jnp.int32, (8, LANES), 1)
    lane_h = lax.broadcasted_iota(jnp.int32, (height, LANES), 1)
    load.wait()

    def take_in(g, carry):
        def one(j, acc):
            s = 16 * g + j
            value = pltpu.roll(res_ref[s].astype(jnp.float32), 8 * j + 4, 1)
            field[0, s, pl.ds(base, height), :] = value
            return jnp.where(lane_h // 8 == j, value, acc)

        acc = lax.fori_loop(0, 16, one, jnp.zeros((height, LANES), jnp.float32), unroll=2)
        west[0, g, pl.ds(base, height), :] = acc
        east[0, g, pl.ds(base, height), :] = acc
        pack[g, pl.ds(0, height), :] = acc.astype(jnp.bfloat16)
        pack_edge[0, g, pl.ds(0, edge), :] = acc[:edge].astype(jnp.bfloat16)
        pack_edge[1, g, pl.ds(0, edge), :] = acc[height - edge :].astype(jnp.bfloat16)
        return carry

    lax.fori_loop(0, 4, take_in, 0)
    for side, first in ((0, 0), (1, height - edge)):
        for e in range(edge):
            edge_rows[side, e] = field[0, :, base + first + e, :].astype(jnp.bfloat16)
    dif_edge[0, pl.ds(0, edge), :] = dif_ref[pl.ds(0, edge), :]
    dif_edge[1, pl.ds(0, edge), :] = dif_ref[pl.ds(height - edge, edge), :]
    pl.semaphore_wait(barrier, sum(n - 1 for n, _, _ in groups) + len(corners))

    stage = stage_count[0]
    stage_count[0] += 3
    halo = []

    def pass_on(source, target, dx, dz):
        at = len(halo)
        copy = pltpu.make_async_remote_copy(
            src_ref=source, dst_ref=target,
            send_sem=send.at[stage + at // 8, at % 8], recv_sem=recv.at[stage + at // 8, at % 8],
            device_id=dev_around(dx, dz), device_id_type=MESH,
        )
        copy.start()
        halo.append(copy)
        pending.append(copy)

    for side, dx in ((0, -1), (1, 1)):
        for dz in (-1, 1):
            pass_on(pack_edge.at[side], got_edge.at[side, dz + 1], dx, dz)
            pass_on(dif_edge.at[side], got_dif_edge.at[side, dz + 1], dx, dz)
        pass_on(pack_edge.at[side], got_edge.at[side, 1], dx, 0)
        pass_on(dif_edge.at[side], got_dif_edge.at[side, 1], dx, 0)
        pass_on(edge_rows.at[side], got_rows.at[side], dx, 0)
    for dz in (-1, 1):
        pass_on(pack, got_pack.at[(dz + 1) // 2], 0, dz)
        pass_on(dif_ref, got_dif.at[(dz + 1) // 2], 0, dz)
    for copy in halo:
        copy.wait_recv()

    has_north, has_south = x > 0, x < nx - 1
    for side, first, there in ((1, base - edge, has_north), (0, base + height, has_south)):
        for e in range(edge):
            row = got_rows[side, e].astype(jnp.float32)
            row = jnp.where(there, row, 0.0)
            field[0, :, first + e, :] = row

    def seam(own, other, rows, own_first):
        t8 = lax.broadcasted_iota(jnp.int32, (rows, LANES), 1) % 8
        return jnp.where((t8 < 4) == own_first, own, other)

    for g in range(4):
        own = west[0, g, pl.ds(base, height), :]
        from_west = got_pack[1, g, pl.ds(0, height), :].astype(jnp.float32)
        from_east = got_pack[0, g, pl.ds(0, height), :].astype(jnp.float32)
        west[0, g, pl.ds(base, height), :] = seam(own, from_west, height, False)
        east[0, g, pl.ds(base, height), :] = seam(own, from_east, height, True)
        for side, first, there in ((1, base - edge, has_north), (0, base + height, has_south)):
            own, from_west, from_east = (
                jnp.where(
                    there, got_edge[side, k, g, pl.ds(0, edge), :].astype(jnp.float32), 0.0
                )
                for k in (1, 2, 0)
            )
            west[0, g, pl.ds(first, edge), :] = seam(own, from_west, edge, False)
            east[0, g, pl.ds(first, edge), :] = seam(own, from_east, edge, True)

    wide = height + 2 * edge

    def tall_of(middle, k):
        north = jnp.where(has_north, got_dif_edge[1, k, pl.ds(0, edge), :], 0.0)
        south = jnp.where(has_south, got_dif_edge[0, k, pl.ds(0, edge), :], 0.0)
        return jnp.concatenate([north, middle, south], axis=0)

    own_d = tall_of(dif_ref[...], 1)
    west_d = tall_of(got_dif[1], 2)
    east_d = tall_of(got_dif[0], 0)
    lane_w = lax.broadcasted_iota(jnp.int32, (wide, LANES), 1)
    row_w = lax.broadcasted_iota(jnp.int32, (wide, LANES), 0)
    inside = ((row_w >= edge) | has_north) & ((row_w < height + edge) | has_south)

    def five(center, left, right):
        zero_row = jnp.zeros((1, LANES), jnp.float32)
        up = jnp.concatenate([zero_row, center[:-1]], axis=0)
        down = jnp.concatenate([center[1:], zero_row], axis=0)
        ks = [jnp.where(inside, 0.5 * (center + v), 0.0) for v in (up, down, left, right)]
        return [1.0 - (ks[0] + ks[1] + ks[2] + ks[3])] + ks

    left = jnp.where(lane_w == 0, pltpu.roll(west_d, 1, 1), pltpu.roll(own_d, 1, 1))
    right = jnp.where(lane_w == LANES - 1, pltpu.roll(east_d, LANES - 1, 1), pltpu.roll(own_d, LANES - 1, 1))
    main = five(own_d, left, right)
    for k in range(5):
        coef_m[0, k, pl.ds(base - edge, wide), :] = main[k]

    def turn(j, carry):
        for k in range(5):
            coef_m[j, k, pl.ds(base - edge, wide), :] = pltpu.roll(
                coef_m[0, k, pl.ds(base - edge, wide), :], 8 * j + 4, 1
            )
        return carry

    lax.fori_loop(1, 16, turn, 0)
    for k in range(5):
        coef_m[0, k, pl.ds(base - edge, wide), :] = pltpu.roll(main[k], 4, 1)
    for which, (first_d, second_d) in enumerate(((west_d, own_d), (own_d, east_d))):
        strip = jnp.where(
            lane_w < 4,
            pltpu.roll(first_d, 4, 1),
            jnp.where(lane_w < 8, pltpu.roll(second_d, 4, 1), 0.0),
        )
        for shift in (8, 16, 32, 64):
            strip = strip + pltpu.roll(strip, shift, 1)
        ks = five(strip, pltpu.roll(strip, 1, 1), pltpu.roll(strip, LANES - 1, 1))
        for k in range(5):
            coef_s[which, k, pl.ds(base - edge, wide), :] = ks[k]

    def weighted_sum(c, center, north, south, left, right):
        return center * c[0] + north * c[1] + south * c[2] + left * c[3] + right * c[4]

    tile_rows = [8 * k for k in range(1, (base + height + edge + 7) // 8)]

    def stencil_rows(src, dst, j, tiles, finish):
        for r in tiles:
            here = pl.ds(r, 8)
            c = [coef_m[j, k, here, :] for k in range(5)]
            for g in range(4):
                s = 16 * g + j
                center = field[src, s, here, :]
                lft = jnp.where(lane8 == 8 * j + 3, west[src, g, here, :], center)
                rgt = jnp.where(lane8 == 8 * j + 4, east[src, g, here, :], center)
                finish(
                    s, r,
                    weighted_sum(
                        c, center, field[src, s, pl.ds(r - 1, 8), :],
                        field[src, s, pl.ds(r + 1, 8), :],
                        pltpu.roll(lft, 1, 1), pltpu.roll(rgt, LANES - 1, 1),
                    ),
                )

    def one_pass(number, carry):
        src = lax.rem(number, 2)
        dst = 1 - src

        def keep(s, r, value):
            field[dst, s, pl.ds(r, 8), :] = value

        def each(j, inner):
            stencil_rows(src, dst, j, tile_rows, keep)
            return inner

        lax.fori_loop(0, 16, each, 0)
        for which, strip in enumerate((west, east)):
            for r in tile_rows:
                here = pl.ds(r, 8)
                c = [coef_s[which, k, here, :] for k in range(5)]
                for g in range(4):
                    center = strip[src, g, here, :]
                    strip[dst, g, here, :] = weighted_sum(
                        c, center, strip[src, g, pl.ds(r - 1, 8), :],
                        strip[src, g, pl.ds(r + 1, 8), :],
                        pltpu.roll(center, 1, 1), pltpu.roll(center, LANES - 1, 1),
                    )
        return carry

    lax.fori_loop(0, PASSES - 1, one_pass, 0)
    last_rows = [8 * k for k in range(1, (base + height + 7) // 8)]
    skip = base - 8
    sub8 = lax.broadcasted_iota(jnp.int32, (8, LANES), 0)

    def scale_of(r):
        row = (x * height + sub8 + (r - base)).astype(jnp.float32)
        latitude = (row + 0.5) * math.pi / (height * nx) - math.pi / 2
        return jnp.sqrt(jnp.maximum(jnp.cos(latitude), 0.0))

    scales = {r: scale_of(r) for r in last_rows}

    def last_pass(j, carry):
        def out(s, r, value):
            value = pltpu.roll(value * scales[r], LANES - 4 - 8 * j, 1)
            grid[pl.ds((r - 8) * 64 + s, 8, stride=64), :] = value

        stencil_rows((PASSES - 1) % 2, None, j, last_rows, out)
        return carry

    lax.fori_loop(0, 16, last_pass, 0)
    for i in range(height):
        y_ref[i] = grid[pl.ds((i + skip) * 64, 64), :].astype(jnp.bfloat16)
    for i in range(height, y_ref.shape[0]):
        y_ref[i] = jnp.zeros((64, LANES), jnp.bfloat16)

    stage = stage_count[0]
    stage_count[0] += 1
    swap = pltpu.make_async_remote_copy(
        src_ref=y_ref.at[pl.ds(half * (1 - c), half)], dst_ref=pair.at[c],
        send_sem=send.at[stage, 0], recv_sem=recv.at[stage, 0],
        device_id=partner, device_id_type=MESH,
    )
    swap.start()
    pending.append(swap)
    pair[c] = y_ref[pl.ds(half * c, half)]
    swap.wait_recv()

    def rows_of(r):
        return jnp.concatenate([pair[0, r], pair[1, r]], axis=0)

    total = jnp.zeros((LANES, LANES), jnp.float32)
    for r in range(0, half, 2):
        wide = jnp.concatenate([rows_of(r), rows_of(r + 1)], axis=1)
        total = total + dot(wide, wide, ((1,), (1,)))
    piece = LANES // nxc
    gram_part[...] = total.reshape(nxc, piece, LANES)
    copies = exchange(nxc, p, dev_xc, lambda q: gram_part.at[q], gram_rs.at[p])
    gram_rs[p] = gram_part[p]
    arrive(copies)
    gram_z[z] = jnp.sum(gram_rs[...], axis=0)
    copies = exchange(nz, z, dev_z, lambda q: gram_z.at[z], gram_z.at[z])
    arrive(copies)
    gram_ag[p] = jnp.sum(gram_z[...], axis=0)
    copies = exchange(nxc, p, dev_xc, lambda q: gram_ag.at[p], gram_ag.at[p])
    arrive(copies)
    gram = gram_ag[...].reshape(LANES, LANES)

    basis = merge_pairs([gram])[0].astype(jnp.bfloat16)

    for r in range(0, half, 2):
        wide = jnp.concatenate([rows_of(r), rows_of(r + 1)], axis=1)
        modes = dot(basis, wide, ((1,), (0,))).astype(jnp.bfloat16)
        a_own[r] = modes[:, :LANES]
        a_own[r + 1] = modes[:, LANES:]
    copies = exchange(ny, y, dev_y, lambda q: a_own.at[pl.ds(per * q, per)], a_all.at[y])
    a_all[y] = a_own[pl.ds(per * y, per)]
    arrive(copies)

    stacked = jnp.concatenate(
        [
            jnp.concatenate([a_all[b, r] for b in range(ny)], axis=0)
            for r in range(per)
        ],
        axis=1,
    )
    big = ny * RANK
    full = dot(stacked, stacked, ((1,), (1,)))
    width = full.shape[1]
    near = ny // 2
    if width % LANES:
        full = jnp.concatenate(
            [full, jnp.zeros((big, LANES - width % LANES), jnp.float32)], axis=1
        )
    tiles = full.shape[1] // LANES
    lane = lax.broadcasted_iota(jnp.int32, (RANK, LANES), 1)

    def lane_window(block, shift):
        if width < LANES:
            rolled = block if shift == 0 else jnp.where(
                lane < width - shift, pltpu.roll(block, LANES - shift, 1),
                pltpu.roll(block, (width - shift) % LANES, 1),
            )
            return rolled
        first, inner = shift // LANES, shift % LANES
        a = block[:, LANES * first : LANES * first + LANES]
        if inner == 0:
            return a
        nxt = (first + 1) % tiles
        bb = block[:, LANES * nxt : LANES * nxt + LANES]
        return jnp.where(
            lane < LANES - inner, pltpu.roll(a, LANES - inner, 1), pltpu.roll(bb, LANES - inner, 1)
        )

    pieces = []
    for b in range(ny):
        window = lane_window(full[RANK * b : RANK * b + RANK], RANK * b)
        pieces.append(jnp.where(lane < RANK * near, window, 0.0))
    extra = jnp.zeros((RANK, LANES), jnp.float32)
    for q in range(near):
        col = RANK * (q + near)
        tile, inner = col // LANES, col % LANES
        block = full[RANK * q : RANK * q + RANK, LANES * tile : LANES * tile + LANES]
        shift = (RANK * q - inner) % LANES
        if shift:
            block = pltpu.roll(block, shift, 1)
        extra = jnp.where((lane >= RANK * q) & (lane < RANK * q + RANK), block, extra)
    pieces.append(extra)
    tall = g2_part.shape[0] * g2_part.shape[1] - RANK * (ny + 1)
    if tall:
        pieces.append(jnp.zeros((tall, LANES), jnp.float32))
    g2_part[...] = jnp.concatenate(pieces, axis=0).reshape(g2_part.shape)
    copies = exchange(nxc, p, dev_xc, lambda q: g2_part.at[q], g2_rs.at[p])
    g2_rs[p] = g2_part[p]
    arrive(copies)
    g2_y[y] = jnp.sum(g2_rs[...], axis=0)
    copies = exchange(ny, y, dev_y, lambda q: g2_y.at[y], g2_y.at[y])
    arrive(copies)
    g2_z[z] = jnp.sum(g2_y[...], axis=0)
    copies = exchange(nz, z, dev_z, lambda q: g2_z.at[z], g2_z.at[z])
    arrive(copies)
    g2_ag[p] = jnp.sum(g2_z[...], axis=0)
    copies = exchange(nxc, p, dev_xc, lambda q: g2_ag.at[p], g2_ag.at[p])
    arrive(copies)
    flat = g2_ag[...].reshape(g2_ag.shape[0] * g2_ag.shape[1], LANES)

    zero = jnp.zeros((RANK, LANES), jnp.float32)
    upper = [[None] * tiles for _ in range(ny)]
    extra = flat[RANK * ny : RANK * ny + RANK]
    for b in range(ny):
        block = flat[RANK * b : RANK * b + RANK]
        block = jnp.where(lane < RANK, 0.5 * block, block)
        for tile in range(tiles):
            got = zero
            for off in range(near):
                col = (RANK * (b + off)) % width
                if col // LANES != tile:
                    continue
                inner = col % LANES
                shift = (inner - RANK * off) % LANES
                moved = pltpu.roll(block, shift, 1) if shift else block
                got = jnp.where((lane >= inner) & (lane < inner + RANK), moved, got)
            if b < near:
                col = RANK * (b + near)
                if col // LANES == tile:
                    inner = col % LANES
                    shift = (inner - RANK * b) % LANES
                    moved = pltpu.roll(extra, shift, 1) if shift else extra
                    got = jnp.where((lane >= inner) & (lane < inner + RANK), moved, got)
            upper[b][tile] = got
    per_tile = LANES // RANK

    def tile_value(i, j):
        rows = [upper[b][j] for b in range(per_tile * i, min(per_tile * i + per_tile, ny))]
        rows += [zero] * (per_tile - len(rows))
        return jnp.concatenate(rows, axis=0)

    up = [[tile_value(i, j) for j in range(tiles)] for i in range(tiles)]
    sym = [[up[i][j] + up[j][i].T for j in range(tiles)] for i in range(tiles)]

    if tiles == 2:
        halves = merge_pairs([sym[0][0], sym[1][1]])
        halves = [rounded(h) for h in halves]
        crossed = matmul_t(matmul(halves[0], sym[0][1]), halves[1])
        zeros64 = jnp.zeros((64, LANES), jnp.float32)

        def spread(a, b):
            return jnp.concatenate([a, b, zeros64], axis=0)

        pad = jnp.zeros((RANK, LANES), jnp.float32)
        first = spread(halves[0], pad)
        second = spread(pad, halves[1])
        upper_part = matmul_t(matmul(first, sym[0][1]), second)
        last = (
            matmul_t(matmul(first, sym[0][0]), first)
            + matmul_t(matmul(second, sym[1][1]), second)
            + upper_part
            + upper_part.T
        )
        sources = [first, second]
    elif ny == 4:
        tops = top_rows([(sym[0][0], 0), (sym[0][0], 1)])
        joined = jnp.concatenate(
            [rounded(tops[0]), rounded(tops[1]), jnp.zeros((64, LANES), jnp.float32)], axis=0
        )
        last = matmul_t(matmul(joined, sym[0][0]), joined)
        sources = [joined]
    else:
        last = sym[0][0]
        row = lax.broadcasted_iota(jnp.int32, (LANES, LANES), 0)
        col = lax.broadcasted_iota(jnp.int32, (LANES, LANES), 1)
        sources = [jnp.where(row == col, 1.0, 0.0).astype(jnp.float32)]
    top = rounded(top_rows([(last, 0)])[0])
    bent = matmul(top, last)
    place = jnp.concatenate(
        [jnp.zeros((64, LANES), jnp.float32), top, jnp.zeros((32, LANES), jnp.float32)], axis=0
    )
    final = factor_rows(top + matmul_t(bent, place), 64)
    final = jnp.where(half_mask(RANK, 0), final, 0.0)
    weights = jnp.concatenate([matmul(final, s) for s in sources], axis=1)[:, :big]
    weights = weights.astype(jnp.bfloat16)

    mine = half * c + per * y
    for r in range(per):
        tall_rows = jnp.concatenate([a_all[b, r] for b in range(ny)], axis=0)
        f_all[mine + r] = dot(weights, tall_rows, ((1,), (0,))).astype(jnp.bfloat16)
    here = f_all.at[pl.ds(mine, per)]
    copies = exchange(ny, y, dev_y, lambda q: here, here)
    stage = stage_count[0]
    stage_count[0] += 1

    def hand_over(d):
        owner = lax.rem(y + ny - d, ny)
        block = f_all.at[pl.ds(half * c + per * owner, per)]
        copy = pltpu.make_async_remote_copy(
            src_ref=block, dst_ref=block,
            send_sem=send.at[stage, d], recv_sem=recv.at[stage, d],
            device_id=partner, device_id_type=MESH,
        )
        copy.start()
        pending.append(copy)
        return copy

    handed = [hand_over(0)]
    for d in sorted(copies, key=lambda d: min(d, ny - d)):
        copies[d].wait_recv()
        handed.append(hand_over(d))
    for copy in handed:
        copy.wait_recv()

    coef = jnp.zeros((RANK, 64), jnp.float32)
    for r in range(0, 2 * half, 2):
        a = jnp.concatenate([f_all[r], f_all[r + 1]], axis=1)
        b = jnp.concatenate([y_ref[r], y_ref[r + 1]], axis=1)
        coef = coef + dot(a, b, ((1,), (1,)))
    coef_x[x] = jnp.concatenate([coef[:16], coef[16:]], axis=1)
    copies = exchange(nx, x, dev_x, lambda q: coef_x.at[x], coef_x.at[x])
    arrive(copies)
    coef_z[z] = jnp.sum(coef_x[...], axis=0)
    copies = exchange(nz, z, dev_z, lambda q: coef_z.at[z], coef_z.at[z])
    arrive(copies)
    packed = jnp.sum(coef_z[...], axis=0)
    solved = jnp.concatenate([packed[:, :64], packed[:, 64:]], axis=0).astype(jnp.bfloat16)

    solved_t = solved.T
    for r in range(height):
        grid[pl.ds(r * 64, 64), :] = dot(solved_t, f_all[r], ((1,), (0,)))

    def lay_out(s, carry):
        parts = [
            grid[pl.ds(8 * k * 64 + s, 8, stride=64), :] for k in range((height + 7) // 8)
        ]
        out_ref[s] = jnp.concatenate(parts, axis=0)[:height].astype(jnp.bfloat16)
        return carry

    lax.fori_loop(0, 64, lay_out, 0, unroll=4)
    for copy in pending:
        copy.wait_send()


def merge_call(residuals, diffusivity, ny, nx, nz):
    height = residuals.shape[1]
    nxc = 2 * nx
    unit = 2 * ny
    padded = -(-height // unit) * unit
    while (padded // 2) % 2:
        padded += unit
    half = padded // 2
    per = half // ny
    tall = RANK * (ny + 1)
    piece2 = -(-tall // (8 * nxc)) * 8
    f32, bf16 = jnp.float32, jnp.bfloat16
    vm = pltpu.VMEM
    reach = -(-(ROW_BASE + height + PASSES) // 8) * 8
    last = -(-(ROW_BASE + height) // 8) * 8
    tall_h = -(-height // 16) * 16
    sems = max(8, nxc, ny, nz)
    return pl.pallas_call(
        functools.partial(merge_kernel, ny, nx, nz),
        out_shape=jax.ShapeDtypeStruct(residuals.shape, bf16),
        in_specs=[pl.BlockSpec(memory_space=pl.ANY), pl.BlockSpec(memory_space=pltpu.VMEM)],
        out_specs=pl.BlockSpec(memory_space=pltpu.VMEM),
        scratch_shapes=[
            vm(residuals.shape, bf16),
            vm((2, 64, reach + 8, LANES), f32),
            vm((2, 4, reach + 8, LANES), f32),
            vm((2, 4, reach + 8, LANES), f32),
            vm((16, 5, reach + 8, LANES), f32),
            vm((2, 5, reach + 8, LANES), f32),
            vm((max(last - 8, -(-height // 8) * 8) * 64, LANES), f32),
            vm((padded, 64, LANES), bf16),
            vm((4, tall_h, LANES), bf16),
            vm((2, 4, 8, LANES), bf16),
            vm((2, PASSES, 64, LANES), bf16),
            vm((2, 8, LANES), f32),
            vm((2, PASSES, 64, LANES), bf16),
            vm((2, 4, tall_h, LANES), bf16),
            vm((2, 3, 4, 8, LANES), bf16),
            vm((2, height, LANES), f32),
            vm((2, 3, 8, LANES), f32),
            vm((2, half, 64, LANES), bf16),
            vm((nxc, LANES // nxc, LANES), f32),
            vm((nxc, LANES // nxc, LANES), f32),
            vm((nz, LANES // nxc, LANES), f32),
            vm((nxc, LANES // nxc, LANES), f32),
            vm((half, RANK, LANES), bf16),
            vm((ny, per, RANK, LANES), bf16),
            vm((nxc, piece2, LANES), f32),
            vm((nxc, piece2, LANES), f32),
            vm((ny, piece2, LANES), f32),
            vm((nz, piece2, LANES), f32),
            vm((nxc, piece2, LANES), f32),
            vm((padded, RANK, LANES), bf16),
            vm((nx, 16, LANES), f32),
            vm((nz, 16, LANES), f32),
            pltpu.SemaphoreType.DMA((16, sems)),
            pltpu.SemaphoreType.DMA((16, sems)),
            pltpu.SemaphoreType.DMA,
        ],
        compiler_params=pltpu.CompilerParams(collective_id=0, has_side_effects=True),
        name="merge",
    )(residuals, diffusivity)


def shards(residuals, diffusivity):
    return merge_call(
        residuals, diffusivity,
        lax.axis_size("tm") // 2, lax.axis_size("lat"), lax.axis_size("lon"),
    )


def solution(mesh):
    return jax.shard_map(
        shards,
        mesh=mesh,
        in_specs=(P("tm", "lat", "lon"), P("lat", "lon")),
        out_specs=P("tm", "lat", "lon"),
        check_vma=False,
    )
```

```python
import functools
import math

import jax
import jax.numpy as jnp
from jax import lax
from jax.experimental import pallas as pl
from jax.experimental.pallas import tpu as pltpu
from jax.sharding import PartitionSpec as P

RANK = 32
PASSES = 4
POWER = 3
LANES = 128
ROW_BASE = 11
HIGHEST = lax.Precision.HIGHEST
MESH = pl.DeviceIdType.MESH


def dot(a, b, dims, precision=None):
    return lax.dot_general(
        a, b, (dims, ((), ())), precision=precision, preferred_element_type=jnp.float32
    )


def matmul(a, b):
    return dot(a, b, ((1,), (0,)), HIGHEST)


def matmul_t(a, b):
    return dot(a, b, ((1,), (1,)), HIGHEST)


def rounded(a):
    return a.astype(jnp.bfloat16).astype(jnp.float32)


def factor_rows(m, start, block=8):
    count = RANK // 8
    v = [m[8 * i : 8 * i + 8] for i in range(count)]
    sub = lax.broadcasted_iota(jnp.int32, (8, LANES), 0)
    lane = lax.broadcasted_iota(jnp.int32, (8, LANES), 1)

    def column(x, j):
        return jnp.broadcast_to(x[:, start + j : start + j + 1], (8, LANES))

    for k in range(0, RANK, block):
        b, s = k // 8, k % 8
        row = [jnp.broadcast_to(v[b][s + j : s + j + 1, :], (8, LANES)) for j in range(block)]
        diag = {(i, j): column(row[i], k + j) for i in range(block) for j in range(i, block)}
        cols = [[column(v[i], k + j) for j in range(block)] for i in range(b, count)]
        inverse = []
        for i in range(block):
            inverse.append(1.0 / diag[i, i])
            ratio = {j: diag[i, j] * inverse[i] for j in range(i + 1, block)}
            for j in range(i + 1, block):
                for n in range(j, block):
                    diag[j, n] = diag[j, n] - ratio[j] * diag[i, n]
                row[j] = row[j] - ratio[j] * row[i]
                for c in cols:
                    c[j] = c[j] - c[i] * ratio[j]
        scaled = [row[i] * inverse[i] for i in range(block)]
        for i in range(b, count):
            total = None
            for j in range(block):
                if i == b and s + j == 7:
                    continue
                c = cols[i - b][j]
                if i == b:
                    c = jnp.where(sub > s + j, c, 0.0)
                term = c * scaled[j]
                total = term if total is None else total + term
            if total is not None:
                v[i] = v[i] - total
    out = []
    for i in range(count):
        pivot = jnp.sum(
            jnp.where(lane == sub + (start + 8 * i), v[i], 0.0), axis=1, keepdims=True
        )
        out.append(v[i] * lax.rsqrt(pivot))
    return jnp.concatenate(out, axis=0)


def half_mask(rows, side):
    lane = lax.broadcasted_iota(jnp.int32, (rows, LANES), 1)
    return (lane < 64) if side == 0 else (lane >= 64)


def inner_beside(p, side):
    start = 64 * (1 - side)
    parts = []
    if start:
        parts.append(jnp.zeros((start, LANES), jnp.float32))
    parts.append(p)
    parts.append(jnp.zeros((LANES - start - RANK, LANES), jnp.float32))
    return p + matmul_t(p, jnp.concatenate(parts, axis=0))


def top_rows(problems):
    row = lax.broadcasted_iota(jnp.int32, (RANK, LANES), 0)
    lane = lax.broadcasted_iota(jnp.int32, (RANK, LANES), 1)
    starts = tuple(
        jnp.where(lane == row + 64 * side, 1.0, 0.0).astype(jnp.float32) for _, side in problems
    )

    def body(_, bases):
        out = []
        for (gram, side), p in zip(problems, bases):
            keep = half_mask(RANK, side)
            p = jnp.where(keep, matmul(p, gram), 0.0)
            out.append((inner_beside(p, side), side, keep))
        return tuple(
            jnp.where(keep, factor_rows(m, 64 * (1 - side)), 0.0) for m, side, keep in out
        )

    return lax.fori_loop(0, POWER + 1, body, starts)


def merge_pairs(grams):
    problems = [(g, side) for g in grams for side in (0, 1)]
    tops = top_rows(problems)
    zeros = jnp.zeros((64, LANES), jnp.float32)
    joined = [
        jnp.concatenate([rounded(tops[2 * i]), rounded(tops[2 * i + 1]), zeros], axis=0)
        for i in range(len(grams))
    ]
    merged = [matmul_t(matmul(j, g), j) for j, g in zip(joined, grams)]
    second = top_rows([(m, 0) for m in merged])
    return [matmul(rounded(p), j) for p, j in zip(second, joined)]


def order_of(n):
    return sorted(range(1, n), key=lambda d: -min(d, n - d))


def merge_kernel(
    ny, nx, nz, res_hbm, dif_ref, out_ref,
    res_ref, field_a, field_b, west_a, west_b, east_a, east_b, coef_0, coef_m, coef_s, grid, y_ref, pack, pack_edge, edge_rows, dif_edge,
    got_rows, got_pack, got_edge, got_dif, got_dif_edge,
    pair, gram_part, gram_rs, gram_z, gram_ag,
    a_own, a_all, g2_part, g2_rs, g2_y, g2_z, g2_ag,
    f_all, coef_x, coef_z,
    send, recv, load_sem,
):
    t, x, z = lax.axis_index("tm"), lax.axis_index("lat"), lax.axis_index("lon")
    y, c = t // 2, lax.rem(t, 2)
    nxc = 2 * nx
    p = x * 2 + c
    half = y_ref.shape[0] // 2
    per = half // ny

    def dev_xc(q):
        return (y * 2 + lax.rem(q, 2), q // 2, z)

    def dev_x(q):
        return (t, q, z)

    def dev_z(q):
        return (t, x, q)

    def dev_y(q):
        return (q * 2 + c, x, z)

    partner = (y * 2 + (1 - c), x, z)
    def dev_around(dx, dz):
        return (t, lax.rem(x + dx + nx, nx), lax.rem(z + dz + nz, nz))

    load = pltpu.make_async_copy(res_hbm, res_ref, load_sem)
    load.start()
    corners = [(dx, dz) for dx in (-1, 1) for dz in (-1, 1)]
    barrier = pltpu.get_barrier_semaphore()
    groups = ((nxc, p, dev_xc), (nz, z, dev_z), (ny, y, dev_y))
    for n, me, dev in groups:
        for d in range(1, n):
            pl.semaphore_signal(
                barrier, inc=1, device_id=dev(lax.rem(me + d, n)), device_id_type=MESH
            )
    for dx, dz in corners:
        pl.semaphore_signal(barrier, inc=1, device_id=dev_around(dx, dz), device_id_type=MESH)

    pending = []
    stage_count = [0]

    def exchange(n, me, dev, source, target):
        stage = stage_count[0]
        stage_count[0] += 1
        copies = {}
        for d in order_of(n):
            q = lax.rem(me + d, n)
            copy = pltpu.make_async_remote_copy(
                src_ref=source(q), dst_ref=target,
                send_sem=send.at[stage, d], recv_sem=recv.at[stage, d],
                device_id=dev(q), device_id_type=MESH,
            )
            copy.start()
            copies[d] = copy
            pending.append(copy)
        return copies

    def arrive(copies):
        for d in sorted(copies, key=lambda d: min(d, len(copies) + 1 - d)):
            copies[d].wait_recv()

    height = res_ref.shape[0]
    base, edge = ROW_BASE, PASSES
    lane8 = lax.broadcasted_iota(jnp.int32, (8, LANES), 1)
    lane_h = lax.broadcasted_iota(jnp.int32, (height, LANES), 1)
    load.wait()
    for r in range(height):
        grid[pl.ds(r * 64, 64), :] = res_ref[r].astype(jnp.float32)

    def take_in(g, carry):
        def one(j, acc):
            s = 16 * g + j
            parts = [
                grid[pl.ds(8 * k * 64 + s, 8, stride=64), :] for k in range((height + 7) // 8)
            ]
            value = pltpu.roll(jnp.concatenate(parts, axis=0)[:height], 8 * j + 4, 1)
            field_a[s, pl.ds(base, height), :] = value
            return jnp.where(lane_h // 8 == j, value, acc)

        acc = lax.fori_loop(0, 16, one, jnp.zeros((height, LANES), jnp.float32), unroll=4)
        west_a[g, pl.ds(base, height), :] = acc
        east_a[g, pl.ds(base, height), :] = acc
        pack[g, pl.ds(0, height), :] = acc.astype(jnp.bfloat16)
        pack_edge[0, g, pl.ds(0, edge), :] = acc[:edge].astype(jnp.bfloat16)
        pack_edge[1, g, pl.ds(0, edge), :] = acc[height - edge :].astype(jnp.bfloat16)
        return carry

    lax.fori_loop(0, 4, take_in, 0)
    for side, first in ((0, 0), (1, height - edge)):
        for e in range(edge):
            edge_rows[side, e] = field_a[:, base + first + e, :].astype(jnp.bfloat16)
    dif_edge[0, pl.ds(0, edge), :] = dif_ref[pl.ds(0, edge), :]
    dif_edge[1, pl.ds(0, edge), :] = dif_ref[pl.ds(height - edge, edge), :]
    pl.semaphore_wait(barrier, sum(n - 1 for n, _, _ in groups) + len(corners))

    stage = stage_count[0]
    stage_count[0] += 3
    halo = []

    def pass_on(source, target, dx, dz):
        at = len(halo)
        copy = pltpu.make_async_remote_copy(
            src_ref=source, dst_ref=target,
            send_sem=send.at[stage + at // 8, at % 8], recv_sem=recv.at[stage + at // 8, at % 8],
            device_id=dev_around(dx, dz), device_id_type=MESH,
        )
        copy.start()
        halo.append(copy)
        pending.append(copy)

    for side, dx in ((0, -1), (1, 1)):
        for dz in (-1, 1):
            pass_on(pack_edge.at[side], got_edge.at[side, dz + 1], dx, dz)
            pass_on(dif_edge.at[side], got_dif_edge.at[side, dz + 1], dx, dz)
        pass_on(pack_edge.at[side], got_edge.at[side, 1], dx, 0)
        pass_on(dif_edge.at[side], got_dif_edge.at[side, 1], dx, 0)
        pass_on(edge_rows.at[side], got_rows.at[side], dx, 0)
    for dz in (-1, 1):
        pass_on(pack, got_pack.at[(dz + 1) // 2], 0, dz)
        pass_on(dif_ref, got_dif.at[(dz + 1) // 2], 0, dz)
    for copy in halo:
        copy.wait_recv()

    has_north, has_south = x > 0, x < nx - 1
    for side, first, there in ((1, base - edge, has_north), (0, base + height, has_south)):
        for e in range(edge):
            row = got_rows[side, e].astype(jnp.float32)
            row = jnp.where(there, row, 0.0)
            field_a[:, first + e, :] = row

    def seam(own, other, rows, own_first):
        t8 = lax.broadcasted_iota(jnp.int32, (rows, LANES), 1) % 8
        return jnp.where((t8 < 4) == own_first, own, other)

    for g in range(4):
        own = west_a[g, pl.ds(base, height), :]
        from_west = got_pack[1, g, pl.ds(0, height), :].astype(jnp.float32)
        from_east = got_pack[0, g, pl.ds(0, height), :].astype(jnp.float32)
        west_a[g, pl.ds(base, height), :] = seam(own, from_west, height, False)
        east_a[g, pl.ds(base, height), :] = seam(own, from_east, height, True)
        for side, first, there in ((1, base - edge, has_north), (0, base + height, has_south)):
            own, from_west, from_east = (
                jnp.where(
                    there, got_edge[side, k, g, pl.ds(0, edge), :].astype(jnp.float32), 0.0
                )
                for k in (1, 2, 0)
            )
            west_a[g, pl.ds(first, edge), :] = seam(own, from_west, edge, False)
            east_a[g, pl.ds(first, edge), :] = seam(own, from_east, edge, True)

    wide = height + 2 * edge

    def tall_of(middle, k):
        north = jnp.where(has_north, got_dif_edge[1, k, pl.ds(0, edge), :], 0.0)
        south = jnp.where(has_south, got_dif_edge[0, k, pl.ds(0, edge), :], 0.0)
        return jnp.concatenate([north, middle, south], axis=0)

    own_d = tall_of(dif_ref[...], 1)
    west_d = tall_of(got_dif[1], 2)
    east_d = tall_of(got_dif[0], 0)
    lane_w = lax.broadcasted_iota(jnp.int32, (wide, LANES), 1)
    row_w = lax.broadcasted_iota(jnp.int32, (wide, LANES), 0)
    inside = ((row_w >= edge) | has_north) & ((row_w < height + edge) | has_south)

    def five(center, left, right):
        zero_row = jnp.zeros((1, LANES), jnp.float32)
        up = jnp.concatenate([zero_row, center[:-1]], axis=0)
        down = jnp.concatenate([center[1:], zero_row], axis=0)
        ks = [jnp.where(inside, 0.5 * (center + v), 0.0) for v in (up, down, left, right)]
        return [1.0 - (ks[0] + ks[1] + ks[2] + ks[3])] + ks

    left = jnp.where(lane_w == 0, pltpu.roll(west_d, 1, 1), pltpu.roll(own_d, 1, 1))
    right = jnp.where(lane_w == LANES - 1, pltpu.roll(east_d, LANES - 1, 1), pltpu.roll(own_d, LANES - 1, 1))
    main = five(own_d, left, right)
    for k in range(5):
        coef_0[k, pl.ds(base - edge, wide), :] = main[k]

    def turn(j, carry):
        for k in range(5):
            coef_m[j, k, pl.ds(base - edge, wide), :] = pltpu.roll(
                coef_0[k, pl.ds(base - edge, wide), :], 8 * j + 4, 1
            )
        return carry

    lax.fori_loop(0, 16, turn, 0)
    for which, (first_d, second_d) in enumerate(((west_d, own_d), (own_d, east_d))):
        strip = jnp.where(
            lane_w < 4,
            pltpu.roll(first_d, 4, 1),
            jnp.where(lane_w < 8, pltpu.roll(second_d, 4, 1), 0.0),
        )
        for shift in (8, 16, 32, 64):
            strip = strip + pltpu.roll(strip, shift, 1)
        ks = five(strip, pltpu.roll(strip, 1, 1), pltpu.roll(strip, LANES - 1, 1))
        for k in range(5):
            coef_s[which, k, pl.ds(base - edge, wide), :] = ks[k]

    def weighted_sum(c, center, north, south, left, right):
        return center * c[0] + north * c[1] + south * c[2] + left * c[3] + right * c[4]

    tile_rows = [8 * k for k in range(1, (base + height + edge + 7) // 8)]

    def stencil_rows(field, west, east, j, tiles, finish):
        for r in tiles:
            here = pl.ds(r, 8)
            c = [coef_m[j, k, here, :] for k in range(5)]
            for g in range(4):
                s = 16 * g + j
                center = field[s, here, :]
                lft = jnp.where(lane8 == 8 * j + 3, west[g, here, :], center)
                rgt = jnp.where(lane8 == 8 * j + 4, east[g, here, :], center)
                finish(
                    s, r,
                    weighted_sum(
                        c, center, field[s, pl.ds(r - 1, 8), :],
                        field[s, pl.ds(r + 1, 8), :],
                        pltpu.roll(lft, 1, 1), pltpu.roll(rgt, LANES - 1, 1),
                    ),
                )

    def one_pass(field, west, east, field_to, west_to, east_to):
        def keep(s, r, value):
            field_to[s, pl.ds(r, 8), :] = value

        def each(j, carry):
            stencil_rows(field, west, east, j, tile_rows, keep)
            return carry

        lax.fori_loop(0, 16, each, 0)
        for which, (strip, strip_to) in enumerate(((west, west_to), (east, east_to))):
            for r in tile_rows:
                here = pl.ds(r, 8)
                c = [coef_s[which, k, here, :] for k in range(5)]
                for g in range(4):
                    center = strip[g, here, :]
                    strip_to[g, here, :] = weighted_sum(
                        c, center, strip[g, pl.ds(r - 1, 8), :], strip[g, pl.ds(r + 1, 8), :],
                        pltpu.roll(center, 1, 1), pltpu.roll(center, LANES - 1, 1),
                    )

    states = ((field_a, west_a, east_a), (field_b, west_b, east_b))
    for number in range(PASSES - 1):
        one_pass(*states[number % 2], *states[1 - number % 2])
    last_rows = [8 * k for k in range(1, (base + height + 7) // 8)]
    skip = base - 8
    sub8 = lax.broadcasted_iota(jnp.int32, (8, LANES), 0)

    def scale_of(r):
        row = (x * height + sub8 + (r - base)).astype(jnp.float32)
        latitude = (row + 0.5) * math.pi / (height * nx) - math.pi / 2
        return jnp.sqrt(jnp.maximum(jnp.cos(latitude), 0.0))

    scales = {r: scale_of(r) for r in last_rows}

    def last_pass(j, carry):
        def out(s, r, value):
            value = pltpu.roll(value * scales[r], LANES - 4 - 8 * j, 1)
            grid[pl.ds((r - 8) * 64 + s, 8, stride=64), :] = value

        stencil_rows(*states[(PASSES - 1) % 2], j, last_rows, out)
        return carry

    lax.fori_loop(0, 16, last_pass, 0)
    for i in range(height):
        y_ref[i] = grid[pl.ds((i + skip) * 64, 64), :].astype(jnp.bfloat16)
    for i in range(height, y_ref.shape[0]):
        y_ref[i] = jnp.zeros((64, LANES), jnp.bfloat16)

    stage = stage_count[0]
    stage_count[0] += 1
    swap = pltpu.make_async_remote_copy(
        src_ref=y_ref.at[pl.ds(half * (1 - c), half)], dst_ref=pair.at[c],
        send_sem=send.at[stage, 0], recv_sem=recv.at[stage, 0],
        device_id=partner, device_id_type=MESH,
    )
    swap.start()
    pending.append(swap)
    pair[c] = y_ref[pl.ds(half * c, half)]
    swap.wait_recv()

    def rows_of(r):
        return jnp.concatenate([pair[0, r], pair[1, r]], axis=0)

    total = jnp.zeros((LANES, LANES), jnp.float32)
    for r in range(0, half, 2):
        wide = jnp.concatenate([rows_of(r), rows_of(r + 1)], axis=1)
        total = total + dot(wide, wide, ((1,), (1,)))
    piece = LANES // nxc
    gram_part[...] = total.reshape(nxc, piece, LANES)
    copies = exchange(nxc, p, dev_xc, lambda q: gram_part.at[q], gram_rs.at[p])
    gram_rs[p] = gram_part[p]
    arrive(copies)
    gram_z[z] = jnp.sum(gram_rs[...], axis=0)
    copies = exchange(nz, z, dev_z, lambda q: gram_z.at[z], gram_z.at[z])
    arrive(copies)
    gram_ag[p] = jnp.sum(gram_z[...], axis=0)
    copies = exchange(nxc, p, dev_xc, lambda q: gram_ag.at[p], gram_ag.at[p])
    arrive(copies)
    gram = gram_ag[...].reshape(LANES, LANES)

    basis = merge_pairs([gram])[0].astype(jnp.bfloat16)

    for r in range(0, half, 2):
        wide = jnp.concatenate([rows_of(r), rows_of(r + 1)], axis=1)
        modes = dot(basis, wide, ((1,), (0,))).astype(jnp.bfloat16)
        a_own[r] = modes[:, :LANES]
        a_own[r + 1] = modes[:, LANES:]
    copies = exchange(ny, y, dev_y, lambda q: a_own.at[pl.ds(per * q, per)], a_all.at[y])
    a_all[y] = a_own[pl.ds(per * y, per)]
    arrive(copies)

    stacked = jnp.concatenate(
        [
            jnp.concatenate([a_all[b, r] for b in range(ny)], axis=0)
            for r in range(per)
        ],
        axis=1,
    )
    big = ny * RANK
    full = dot(stacked, stacked, ((1,), (1,)))
    width = full.shape[1]
    near = ny // 2
    if width % LANES:
        full = jnp.concatenate(
            [full, jnp.zeros((big, LANES - width % LANES), jnp.float32)], axis=1
        )
    tiles = full.shape[1] // LANES
    lane = lax.broadcasted_iota(jnp.int32, (RANK, LANES), 1)

    def lane_window(block, shift):
        if width < LANES:
            rolled = block if shift == 0 else jnp.where(
                lane < width - shift, pltpu.roll(block, LANES - shift, 1),
                pltpu.roll(block, (width - shift) % LANES, 1),
            )
            return rolled
        first, inner = shift // LANES, shift % LANES
        a = block[:, LANES * first : LANES * first + LANES]
        if inner == 0:
            return a
        nxt = (first + 1) % tiles
        bb = block[:, LANES * nxt : LANES * nxt + LANES]
        return jnp.where(
            lane < LANES - inner, pltpu.roll(a, LANES - inner, 1), pltpu.roll(bb, LANES - inner, 1)
        )

    pieces = []
    for b in range(ny):
        window = lane_window(full[RANK * b : RANK * b + RANK], RANK * b)
        pieces.append(jnp.where(lane < RANK * near, window, 0.0))
    extra = jnp.zeros((RANK, LANES), jnp.float32)
    for q in range(near):
        col = RANK * (q + near)
        tile, inner = col // LANES, col % LANES
        block = full[RANK * q : RANK * q + RANK, LANES * tile : LANES * tile + LANES]
        shift = (RANK * q - inner) % LANES
        if shift:
            block = pltpu.roll(block, shift, 1)
        extra = jnp.where((lane >= RANK * q) & (lane < RANK * q + RANK), block, extra)
    pieces.append(extra)
    tall = g2_part.shape[0] * g2_part.shape[1] - RANK * (ny + 1)
    if tall:
        pieces.append(jnp.zeros((tall, LANES), jnp.float32))
    g2_part[...] = jnp.concatenate(pieces, axis=0).reshape(g2_part.shape)
    copies = exchange(nxc, p, dev_xc, lambda q: g2_part.at[q], g2_rs.at[p])
    g2_rs[p] = g2_part[p]
    arrive(copies)
    g2_y[y] = jnp.sum(g2_rs[...], axis=0)
    copies = exchange(ny, y, dev_y, lambda q: g2_y.at[y], g2_y.at[y])
    arrive(copies)
    g2_z[z] = jnp.sum(g2_y[...], axis=0)
    copies = exchange(nz, z, dev_z, lambda q: g2_z.at[z], g2_z.at[z])
    arrive(copies)
    g2_ag[p] = jnp.sum(g2_z[...], axis=0)
    copies = exchange(nxc, p, dev_xc, lambda q: g2_ag.at[p], g2_ag.at[p])
    arrive(copies)
    flat = g2_ag[...].reshape(g2_ag.shape[0] * g2_ag.shape[1], LANES)

    zero = jnp.zeros((RANK, LANES), jnp.float32)
    upper = [[None] * tiles for _ in range(ny)]
    extra = flat[RANK * ny : RANK * ny + RANK]
    for b in range(ny):
        block = flat[RANK * b : RANK * b + RANK]
        block = jnp.where(lane < RANK, 0.5 * block, block)
        for tile in range(tiles):
            got = zero
            for off in range(near):
                col = (RANK * (b + off)) % width
                if col // LANES != tile:
                    continue
                inner = col % LANES
                shift = (inner - RANK * off) % LANES
                moved = pltpu.roll(block, shift, 1) if shift else block
                got = jnp.where((lane >= inner) & (lane < inner + RANK), moved, got)
            if b < near:
                col = RANK * (b + near)
                if col // LANES == tile:
                    inner = col % LANES
                    shift = (inner - RANK * b) % LANES
                    moved = pltpu.roll(extra, shift, 1) if shift else extra
                    got = jnp.where((lane >= inner) & (lane < inner + RANK), moved, got)
            upper[b][tile] = got
    per_tile = LANES // RANK

    def tile_value(i, j):
        rows = [upper[b][j] for b in range(per_tile * i, min(per_tile * i + per_tile, ny))]
        rows += [zero] * (per_tile - len(rows))
        return jnp.concatenate(rows, axis=0)

    up = [[tile_value(i, j) for j in range(tiles)] for i in range(tiles)]
    sym = [[up[i][j] + up[j][i].T for j in range(tiles)] for i in range(tiles)]

    if tiles == 2:
        halves = merge_pairs([sym[0][0], sym[1][1]])
        halves = [rounded(h) for h in halves]
        crossed = matmul_t(matmul(halves[0], sym[0][1]), halves[1])
        zeros64 = jnp.zeros((64, LANES), jnp.float32)

        def spread(a, b):
            return jnp.concatenate([a, b, zeros64], axis=0)

        pad = jnp.zeros((RANK, LANES), jnp.float32)
        first = spread(halves[0], pad)
        second = spread(pad, halves[1])
        upper_part = matmul_t(matmul(first, sym[0][1]), second)
        last = (
            matmul_t(matmul(first, sym[0][0]), first)
            + matmul_t(matmul(second, sym[1][1]), second)
            + upper_part
            + upper_part.T
        )
        sources = [first, second]
    elif ny == 4:
        tops = top_rows([(sym[0][0], 0), (sym[0][0], 1)])
        joined = jnp.concatenate(
            [rounded(tops[0]), rounded(tops[1]), jnp.zeros((64, LANES), jnp.float32)], axis=0
        )
        last = matmul_t(matmul(joined, sym[0][0]), joined)
        sources = [joined]
    else:
        last = sym[0][0]
        row = lax.broadcasted_iota(jnp.int32, (LANES, LANES), 0)
        col = lax.broadcasted_iota(jnp.int32, (LANES, LANES), 1)
        sources = [jnp.where(row == col, 1.0, 0.0).astype(jnp.float32)]
    top = rounded(top_rows([(last, 0)])[0])
    bent = matmul(top, last)
    place = jnp.concatenate(
        [jnp.zeros((64, LANES), jnp.float32), top, jnp.zeros((32, LANES), jnp.float32)], axis=0
    )
    final = factor_rows(top + matmul_t(bent, place), 64)
    final = jnp.where(half_mask(RANK, 0), final, 0.0)
    weights = jnp.concatenate([matmul(final, s) for s in sources], axis=1)[:, :big]
    weights = weights.astype(jnp.bfloat16)

    mine = half * c + per * y
    for r in range(per):
        tall_rows = jnp.concatenate([a_all[b, r] for b in range(ny)], axis=0)
        f_all[mine + r] = dot(weights, tall_rows, ((1,), (0,))).astype(jnp.bfloat16)
    here = f_all.at[pl.ds(mine, per)]
    copies = exchange(ny, y, dev_y, lambda q: here, here)
    stage = stage_count[0]
    stage_count[0] += 1

    def hand_over(d):
        owner = lax.rem(y + ny - d, ny)
        block = f_all.at[pl.ds(half * c + per * owner, per)]
        copy = pltpu.make_async_remote_copy(
            src_ref=block, dst_ref=block,
            send_sem=send.at[stage, d], recv_sem=recv.at[stage, d],
            device_id=partner, device_id_type=MESH,
        )
        copy.start()
        pending.append(copy)
        return copy

    handed = [hand_over(0)]
    for d in sorted(copies, key=lambda d: min(d, ny - d)):
        copies[d].wait_recv()
        handed.append(hand_over(d))
    for copy in handed:
        copy.wait_recv()

    coef = jnp.zeros((RANK, 64), jnp.float32)
    for r in range(0, 2 * half, 2):
        a = jnp.concatenate([f_all[r], f_all[r + 1]], axis=1)
        b = jnp.concatenate([y_ref[r], y_ref[r + 1]], axis=1)
        coef = coef + dot(a, b, ((1,), (1,)))
    coef_x[x] = jnp.concatenate([coef[:16], coef[16:]], axis=1)
    copies = exchange(nx, x, dev_x, lambda q: coef_x.at[x], coef_x.at[x])
    arrive(copies)
    coef_z[z] = jnp.sum(coef_x[...], axis=0)
    copies = exchange(nz, z, dev_z, lambda q: coef_z.at[z], coef_z.at[z])
    arrive(copies)
    packed = jnp.sum(coef_z[...], axis=0)
    solved = jnp.concatenate([packed[:, :64], packed[:, 64:]], axis=0).astype(jnp.bfloat16)

    solved_t = solved.T
    for r in range(height):
        out_ref[r] = dot(solved_t, f_all[r], ((1,), (0,))).astype(jnp.bfloat16)
    for copy in pending:
        copy.wait_send()


def merge_call(residuals, diffusivity, ny, nx, nz):
    height = residuals.shape[0]
    nxc = 2 * nx
    unit = 2 * ny
    padded = -(-height // unit) * unit
    while (padded // 2) % 2:
        padded += unit
    half = padded // 2
    per = half // ny
    tall = RANK * (ny + 1)
    piece2 = -(-tall // (8 * nxc)) * 8
    f32, bf16 = jnp.float32, jnp.bfloat16
    vm = pltpu.VMEM
    reach = -(-(ROW_BASE + height + PASSES) // 8) * 8
    last = -(-(ROW_BASE + height) // 8) * 8
    tall_h = -(-height // 16) * 16
    sems = max(8, nxc, ny, nz)
    return pl.pallas_call(
        functools.partial(merge_kernel, ny, nx, nz),
        out_shape=jax.ShapeDtypeStruct(residuals.shape, bf16),
        in_specs=[pl.BlockSpec(memory_space=pl.ANY), pl.BlockSpec(memory_space=pltpu.VMEM)],
        out_specs=pl.BlockSpec(memory_space=pltpu.VMEM),
        scratch_shapes=[
            vm(residuals.shape, bf16),
            vm((64, reach + 8, LANES), f32),
            vm((64, reach + 8, LANES), f32),
            vm((4, reach + 8, LANES), f32),
            vm((4, reach + 8, LANES), f32),
            vm((4, reach + 8, LANES), f32),
            vm((4, reach + 8, LANES), f32),
            vm((5, reach + 8, LANES), f32),
            vm((16, 5, reach + 8, LANES), f32),
            vm((2, 5, reach + 8, LANES), f32),
            vm((max(last - 8, -(-height // 8) * 8) * 64, LANES), f32),
            vm((padded, 64, LANES), bf16),
            vm((4, tall_h, LANES), bf16),
            vm((2, 4, 8, LANES), bf16),
            vm((2, PASSES, 64, LANES), bf16),
            vm((2, 8, LANES), f32),
            vm((2, PASSES, 64, LANES), bf16),
            vm((2, 4, tall_h, LANES), bf16),
            vm((2, 3, 4, 8, LANES), bf16),
            vm((2, height, LANES), f32),
            vm((2, 3, 8, LANES), f32),
            vm((2, half, 64, LANES), bf16),
            vm((nxc, LANES // nxc, LANES), f32),
            vm((nxc, LANES // nxc, LANES), f32),
            vm((nz, LANES // nxc, LANES), f32),
            vm((nxc, LANES // nxc, LANES), f32),
            vm((half, RANK, LANES), bf16),
            vm((ny, per, RANK, LANES), bf16),
            vm((nxc, piece2, LANES), f32),
            vm((nxc, piece2, LANES), f32),
            vm((ny, piece2, LANES), f32),
            vm((nz, piece2, LANES), f32),
            vm((nxc, piece2, LANES), f32),
            vm((padded, RANK, LANES), bf16),
            vm((nx, 16, LANES), f32),
            vm((nz, 16, LANES), f32),
            pltpu.SemaphoreType.DMA((16, sems)),
            pltpu.SemaphoreType.DMA((16, sems)),
            pltpu.SemaphoreType.DMA,
        ],
        compiler_params=pltpu.CompilerParams(collective_id=0, has_side_effects=True),
        name="merge",
    )(residuals, diffusivity)


def shards(residuals, diffusivity):
    projected = merge_call(
        residuals.transpose(1, 0, 2), diffusivity,
        lax.axis_size("tm") // 2, lax.axis_size("lat"), lax.axis_size("lon"),
    )
    return projected.transpose(1, 0, 2)


def solution(mesh):
    return jax.shard_map(
        shards,
        mesh=mesh,
        in_specs=(P("tm", "lat", "lon"), P("lat", "lon")),
        out_specs=P("tm", "lat", "lon"),
        check_vma=False,
    )
```

```python
import functools
import math

import jax
import jax.numpy as jnp
from jax import lax
from jax.experimental import pallas as pl
from jax.experimental.pallas import tpu as pltpu
from jax.sharding import PartitionSpec as P

RANK = 32
PASSES = 4
POWER = 3
LANES = 128
ROW_BASE = 11
HIGHEST = lax.Precision.HIGHEST
MESH = pl.DeviceIdType.MESH


def dot(a, b, dims, precision=None):
    return lax.dot_general(
        a, b, (dims, ((), ())), precision=precision, preferred_element_type=jnp.float32
    )


def matmul(a, b):
    return dot(a, b, ((1,), (0,)), HIGHEST)


def matmul_t(a, b):
    return dot(a, b, ((1,), (1,)), HIGHEST)


def rounded(a):
    return a.astype(jnp.bfloat16).astype(jnp.float32)


def factor_rows(m, start, block=8):
    count = RANK // 8
    v = [m[8 * i : 8 * i + 8] for i in range(count)]
    sub = lax.broadcasted_iota(jnp.int32, (8, LANES), 0)
    pivots = [None] * count

    def column(x, j):
        return jnp.broadcast_to(x[:, start + j : start + j + 1], (8, LANES))

    for k in range(0, RANK, block):
        b, s = k // 8, k % 8
        row = [jnp.broadcast_to(v[b][s + j : s + j + 1, :], (8, LANES)) for j in range(block)]
        diag = {(i, j): column(row[i], k + j) for i in range(block) for j in range(i, block)}
        cols = [[column(v[i], k + j) for j in range(block)] for i in range(b, count)]
        inverse = []
        for i in range(block):
            inverse.append(1.0 / diag[i, i])
            ratio = {j: diag[i, j] * inverse[i] for j in range(i + 1, block)}
            for j in range(i + 1, block):
                for n in range(j, block):
                    diag[j, n] = diag[j, n] - ratio[j] * diag[i, n]
                row[j] = row[j] - ratio[j] * row[i]
                for c in cols:
                    c[j] = c[j] - c[i] * ratio[j]
            kept = pivots[(k + i) // 8]
            pivots[(k + i) // 8] = (
                diag[i, i] if kept is None else jnp.where(sub == (k + i) % 8, diag[i, i], kept)
            )
        scaled = [row[i] * inverse[i] for i in range(block)]
        for i in range(b, count):
            total = None
            for j in range(block):
                if i == b and s + j == 7:
                    continue
                c = cols[i - b][j]
                if i == b:
                    c = jnp.where(sub > s + j, c, 0.0)
                term = c * scaled[j]
                total = term if total is None else total + term
            if total is not None:
                v[i] = v[i] - total
    return jnp.concatenate([v[i] * lax.rsqrt(pivots[i]) for i in range(count)], axis=0)


def half_mask(rows, side):
    lane = lax.broadcasted_iota(jnp.int32, (rows, LANES), 1)
    return (lane < 64) if side == 0 else (lane >= 64)


def inner_beside(p, side):
    start = 64 * (1 - side)
    parts = []
    if start:
        parts.append(jnp.zeros((start, LANES), jnp.float32))
    parts.append(p)
    parts.append(jnp.zeros((LANES - start - RANK, LANES), jnp.float32))
    return p + matmul_t(p, jnp.concatenate(parts, axis=0))


def top_rows(problems):
    def orthonormal(bases):
        keeps = [half_mask(RANK, side) for _, side in problems]
        bases = [jnp.where(keep, p, 0.0) for keep, p in zip(keeps, bases)]
        beside = [inner_beside(p, side) for (_, side), p in zip(problems, bases)]
        return tuple(
            jnp.where(keep, factor_rows(m, 64 * (1 - side)), 0.0)
            for keep, m, (_, side) in zip(keeps, beside, problems)
        )

    def body(_, bases):
        return orthonormal([matmul(p, gram) for (gram, _), p in zip(problems, bases)])

    start = orthonormal([gram[64 * side : 64 * side + RANK] for gram, side in problems])
    return lax.fori_loop(0, POWER, body, start)


def merge_pairs(grams):
    problems = [(g, side) for g in grams for side in (0, 1)]
    tops = top_rows(problems)
    zeros = jnp.zeros((64, LANES), jnp.float32)
    joined = [
        jnp.concatenate([rounded(tops[2 * i]), rounded(tops[2 * i + 1]), zeros], axis=0)
        for i in range(len(grams))
    ]
    merged = [matmul_t(matmul(j, g), j) for j, g in zip(joined, grams)]
    second = top_rows([(m, 0) for m in merged])
    return [matmul(rounded(p), j) for p, j in zip(second, joined)]


def order_of(n):
    return sorted(range(1, n), key=lambda d: -min(d, n - d))


def merge_kernel(
    ny, nx, nz, res_hbm, dif_ref, out_ref,
    res_ref, field_a, field_b, west_a, west_b, east_a, east_b, coef_0, coef_m, coef_s, grid, y_ref, pack, pack_edge, edge_rows, dif_edge,
    got_rows, got_pack, got_edge, got_dif, got_dif_edge,
    pair, gram_part, gram_rs, gram_z, gram_ag,
    a_own, a_all, g2_part, g2_rs, g2_y, g2_z, g2_ag,
    f_all, coef_x, coef_z, top_own, half_own,
    send, recv, load_sem,
):
    t, x, z = lax.axis_index("tm"), lax.axis_index("lat"), lax.axis_index("lon")
    y, c = t // 2, lax.rem(t, 2)
    nxc = 2 * nx
    p = x * 2 + c
    half = y_ref.shape[0] // 2
    per = half // ny

    def dev_xc(q):
        return (y * 2 + lax.rem(q, 2), q // 2, z)

    def dev_x(q):
        return (t, q, z)

    def dev_z(q):
        return (t, x, q)

    def dev_y(q):
        return (q * 2 + c, x, z)

    partner = (y * 2 + (1 - c), x, z)
    def dev_around(dx, dz):
        return (t, lax.rem(x + dx + nx, nx), lax.rem(z + dz + nz, nz))

    load = pltpu.make_async_copy(res_hbm, res_ref, load_sem)
    load.start()
    corners = [(dx, dz) for dx in (-1, 1) for dz in (-1, 1)]
    barrier = pltpu.get_barrier_semaphore()
    groups = ((nxc, p, dev_xc), (nz, z, dev_z), (ny, y, dev_y))
    for n, me, dev in groups:
        for d in range(1, n):
            pl.semaphore_signal(
                barrier, inc=1, device_id=dev(lax.rem(me + d, n)), device_id_type=MESH
            )
    for dx, dz in corners:
        pl.semaphore_signal(barrier, inc=1, device_id=dev_around(dx, dz), device_id_type=MESH)

    pending = []
    stage_count = [0]

    def exchange(n, me, dev, source, target):
        stage = stage_count[0]
        stage_count[0] += 1
        copies = {}
        for d in order_of(n):
            q = lax.rem(me + d, n)
            copy = pltpu.make_async_remote_copy(
                src_ref=source(q), dst_ref=target,
                send_sem=send.at[stage, d], recv_sem=recv.at[stage, d],
                device_id=dev(q), device_id_type=MESH,
            )
            copy.start()
            copies[d] = copy
            pending.append(copy)
        return copies

    def arrive(copies):
        for d in sorted(copies, key=lambda d: min(d, len(copies) + 1 - d)):
            copies[d].wait_recv()

    height = res_ref.shape[0]
    base, edge = ROW_BASE, PASSES
    lane8 = lax.broadcasted_iota(jnp.int32, (8, LANES), 1)
    lane_h = lax.broadcasted_iota(jnp.int32, (height, LANES), 1)
    load.wait()
    for r in range(height):
        grid[pl.ds(r * 72, 64), :] = res_ref[r].astype(jnp.float32)

    def take_in(g, carry):
        def one(j, acc):
            s = 16 * g + j
            parts = [
                grid[pl.ds(8 * k * 72 + s, 8, stride=72), :] for k in range((height + 7) // 8)
            ]
            value = pltpu.roll(jnp.concatenate(parts, axis=0)[:height], 8 * j + 4, 1)
            field_a[s, pl.ds(base, height), :] = value
            return jnp.where(lane_h // 8 == j, value, acc)

        acc = lax.fori_loop(0, 16, one, jnp.zeros((height, LANES), jnp.float32), unroll=8)
        west_a[g, pl.ds(base, height), :] = acc
        east_a[g, pl.ds(base, height), :] = acc
        pack[g, pl.ds(0, height), :] = acc.astype(jnp.bfloat16)
        pack_edge[0, g, pl.ds(0, edge), :] = acc[:edge].astype(jnp.bfloat16)
        pack_edge[1, g, pl.ds(0, edge), :] = acc[height - edge :].astype(jnp.bfloat16)
        return carry

    lax.fori_loop(0, 4, take_in, 0)
    for side, first in ((0, 0), (1, height - edge)):
        for e in range(edge):
            edge_rows[side, e] = field_a[:, base + first + e, :].astype(jnp.bfloat16)
    dif_edge[0, pl.ds(0, edge), :] = dif_ref[pl.ds(0, edge), :]
    dif_edge[1, pl.ds(0, edge), :] = dif_ref[pl.ds(height - edge, edge), :]
    pl.semaphore_wait(barrier, sum(n - 1 for n, _, _ in groups) + len(corners))

    stage = stage_count[0]
    stage_count[0] += 3
    halo = []

    def pass_on(source, target, dx, dz):
        at = len(halo)
        copy = pltpu.make_async_remote_copy(
            src_ref=source, dst_ref=target,
            send_sem=send.at[stage + at // 8, at % 8], recv_sem=recv.at[stage + at // 8, at % 8],
            device_id=dev_around(dx, dz), device_id_type=MESH,
        )
        copy.start()
        halo.append(copy)
        pending.append(copy)

    for side, dx in ((0, -1), (1, 1)):
        for dz in (-1, 1):
            pass_on(pack_edge.at[side], got_edge.at[side, dz + 1], dx, dz)
            pass_on(dif_edge.at[side], got_dif_edge.at[side, dz + 1], dx, dz)
        pass_on(pack_edge.at[side], got_edge.at[side, 1], dx, 0)
        pass_on(dif_edge.at[side], got_dif_edge.at[side, 1], dx, 0)
        pass_on(edge_rows.at[side], got_rows.at[side], dx, 0)
    for dz in (-1, 1):
        pass_on(pack, got_pack.at[(dz + 1) // 2], 0, dz)
        pass_on(dif_ref, got_dif.at[(dz + 1) // 2], 0, dz)
    for copy in halo:
        copy.wait_recv()

    has_north, has_south = x > 0, x < nx - 1
    for side, first, there in ((1, base - edge, has_north), (0, base + height, has_south)):
        for e in range(edge):
            row = got_rows[side, e].astype(jnp.float32)
            row = jnp.where(there, row, 0.0)
            field_a[:, first + e, :] = row

    def seam(own, other, rows, own_first):
        t8 = lax.broadcasted_iota(jnp.int32, (rows, LANES), 1) % 8
        return jnp.where((t8 < 4) == own_first, own, other)

    for g in range(4):
        own = west_a[g, pl.ds(base, height), :]
        from_west = got_pack[1, g, pl.ds(0, height), :].astype(jnp.float32)
        from_east = got_pack[0, g, pl.ds(0, height), :].astype(jnp.float32)
        west_a[g, pl.ds(base, height), :] = seam(own, from_west, height, False)
        east_a[g, pl.ds(base, height), :] = seam(own, from_east, height, True)
        for side, first, there in ((1, base - edge, has_north), (0, base + height, has_south)):
            own, from_west, from_east = (
                jnp.where(
                    there, got_edge[side, k, g, pl.ds(0, edge), :].astype(jnp.float32), 0.0
                )
                for k in (1, 2, 0)
            )
            west_a[g, pl.ds(first, edge), :] = seam(own, from_west, edge, False)
            east_a[g, pl.ds(first, edge), :] = seam(own, from_east, edge, True)

    wide = height + 2 * edge

    def tall_of(middle, k):
        north = jnp.where(has_north, got_dif_edge[1, k, pl.ds(0, edge), :], 0.0)
        south = jnp.where(has_south, got_dif_edge[0, k, pl.ds(0, edge), :], 0.0)
        return jnp.concatenate([north, middle, south], axis=0)

    own_d = tall_of(dif_ref[...], 1)
    west_d = tall_of(got_dif[1], 2)
    east_d = tall_of(got_dif[0], 0)
    lane_w = lax.broadcasted_iota(jnp.int32, (wide, LANES), 1)
    row_w = lax.broadcasted_iota(jnp.int32, (wide, LANES), 0)
    inside = ((row_w >= edge) | has_north) & ((row_w < height + edge) | has_south)

    def five(center, left, right):
        zero_row = jnp.zeros((1, LANES), jnp.float32)
        up = jnp.concatenate([zero_row, center[:-1]], axis=0)
        down = jnp.concatenate([center[1:], zero_row], axis=0)
        ks = [jnp.where(inside, 0.5 * (center + v), 0.0) for v in (up, down, left, right)]
        return [1.0 - (ks[0] + ks[1] + ks[2] + ks[3])] + ks

    left = jnp.where(lane_w == 0, pltpu.roll(west_d, 1, 1), pltpu.roll(own_d, 1, 1))
    right = jnp.where(lane_w == LANES - 1, pltpu.roll(east_d, LANES - 1, 1), pltpu.roll(own_d, LANES - 1, 1))
    main = five(own_d, left, right)
    for k in range(5):
        coef_0[k, pl.ds(base - edge, wide), :] = main[k]

    def turn(j, carry):
        for k in range(5):
            coef_m[j, k, pl.ds(base - edge, wide), :] = pltpu.roll(
                coef_0[k, pl.ds(base - edge, wide), :], 8 * j + 4, 1
            )
        return carry

    lax.fori_loop(0, 16, turn, 0, unroll=2)
    for which, (first_d, second_d) in enumerate(((west_d, own_d), (own_d, east_d))):
        strip = jnp.where(
            lane_w < 4,
            pltpu.roll(first_d, 4, 1),
            jnp.where(lane_w < 8, pltpu.roll(second_d, 4, 1), 0.0),
        )
        for shift in (8, 16, 32, 64):
            strip = strip + pltpu.roll(strip, shift, 1)
        ks = five(strip, pltpu.roll(strip, 1, 1), pltpu.roll(strip, LANES - 1, 1))
        for k in range(5):
            coef_s[which, k, pl.ds(base - edge, wide), :] = ks[k]

    def weighted_sum(c, center, north, south, left, right):
        return center * c[0] + north * c[1] + south * c[2] + left * c[3] + right * c[4]

    tile_rows = [8 * k for k in range(1, (base + height + edge + 7) // 8)]

    def stencil_rows(field, west, east, j, tiles, finish):
        for r in tiles:
            here = pl.ds(r, 8)
            c = [coef_m[j, k, here, :] for k in range(5)]
            for g in range(4):
                s = 16 * g + j
                center = field[s, here, :]
                lft = jnp.where(lane8 == 8 * j + 3, west[g, here, :], center)
                rgt = jnp.where(lane8 == 8 * j + 4, east[g, here, :], center)
                finish(
                    s, r,
                    weighted_sum(
                        c, center, field[s, pl.ds(r - 1, 8), :],
                        field[s, pl.ds(r + 1, 8), :],
                        pltpu.roll(lft, 1, 1), pltpu.roll(rgt, LANES - 1, 1),
                    ),
                )

    def one_pass(field, west, east, field_to, west_to, east_to):
        def keep(s, r, value):
            field_to[s, pl.ds(r, 8), :] = value

        def each(j, carry):
            stencil_rows(field, west, east, j, tile_rows, keep)
            return carry

        lax.fori_loop(0, 16, each, 0, unroll=2)
        for which, (strip, strip_to) in enumerate(((west, west_to), (east, east_to))):
            for r in tile_rows:
                here = pl.ds(r, 8)
                c = [coef_s[which, k, here, :] for k in range(5)]
                for g in range(4):
                    center = strip[g, here, :]
                    strip_to[g, here, :] = weighted_sum(
                        c, center, strip[g, pl.ds(r - 1, 8), :], strip[g, pl.ds(r + 1, 8), :],
                        pltpu.roll(center, 1, 1), pltpu.roll(center, LANES - 1, 1),
                    )

    states = ((field_a, west_a, east_a), (field_b, west_b, east_b))
    for number in range(PASSES - 1):
        one_pass(*states[number % 2], *states[1 - number % 2])
    last_rows = [8 * k for k in range(1, (base + height + 7) // 8)]
    skip = base - 8
    sub8 = lax.broadcasted_iota(jnp.int32, (8, LANES), 0)

    def scale_of(r):
        row = (x * height + sub8 + (r - base)).astype(jnp.float32)
        latitude = (row + 0.5) * math.pi / (height * nx) - math.pi / 2
        return jnp.sqrt(jnp.maximum(jnp.cos(latitude), 0.0))

    scales = {r: scale_of(r) for r in last_rows}

    def last_pass(j, carry):
        def out(s, r, value):
            value = pltpu.roll(value * scales[r], LANES - 4 - 8 * j, 1)
            grid[pl.ds((r - 8) * 72 + s, 8, stride=72), :] = value

        stencil_rows(*states[(PASSES - 1) % 2], j, last_rows, out)
        return carry

    lax.fori_loop(0, 16, last_pass, 0, unroll=2)
    for i in range(height):
        y_ref[i] = grid[pl.ds((i + skip) * 72, 64), :].astype(jnp.bfloat16)
    for i in range(height, y_ref.shape[0]):
        y_ref[i] = jnp.zeros((64, LANES), jnp.bfloat16)

    def give(block):
        at = stage_count[0]
        stage_count[0] += 1
        copy = pltpu.make_async_remote_copy(
            src_ref=block, dst_ref=block,
            send_sem=send.at[at, 0], recv_sem=recv.at[at, 0],
            device_id=partner, device_id_type=MESH,
        )
        copy.start()
        pending.append(copy)
        copy.wait_recv()

    stage = stage_count[0]
    stage_count[0] += 1
    swap = pltpu.make_async_remote_copy(
        src_ref=y_ref.at[pl.ds(half * (1 - c), half)], dst_ref=pair.at[c],
        send_sem=send.at[stage, 0], recv_sem=recv.at[stage, 0],
        device_id=partner, device_id_type=MESH,
    )
    swap.start()
    pending.append(swap)
    pair[c] = y_ref[pl.ds(half * c, half)]
    swap.wait_recv()

    def rows_of(r):
        return jnp.concatenate([pair[0, r], pair[1, r]], axis=0)

    total = jnp.zeros((LANES, LANES), jnp.float32)
    for r in range(0, half, 2):
        wide = jnp.concatenate([rows_of(r), rows_of(r + 1)], axis=1)
        total = total + dot(wide, wide, ((1,), (1,)))
    piece = LANES // nxc
    gram_part[...] = total.reshape(nxc, piece, LANES)
    copies = exchange(nxc, p, dev_xc, lambda q: gram_part.at[q], gram_rs.at[p])
    gram_rs[p] = gram_part[p]
    arrive(copies)
    gram_z[z] = jnp.sum(gram_rs[...], axis=0)
    copies = exchange(nz, z, dev_z, lambda q: gram_z.at[z], gram_z.at[z])
    arrive(copies)
    gram_ag[p] = jnp.sum(gram_z[...], axis=0)
    copies = exchange(nxc, p, dev_xc, lambda q: gram_ag.at[p], gram_ag.at[p])
    arrive(copies)
    gram = gram_ag[...].reshape(LANES, LANES)

    own_gram = jnp.where(c == 0, gram[:64], pltpu.roll(gram[64:], 64, 1))
    zeros64 = jnp.zeros((64, LANES), jnp.float32)
    top_own[c] = rounded(top_rows([(jnp.concatenate([own_gram, zeros64], axis=0), 0)])[0])
    give(top_own.at[c])
    joined = jnp.concatenate([top_own[0], pltpu.roll(top_own[1], 64, 1), zeros64], axis=0)
    merged = matmul_t(matmul(joined, gram), joined)
    basis = matmul(rounded(top_rows([(merged, 0)])[0]), joined).astype(jnp.bfloat16)

    for r in range(0, half, 2):
        wide = jnp.concatenate([rows_of(r), rows_of(r + 1)], axis=1)
        modes = dot(basis, wide, ((1,), (0,))).astype(jnp.bfloat16)
        a_own[r] = modes[:, :LANES]
        a_own[r + 1] = modes[:, LANES:]
    copies = exchange(ny, y, dev_y, lambda q: a_own.at[pl.ds(per * q, per)], a_all.at[y])
    a_all[y] = a_own[pl.ds(per * y, per)]
    arrive(copies)

    stacked = jnp.concatenate(
        [
            jnp.concatenate([a_all[b, r] for b in range(ny)], axis=0)
            for r in range(per)
        ],
        axis=1,
    )
    big = ny * RANK
    full = dot(stacked, stacked, ((1,), (1,)))
    width = full.shape[1]
    near = ny // 2
    if width % LANES:
        full = jnp.concatenate(
            [full, jnp.zeros((big, LANES - width % LANES), jnp.float32)], axis=1
        )
    tiles = full.shape[1] // LANES
    lane = lax.broadcasted_iota(jnp.int32, (RANK, LANES), 1)

    def lane_window(block, shift):
        if width < LANES:
            rolled = block if shift == 0 else jnp.where(
                lane < width - shift, pltpu.roll(block, LANES - shift, 1),
                pltpu.roll(block, (width - shift) % LANES, 1),
            )
            return rolled
        first, inner = shift // LANES, shift % LANES
        a = block[:, LANES * first : LANES * first + LANES]
        if inner == 0:
            return a
        nxt = (first + 1) % tiles
        bb = block[:, LANES * nxt : LANES * nxt + LANES]
        return jnp.where(
            lane < LANES - inner, pltpu.roll(a, LANES - inner, 1), pltpu.roll(bb, LANES - inner, 1)
        )

    pieces = []
    for b in range(ny):
        window = lane_window(full[RANK * b : RANK * b + RANK], RANK * b)
        pieces.append(jnp.where(lane < RANK * near, window, 0.0))
    extra = jnp.zeros((RANK, LANES), jnp.float32)
    for q in range(near):
        col = RANK * (q + near)
        tile, inner = col // LANES, col % LANES
        block = full[RANK * q : RANK * q + RANK, LANES * tile : LANES * tile + LANES]
        shift = (RANK * q - inner) % LANES
        if shift:
            block = pltpu.roll(block, shift, 1)
        extra = jnp.where((lane >= RANK * q) & (lane < RANK * q + RANK), block, extra)
    pieces.append(extra)
    tall = g2_part.shape[0] * g2_part.shape[1] - RANK * (ny + 1)
    if tall:
        pieces.append(jnp.zeros((tall, LANES), jnp.float32))
    g2_part[...] = jnp.concatenate(pieces, axis=0).reshape(g2_part.shape)
    copies = exchange(nxc, p, dev_xc, lambda q: g2_part.at[q], g2_rs.at[p])
    g2_rs[p] = g2_part[p]
    arrive(copies)
    deep = g2_part.shape[1]
    cut = -(-deep // 16) * 8
    low, high = pl.ds(0, cut), pl.ds(cut, deep - cut)
    share = jnp.sum(g2_rs[...], axis=0)
    g2_y[y, low, :] = share[:cut]
    if deep > cut:
        g2_z[z, high, :] = share[cut:]
    for order in range(2):
        along_y, along_z = (low, high) if order == 0 else (high, low)
        rows_y, rows_z = (cut, deep - cut) if order == 0 else (deep - cut, cut)
        copies_y, copies_z = {}, {}
        if rows_y:
            copies_y = exchange(
                ny, y, dev_y, lambda q: g2_y.at[y, along_y], g2_y.at[y, along_y]
            )
        if rows_z:
            copies_z = exchange(
                nz, z, dev_z, lambda q: g2_z.at[z, along_z], g2_z.at[z, along_z]
            )
        arrive(copies_y)
        arrive(copies_z)
        if order == 0:
            g2_z[z, low, :] = jnp.sum(g2_y[:, low, :], axis=0)
            if deep > cut:
                g2_y[y, high, :] = jnp.sum(g2_z[:, high, :], axis=0)
    g2_ag[p, low, :] = jnp.sum(g2_z[:, low, :], axis=0)
    if deep > cut:
        g2_ag[p, high, :] = jnp.sum(g2_y[:, high, :], axis=0)
    copies = exchange(nxc, p, dev_xc, lambda q: g2_ag.at[p], g2_ag.at[p])
    arrive(copies)
    flat = g2_ag[...].reshape(g2_ag.shape[0] * g2_ag.shape[1], LANES)

    zero = jnp.zeros((RANK, LANES), jnp.float32)
    upper = [[None] * tiles for _ in range(ny)]
    extra = flat[RANK * ny : RANK * ny + RANK]
    for b in range(ny):
        block = flat[RANK * b : RANK * b + RANK]
        block = jnp.where(lane < RANK, 0.5 * block, block)
        for tile in range(tiles):
            got = zero
            for off in range(near):
                col = (RANK * (b + off)) % width
                if col // LANES != tile:
                    continue
                inner = col % LANES
                shift = (inner - RANK * off) % LANES
                moved = pltpu.roll(block, shift, 1) if shift else block
                got = jnp.where((lane >= inner) & (lane < inner + RANK), moved, got)
            if b < near:
                col = RANK * (b + near)
                if col // LANES == tile:
                    inner = col % LANES
                    shift = (inner - RANK * b) % LANES
                    moved = pltpu.roll(extra, shift, 1) if shift else extra
                    got = jnp.where((lane >= inner) & (lane < inner + RANK), moved, got)
            upper[b][tile] = got
    per_tile = LANES // RANK

    def tile_value(i, j):
        rows = [upper[b][j] for b in range(per_tile * i, min(per_tile * i + per_tile, ny))]
        rows += [zero] * (per_tile - len(rows))
        return jnp.concatenate(rows, axis=0)

    up = [[tile_value(i, j) for j in range(tiles)] for i in range(tiles)]
    sym = [[up[i][j] + up[j][i].T for j in range(tiles)] for i in range(tiles)]

    if tiles == 2:
        half_own[c] = rounded(merge_pairs([jnp.where(c == 0, sym[0][0], sym[1][1])])[0])
        give(half_own.at[c])
        halves = [half_own[0], half_own[1]]

        def spread(a, b):
            return jnp.concatenate([a, b, zeros64], axis=0)

        pad = jnp.zeros((RANK, LANES), jnp.float32)
        first = spread(halves[0], pad)
        second = spread(pad, halves[1])
        upper_part = matmul_t(matmul(first, sym[0][1]), second)
        last = (
            matmul_t(matmul(first, sym[0][0]), first)
            + matmul_t(matmul(second, sym[1][1]), second)
            + upper_part
            + upper_part.T
        )
        sources = [first, second]
    elif ny == 4:
        tops = top_rows([(sym[0][0], 0), (sym[0][0], 1)])
        joined = jnp.concatenate(
            [rounded(tops[0]), rounded(tops[1]), jnp.zeros((64, LANES), jnp.float32)], axis=0
        )
        last = matmul_t(matmul(joined, sym[0][0]), joined)
        sources = [joined]
    else:
        last = sym[0][0]
        row = lax.broadcasted_iota(jnp.int32, (LANES, LANES), 0)
        col = lax.broadcasted_iota(jnp.int32, (LANES, LANES), 1)
        sources = [jnp.where(row == col, 1.0, 0.0).astype(jnp.float32)]
    top = rounded(top_rows([(last, 0)])[0])
    bent = matmul(top, last)
    place = jnp.concatenate(
        [jnp.zeros((64, LANES), jnp.float32), top, jnp.zeros((32, LANES), jnp.float32)], axis=0
    )
    final = factor_rows(top + matmul_t(bent, place), 64)
    final = jnp.where(half_mask(RANK, 0), final, 0.0)
    weights = jnp.concatenate([matmul(final, s) for s in sources], axis=1)[:, :big]
    weights = weights.astype(jnp.bfloat16)

    mine = half * c + per * y
    for r in range(per):
        tall_rows = jnp.concatenate([a_all[b, r] for b in range(ny)], axis=0)
        f_all[mine + r] = dot(weights, tall_rows, ((1,), (0,))).astype(jnp.bfloat16)
    here = f_all.at[pl.ds(mine, per)]
    copies = exchange(ny, y, dev_y, lambda q: here, here)
    stage = stage_count[0]
    stage_count[0] += 1

    def hand_over(d):
        owner = lax.rem(y + ny - d, ny)
        block = f_all.at[pl.ds(half * c + per * owner, per)]
        copy = pltpu.make_async_remote_copy(
            src_ref=block, dst_ref=block,
            send_sem=send.at[stage, d], recv_sem=recv.at[stage, d],
            device_id=partner, device_id_type=MESH,
        )
        copy.start()
        pending.append(copy)
        return copy

    handed = [hand_over(0)]
    for d in sorted(copies, key=lambda d: min(d, ny - d)):
        copies[d].wait_recv()
        handed.append(hand_over(d))
    for copy in handed:
        copy.wait_recv()

    coef = jnp.zeros((RANK, 64), jnp.float32)
    for r in range(0, 2 * half, 2):
        a = jnp.concatenate([f_all[r], f_all[r + 1]], axis=1)
        b = jnp.concatenate([y_ref[r], y_ref[r + 1]], axis=1)
        coef = coef + dot(a, b, ((1,), (1,)))
    coef_x[x] = jnp.concatenate([coef[:16], coef[16:]], axis=1).astype(jnp.bfloat16)
    copies = exchange(nx, x, dev_x, lambda q: coef_x.at[x], coef_x.at[x])
    arrive(copies)
    coef_z[z] = jnp.sum(coef_x[...].astype(jnp.float32), axis=0).astype(jnp.bfloat16)
    copies = exchange(nz, z, dev_z, lambda q: coef_z.at[z], coef_z.at[z])
    arrive(copies)
    packed = jnp.sum(coef_z[...].astype(jnp.float32), axis=0)
    solved = jnp.concatenate([packed[:, :64], packed[:, 64:]], axis=0).astype(jnp.bfloat16)

    solved_t = solved.T
    for r in range(height):
        out_ref[r] = dot(solved_t, f_all[r], ((1,), (0,))).astype(jnp.bfloat16)
    for copy in pending:
        copy.wait_send()


def merge_call(residuals, diffusivity, ny, nx, nz):
    height = residuals.shape[0]
    nxc = 2 * nx
    unit = 2 * ny
    padded = -(-height // unit) * unit
    while (padded // 2) % 2:
        padded += unit
    half = padded // 2
    per = half // ny
    tall = RANK * (ny + 1)
    piece2 = -(-tall // (8 * nxc)) * 8
    f32, bf16 = jnp.float32, jnp.bfloat16
    vm = pltpu.VMEM
    reach = -(-(ROW_BASE + height + PASSES) // 8) * 8
    last = -(-(ROW_BASE + height) // 8) * 8
    tall_h = -(-height // 16) * 16
    sems = max(8, nxc, ny, nz)
    return pl.pallas_call(
        functools.partial(merge_kernel, ny, nx, nz),
        out_shape=jax.ShapeDtypeStruct(residuals.shape, bf16),
        in_specs=[pl.BlockSpec(memory_space=pl.ANY), pl.BlockSpec(memory_space=pltpu.VMEM)],
        out_specs=pl.BlockSpec(memory_space=pltpu.VMEM),
        scratch_shapes=[
            vm(residuals.shape, bf16),
            vm((64, reach + 8, LANES), f32),
            vm((64, reach + 8, LANES), f32),
            vm((4, reach + 8, LANES), f32),
            vm((4, reach + 8, LANES), f32),
            vm((4, reach + 8, LANES), f32),
            vm((4, reach + 8, LANES), f32),
            vm((5, reach + 8, LANES), f32),
            vm((16, 5, reach + 8, LANES), f32),
            vm((2, 5, reach + 8, LANES), f32),
            vm((max(last - 8, -(-height // 8) * 8) * 72, LANES), f32),
            vm((padded, 64, LANES), bf16),
            vm((4, tall_h, LANES), bf16),
            vm((2, 4, 8, LANES), bf16),
            vm((2, PASSES, 64, LANES), bf16),
            vm((2, 8, LANES), f32),
            vm((2, PASSES, 64, LANES), bf16),
            vm((2, 4, tall_h, LANES), bf16),
            vm((2, 3, 4, 8, LANES), bf16),
            vm((2, height, LANES), f32),
            vm((2, 3, 8, LANES), f32),
            vm((2, half, 64, LANES), bf16),
            vm((nxc, LANES // nxc, LANES), f32),
            vm((nxc, LANES // nxc, LANES), f32),
            vm((nz, LANES // nxc, LANES), f32),
            vm((nxc, LANES // nxc, LANES), f32),
            vm((half, RANK, LANES), bf16),
            vm((ny, per, RANK, LANES), bf16),
            vm((nxc, piece2, LANES), f32),
            vm((nxc, piece2, LANES), f32),
            vm((ny, piece2, LANES), f32),
            vm((nz, piece2, LANES), f32),
            vm((nxc, piece2, LANES), f32),
            vm((padded, RANK, LANES), bf16),
            vm((nx, 16, LANES), bf16),
            vm((nz, 16, LANES), bf16),
            vm((2, RANK, LANES), f32),
            vm((2, RANK, LANES), f32),
            pltpu.SemaphoreType.DMA((20, sems)),
            pltpu.SemaphoreType.DMA((20, sems)),
            pltpu.SemaphoreType.DMA,
        ],
        compiler_params=pltpu.CompilerParams(collective_id=0, has_side_effects=True),
        name="merge",
    )(residuals, diffusivity)


def shards(residuals, diffusivity):
    projected = merge_call(
        residuals.transpose(1, 0, 2), diffusivity,
        lax.axis_size("tm") // 2, lax.axis_size("lat"), lax.axis_size("lon"),
    )
    return projected.transpose(1, 0, 2)


def solution(mesh):
    return jax.shard_map(
        shards,
        mesh=mesh,
        in_specs=(P("tm", "lat", "lon"), P("lat", "lon")),
        out_specs=P("tm", "lat", "lon"),
        check_vma=False,
    )
```

```python
import functools
import math

import jax
import jax.numpy as jnp
from jax import lax
from jax.experimental import pallas as pl
from jax.experimental.pallas import tpu as pltpu
from jax.sharding import PartitionSpec as P

RANK = 32
PASSES = 4
POWER = 3
LANES = 128
ROW_BASE = 11
HIGHEST = lax.Precision.HIGHEST
MESH = pl.DeviceIdType.MESH


def dot(a, b, dims, precision=None):
    return lax.dot_general(
        a, b, (dims, ((), ())), precision=precision, preferred_element_type=jnp.float32
    )


def matmul(a, b):
    return dot(a, b, ((1,), (0,)), HIGHEST)


def matmul_t(a, b):
    return dot(a, b, ((1,), (1,)), HIGHEST)


def rounded(a):
    return a.astype(jnp.bfloat16).astype(jnp.float32)


def factor_rows(m, start, block=8):
    count = RANK // 8
    v = [m[8 * i : 8 * i + 8] for i in range(count)]
    sub = lax.broadcasted_iota(jnp.int32, (8, LANES), 0)
    pivots = [None] * count

    def column(x, j):
        return jnp.broadcast_to(x[:, start + j : start + j + 1], (8, LANES))

    for k in range(0, RANK, block):
        b, s = k // 8, k % 8
        row = [jnp.broadcast_to(v[b][s + j : s + j + 1, :], (8, LANES)) for j in range(block)]
        diag = {(i, j): column(row[i], k + j) for i in range(block) for j in range(i, block)}
        cols = [[column(v[i], k + j) for j in range(block)] for i in range(b, count)]
        inverse = []
        for i in range(block):
            inverse.append(1.0 / diag[i, i])
            ratio = {j: diag[i, j] * inverse[i] for j in range(i + 1, block)}
            for j in range(i + 1, block):
                for n in range(j, block):
                    diag[j, n] = diag[j, n] - ratio[j] * diag[i, n]
                row[j] = row[j] - ratio[j] * row[i]
                for c in cols:
                    c[j] = c[j] - c[i] * ratio[j]
            kept = pivots[(k + i) // 8]
            pivots[(k + i) // 8] = (
                diag[i, i] if kept is None else jnp.where(sub == (k + i) % 8, diag[i, i], kept)
            )
        scaled = [row[i] * inverse[i] for i in range(block)]
        for i in range(b, count):
            total = None
            for j in range(block):
                if i == b and s + j == 7:
                    continue
                c = cols[i - b][j]
                if i == b:
                    c = jnp.where(sub > s + j, c, 0.0)
                term = c * scaled[j]
                total = term if total is None else total + term
            if total is not None:
                v[i] = v[i] - total
    return jnp.concatenate([v[i] * lax.rsqrt(pivots[i]) for i in range(count)], axis=0)


def half_mask(rows, side):
    lane = lax.broadcasted_iota(jnp.int32, (rows, LANES), 1)
    return (lane < 64) if side == 0 else (lane >= 64)


def inner_beside(p, side):
    start = 64 * (1 - side)
    parts = []
    if start:
        parts.append(jnp.zeros((start, LANES), jnp.float32))
    parts.append(p)
    parts.append(jnp.zeros((LANES - start - RANK, LANES), jnp.float32))
    return p + matmul_t(p, jnp.concatenate(parts, axis=0))


def top_rows(problems):
    def orthonormal(bases):
        keeps = [half_mask(RANK, side) for _, side in problems]
        bases = [jnp.where(keep, p, 0.0) for keep, p in zip(keeps, bases)]
        beside = [inner_beside(p, side) for (_, side), p in zip(problems, bases)]
        return tuple(
            jnp.where(keep, factor_rows(m, 64 * (1 - side)), 0.0)
            for keep, m, (_, side) in zip(keeps, beside, problems)
        )

    def body(_, bases):
        return orthonormal([matmul(p, gram) for (gram, _), p in zip(problems, bases)])

    start = orthonormal([gram[64 * side : 64 * side + RANK] for gram, side in problems])
    return lax.fori_loop(0, POWER, body, start)


def merge_pairs(grams):
    problems = [(g, side) for g in grams for side in (0, 1)]
    tops = top_rows(problems)
    zeros = jnp.zeros((64, LANES), jnp.float32)
    joined = [
        jnp.concatenate([rounded(tops[2 * i]), rounded(tops[2 * i + 1]), zeros], axis=0)
        for i in range(len(grams))
    ]
    merged = [matmul_t(matmul(j, g), j) for j, g in zip(joined, grams)]
    second = top_rows([(m, 0) for m in merged])
    return [matmul(rounded(p), j) for p, j in zip(second, joined)]


def order_of(n):
    return sorted(range(1, n), key=lambda d: -min(d, n - d))


def merge_kernel(
    ny, nx, nz, res_hbm, dif_ref, solved_out, f_out,
    res_ref, field_a, field_b, west_a, west_b, east_a, east_b, coef_0, coef_m, coef_s, grid, y_ref, pack, pack_edge, edge_rows, dif_edge,
    got_rows, got_pack, got_edge, got_dif, got_dif_edge,
    pair, y_all, basis_all, own_blocks, gram_part, gram_rs, gram_z, gram_ag,
    a_all, g2_part, g2_rs, g2_y, g2_z, g2_ag,
    f_all, coef_x, coef_z, top_own, half_own,
    send, recv, load_sem,
):
    t, x, z = lax.axis_index("tm"), lax.axis_index("lat"), lax.axis_index("lon")
    y, c = t // 2, lax.rem(t, 2)
    nxc = 2 * nx
    p = x * 2 + c
    half = y_ref.shape[0] // 2
    per = half // ny

    def dev_xc(q):
        return (y * 2 + lax.rem(q, 2), q // 2, z)

    def dev_x(q):
        return (t, q, z)

    def dev_z(q):
        return (t, x, q)

    def dev_y(q):
        return (q * 2 + c, x, z)

    partner = (y * 2 + (1 - c), x, z)
    def dev_around(dx, dz):
        return (t, lax.rem(x + dx + nx, nx), lax.rem(z + dz + nz, nz))

    load = pltpu.make_async_copy(res_hbm, res_ref, load_sem)
    load.start()
    corners = [(dx, dz) for dx in (-1, 1) for dz in (-1, 1)]
    barrier = pltpu.get_barrier_semaphore()
    groups = ((nxc, p, dev_xc), (nz, z, dev_z), (ny, y, dev_y))
    for n, me, dev in groups:
        for d in range(1, n):
            pl.semaphore_signal(
                barrier, inc=1, device_id=dev(lax.rem(me + d, n)), device_id_type=MESH
            )
    for dx, dz in corners:
        pl.semaphore_signal(barrier, inc=1, device_id=dev_around(dx, dz), device_id_type=MESH)

    pending = []
    stage_count = [0]

    def exchange(n, me, dev, source, target):
        stage = stage_count[0]
        stage_count[0] += 1
        copies = {}
        for d in order_of(n):
            q = lax.rem(me + d, n)
            copy = pltpu.make_async_remote_copy(
                src_ref=source(q), dst_ref=target,
                send_sem=send.at[stage, d], recv_sem=recv.at[stage, d],
                device_id=dev(q), device_id_type=MESH,
            )
            copy.start()
            copies[d] = copy
            pending.append(copy)
        return copies

    def arrive(copies):
        for d in sorted(copies, key=lambda d: min(d, len(copies) + 1 - d)):
            copies[d].wait_recv()

    height = res_ref.shape[0]
    base, edge = ROW_BASE, PASSES
    lane8 = lax.broadcasted_iota(jnp.int32, (8, LANES), 1)
    lane_h = lax.broadcasted_iota(jnp.int32, (height, LANES), 1)
    load.wait()
    for r in range(height):
        grid[pl.ds(r * 72, 64), :] = res_ref[r].astype(jnp.float32)

    def take_in(g, carry):
        def one(j, acc):
            s = 16 * g + j
            parts = [
                grid[pl.ds(8 * k * 72 + s, 8, stride=72), :] for k in range((height + 7) // 8)
            ]
            value = pltpu.roll(jnp.concatenate(parts, axis=0)[:height], 8 * j + 4, 1)
            field_a[s, pl.ds(base, height), :] = value
            return jnp.where(lane_h // 8 == j, value, acc)

        acc = lax.fori_loop(0, 16, one, jnp.zeros((height, LANES), jnp.float32), unroll=8)
        west_a[g, pl.ds(base, height), :] = acc
        east_a[g, pl.ds(base, height), :] = acc
        pack[g, pl.ds(0, height), :] = acc.astype(jnp.bfloat16)
        pack_edge[0, g, pl.ds(0, edge), :] = acc[:edge].astype(jnp.bfloat16)
        pack_edge[1, g, pl.ds(0, edge), :] = acc[height - edge :].astype(jnp.bfloat16)
        return carry

    lax.fori_loop(0, 4, take_in, 0)
    for side, first in ((0, 0), (1, height - edge)):
        for e in range(edge):
            edge_rows[side, e] = field_a[:, base + first + e, :].astype(jnp.bfloat16)
    dif_edge[0, pl.ds(0, edge), :] = dif_ref[pl.ds(0, edge), :]
    dif_edge[1, pl.ds(0, edge), :] = dif_ref[pl.ds(height - edge, edge), :]
    pl.semaphore_wait(barrier, sum(n - 1 for n, _, _ in groups) + len(corners))

    stage = stage_count[0]
    stage_count[0] += 3
    halo = []

    def pass_on(source, target, dx, dz):
        at = len(halo)
        copy = pltpu.make_async_remote_copy(
            src_ref=source, dst_ref=target,
            send_sem=send.at[stage + at // 8, at % 8], recv_sem=recv.at[stage + at // 8, at % 8],
            device_id=dev_around(dx, dz), device_id_type=MESH,
        )
        copy.start()
        halo.append(copy)
        pending.append(copy)

    for side, dx in ((0, -1), (1, 1)):
        for dz in (-1, 1):
            pass_on(pack_edge.at[side], got_edge.at[side, dz + 1], dx, dz)
            pass_on(dif_edge.at[side], got_dif_edge.at[side, dz + 1], dx, dz)
        pass_on(pack_edge.at[side], got_edge.at[side, 1], dx, 0)
        pass_on(dif_edge.at[side], got_dif_edge.at[side, 1], dx, 0)
        pass_on(edge_rows.at[side], got_rows.at[side], dx, 0)
    for dz in (-1, 1):
        pass_on(pack, got_pack.at[(dz + 1) // 2], 0, dz)
        pass_on(dif_ref, got_dif.at[(dz + 1) // 2], 0, dz)
    for copy in halo:
        copy.wait_recv()

    has_north, has_south = x > 0, x < nx - 1
    for side, first, there in ((1, base - edge, has_north), (0, base + height, has_south)):
        for e in range(edge):
            row = got_rows[side, e].astype(jnp.float32)
            row = jnp.where(there, row, 0.0)
            field_a[:, first + e, :] = row

    def seam(own, other, rows, own_first):
        t8 = lax.broadcasted_iota(jnp.int32, (rows, LANES), 1) % 8
        return jnp.where((t8 < 4) == own_first, own, other)

    for g in range(4):
        own = west_a[g, pl.ds(base, height), :]
        from_west = got_pack[1, g, pl.ds(0, height), :].astype(jnp.float32)
        from_east = got_pack[0, g, pl.ds(0, height), :].astype(jnp.float32)
        west_a[g, pl.ds(base, height), :] = seam(own, from_west, height, False)
        east_a[g, pl.ds(base, height), :] = seam(own, from_east, height, True)
        for side, first, there in ((1, base - edge, has_north), (0, base + height, has_south)):
            own, from_west, from_east = (
                jnp.where(
                    there, got_edge[side, k, g, pl.ds(0, edge), :].astype(jnp.float32), 0.0
                )
                for k in (1, 2, 0)
            )
            west_a[g, pl.ds(first, edge), :] = seam(own, from_west, edge, False)
            east_a[g, pl.ds(first, edge), :] = seam(own, from_east, edge, True)

    wide = height + 2 * edge

    def tall_of(middle, k):
        north = jnp.where(has_north, got_dif_edge[1, k, pl.ds(0, edge), :], 0.0)
        south = jnp.where(has_south, got_dif_edge[0, k, pl.ds(0, edge), :], 0.0)
        return jnp.concatenate([north, middle, south], axis=0)

    own_d = tall_of(dif_ref[...], 1)
    west_d = tall_of(got_dif[1], 2)
    east_d = tall_of(got_dif[0], 0)
    lane_w = lax.broadcasted_iota(jnp.int32, (wide, LANES), 1)
    row_w = lax.broadcasted_iota(jnp.int32, (wide, LANES), 0)
    inside = ((row_w >= edge) | has_north) & ((row_w < height + edge) | has_south)

    def five(center, left, right):
        zero_row = jnp.zeros((1, LANES), jnp.float32)
        up = jnp.concatenate([zero_row, center[:-1]], axis=0)
        down = jnp.concatenate([center[1:], zero_row], axis=0)
        ks = [jnp.where(inside, 0.5 * (center + v), 0.0) for v in (up, down, left, right)]
        return [1.0 - (ks[0] + ks[1] + ks[2] + ks[3])] + ks

    left = jnp.where(lane_w == 0, pltpu.roll(west_d, 1, 1), pltpu.roll(own_d, 1, 1))
    right = jnp.where(lane_w == LANES - 1, pltpu.roll(east_d, LANES - 1, 1), pltpu.roll(own_d, LANES - 1, 1))
    main = five(own_d, left, right)
    for k in range(5):
        coef_0[k, pl.ds(base - edge, wide), :] = main[k]

    def turn(j, carry):
        for k in range(5):
            coef_m[j, k, pl.ds(base - edge, wide), :] = pltpu.roll(
                coef_0[k, pl.ds(base - edge, wide), :], 8 * j + 4, 1
            )
        return carry

    lax.fori_loop(0, 16, turn, 0, unroll=2)
    for which, (first_d, second_d) in enumerate(((west_d, own_d), (own_d, east_d))):
        strip = jnp.where(
            lane_w < 4,
            pltpu.roll(first_d, 4, 1),
            jnp.where(lane_w < 8, pltpu.roll(second_d, 4, 1), 0.0),
        )
        for shift in (8, 16, 32, 64):
            strip = strip + pltpu.roll(strip, shift, 1)
        ks = five(strip, pltpu.roll(strip, 1, 1), pltpu.roll(strip, LANES - 1, 1))
        for k in range(5):
            coef_s[which, k, pl.ds(base - edge, wide), :] = ks[k]

    def weighted_sum(c, center, north, south, left, right):
        return center * c[0] + north * c[1] + south * c[2] + left * c[3] + right * c[4]

    tile_rows = [8 * k for k in range(1, (base + height + edge + 7) // 8)]

    def stencil_rows(field, west, east, j, tiles, finish):
        for r in tiles:
            here = pl.ds(r, 8)
            c = [coef_m[j, k, here, :] for k in range(5)]
            for g in range(4):
                s = 16 * g + j
                center = field[s, here, :]
                lft = jnp.where(lane8 == 8 * j + 3, west[g, here, :], center)
                rgt = jnp.where(lane8 == 8 * j + 4, east[g, here, :], center)
                finish(
                    s, r,
                    weighted_sum(
                        c, center, field[s, pl.ds(r - 1, 8), :],
                        field[s, pl.ds(r + 1, 8), :],
                        pltpu.roll(lft, 1, 1), pltpu.roll(rgt, LANES - 1, 1),
                    ),
                )

    def one_pass(field, west, east, field_to, west_to, east_to):
        def keep(s, r, value):
            field_to[s, pl.ds(r, 8), :] = value

        def each(j, carry):
            stencil_rows(field, west, east, j, tile_rows, keep)
            return carry

        lax.fori_loop(0, 16, each, 0, unroll=2)
        for which, (strip, strip_to) in enumerate(((west, west_to), (east, east_to))):
            for r in tile_rows:
                here = pl.ds(r, 8)
                c = [coef_s[which, k, here, :] for k in range(5)]
                for g in range(4):
                    center = strip[g, here, :]
                    strip_to[g, here, :] = weighted_sum(
                        c, center, strip[g, pl.ds(r - 1, 8), :], strip[g, pl.ds(r + 1, 8), :],
                        pltpu.roll(center, 1, 1), pltpu.roll(center, LANES - 1, 1),
                    )

    states = ((field_a, west_a, east_a), (field_b, west_b, east_b))
    for number in range(PASSES - 1):
        one_pass(*states[number % 2], *states[1 - number % 2])
    last_rows = [8 * k for k in range(1, (base + height + 7) // 8)]
    skip = base - 8
    sub8 = lax.broadcasted_iota(jnp.int32, (8, LANES), 0)

    def scale_of(r):
        row = (x * height + sub8 + (r - base)).astype(jnp.float32)
        latitude = (row + 0.5) * math.pi / (height * nx) - math.pi / 2
        return jnp.sqrt(jnp.maximum(jnp.cos(latitude), 0.0))

    scales = {r: scale_of(r) for r in last_rows}

    def last_pass(j, carry):
        def out(s, r, value):
            value = pltpu.roll(value * scales[r], LANES - 4 - 8 * j, 1)
            grid[pl.ds((r - 8) * 72 + s, 8, stride=72), :] = value

        stencil_rows(*states[(PASSES - 1) % 2], j, last_rows, out)
        return carry

    lax.fori_loop(0, 16, last_pass, 0, unroll=2)
    for i in range(height):
        y_ref[i] = grid[pl.ds((i + skip) * 72, 64), :].astype(jnp.bfloat16)
    for i in range(height, y_ref.shape[0]):
        y_ref[i] = jnp.zeros((64, LANES), jnp.bfloat16)

    def give(block):
        at = stage_count[0]
        stage_count[0] += 1
        copy = pltpu.make_async_remote_copy(
            src_ref=block, dst_ref=block,
            send_sem=send.at[at, 0], recv_sem=recv.at[at, 0],
            device_id=partner, device_id_type=MESH,
        )
        copy.start()
        pending.append(copy)
        copy.wait_recv()

    stage = stage_count[0]
    stage_count[0] += 1
    swap = pltpu.make_async_remote_copy(
        src_ref=y_ref.at[pl.ds(half * (1 - c), half)], dst_ref=pair.at[:, c],
        send_sem=send.at[stage, 0], recv_sem=recv.at[stage, 0],
        device_id=partner, device_id_type=MESH,
    )
    swap.start()
    pending.append(swap)
    pair[:, c] = y_ref[pl.ds(half * c, half)]
    swap.wait_recv()

    def rows_of(r):
        return jnp.concatenate([pair[r, 0], pair[r, 1]], axis=0)

    spread = exchange(ny, y, dev_y, lambda q: pair.at[pl.ds(per * q, per)], y_all.at[y])
    y_all[y] = pair[pl.ds(per * y, per)]

    total = jnp.zeros((LANES, LANES), jnp.float32)
    for r in range(0, half, 2):
        wide = jnp.concatenate([rows_of(r), rows_of(r + 1)], axis=1)
        total = total + dot(wide, wide, ((1,), (1,)))
    piece = LANES // nxc
    gram_part[...] = total.reshape(nxc, piece, LANES)
    copies = exchange(nxc, p, dev_xc, lambda q: gram_part.at[q], gram_rs.at[p])
    gram_rs[p] = gram_part[p]
    arrive(copies)
    gram_z[z] = jnp.sum(gram_rs[...], axis=0)
    copies = exchange(nz, z, dev_z, lambda q: gram_z.at[z], gram_z.at[z])
    arrive(copies)
    gram_ag[p] = jnp.sum(gram_z[...], axis=0)
    copies = exchange(nxc, p, dev_xc, lambda q: gram_ag.at[p], gram_ag.at[p])
    arrive(copies)
    gram = gram_ag[...].reshape(LANES, LANES)

    own_gram = jnp.where(c == 0, gram[:64], pltpu.roll(gram[64:], 64, 1))
    zeros64 = jnp.zeros((64, LANES), jnp.float32)
    top_own[c] = rounded(top_rows([(jnp.concatenate([own_gram, zeros64], axis=0), 0)])[0])
    give(top_own.at[c])
    joined = jnp.concatenate([top_own[0], pltpu.roll(top_own[1], 64, 1), zeros64], axis=0)
    merged = matmul_t(matmul(joined, gram), joined)
    basis = matmul(rounded(top_rows([(merged, 0)])[0]), joined).astype(jnp.bfloat16)

    basis_all[y] = basis
    copies = exchange(ny, y, dev_y, lambda q: basis_all.at[y], basis_all.at[y])
    used = basis.astype(jnp.float32)
    below = jnp.zeros((LANES - RANK, LANES), jnp.float32)
    block = matmul_t(matmul(used, gram), jnp.concatenate([used, below], axis=0))
    folded = block[:8]
    for i in range(1, RANK // 8):
        folded = folded + pltpu.roll(block[8 * i : 8 * i + 8], RANK * i, 1)
    own_blocks[y] = folded
    block_copies = exchange(ny, y, dev_y, lambda q: own_blocks.at[y], own_blocks.at[y])
    arrive(copies)
    arrive(spread)
    for b in range(ny):
        weights = basis_all[b]
        for r in range(per):
            snaps = jnp.concatenate([y_all[b, r, 0], y_all[b, r, 1]], axis=0)
            a_all[b, r] = dot(weights, snaps, ((1,), (0,))).astype(jnp.bfloat16)

    stacked = jnp.concatenate(
        [
            jnp.concatenate([a_all[b, r] for b in range(ny)], axis=0)
            for r in range(per)
        ],
        axis=1,
    )
    big = ny * RANK
    full = dot(stacked, stacked, ((1,), (1,)))
    width = full.shape[1]
    near = ny // 2
    if width % LANES:
        full = jnp.concatenate(
            [full, jnp.zeros((big, LANES - width % LANES), jnp.float32)], axis=1
        )
    tiles = full.shape[1] // LANES
    lane = lax.broadcasted_iota(jnp.int32, (RANK, LANES), 1)

    def lane_window(block, shift):
        if width < LANES:
            rolled = block if shift == 0 else jnp.where(
                lane < width - shift, pltpu.roll(block, LANES - shift, 1),
                pltpu.roll(block, (width - shift) % LANES, 1),
            )
            return rolled
        first, inner = shift // LANES, shift % LANES
        a = block[:, LANES * first : LANES * first + LANES]
        if inner == 0:
            return a
        nxt = (first + 1) % tiles
        bb = block[:, LANES * nxt : LANES * nxt + LANES]
        return jnp.where(
            lane < LANES - inner, pltpu.roll(a, LANES - inner, 1), pltpu.roll(bb, LANES - inner, 1)
        )

    pieces = []
    for b in range(ny):
        window = lane_window(full[RANK * b : RANK * b + RANK], RANK * (b + 1) % width)
        valid = RANK * (near if b < near else near - 1)
        pieces.append(jnp.where(lane < valid, window, 0.0))
    g2_part[...] = jnp.concatenate(pieces, axis=0).reshape(g2_part.shape)
    copies = exchange(nxc, p, dev_xc, lambda q: g2_part.at[q], g2_rs.at[p])
    g2_rs[p] = g2_part[p]
    arrive(copies)
    deep = g2_part.shape[1]
    cut = -(-deep // 16) * 8
    low, high = pl.ds(0, cut), pl.ds(cut, deep - cut)
    share = jnp.sum(g2_rs[...], axis=0)
    g2_y[y, low, :] = share[:cut]
    if deep > cut:
        g2_z[z, high, :] = share[cut:]
    for order in range(2):
        along_y, along_z = (low, high) if order == 0 else (high, low)
        rows_y, rows_z = (cut, deep - cut) if order == 0 else (deep - cut, cut)
        copies_y, copies_z = {}, {}
        if rows_y:
            copies_y = exchange(
                ny, y, dev_y, lambda q: g2_y.at[y, along_y], g2_y.at[y, along_y]
            )
        if rows_z:
            copies_z = exchange(
                nz, z, dev_z, lambda q: g2_z.at[z, along_z], g2_z.at[z, along_z]
            )
        arrive(copies_y)
        arrive(copies_z)
        if order == 0:
            g2_z[z, low, :] = jnp.sum(g2_y[:, low, :], axis=0)
            if deep > cut:
                g2_y[y, high, :] = jnp.sum(g2_z[:, high, :], axis=0)
    g2_ag[p, low, :] = jnp.sum(g2_z[:, low, :], axis=0)
    if deep > cut:
        g2_ag[p, high, :] = jnp.sum(g2_y[:, high, :], axis=0)
    copies = exchange(nxc, p, dev_xc, lambda q: g2_ag.at[p], g2_ag.at[p])
    arrive(copies)
    flat = g2_ag[...].reshape(g2_ag.shape[0] * g2_ag.shape[1], LANES)

    zero = jnp.zeros((RANK, LANES), jnp.float32)
    upper = [[None] * tiles for _ in range(ny)]
    arrive(block_copies)
    for b in range(ny):
        block = flat[RANK * b : RANK * b + RANK]
        folded = own_blocks[b]
        for tile in range(tiles):
            got = zero
            for off in range(near + 1 if b < near else near):
                col = (RANK * (b + off)) % width
                if col // LANES != tile:
                    continue
                inner = col % LANES
                if off == 0:
                    moved = 0.5 * jnp.concatenate(
                        [
                            pltpu.roll(folded, (inner - RANK * i) % LANES, 1)
                            if (inner - RANK * i) % LANES else folded
                            for i in range(RANK // 8)
                        ],
                        axis=0,
                    )
                else:
                    shift = (inner - RANK * (off - 1)) % LANES
                    moved = pltpu.roll(block, shift, 1) if shift else block
                got = jnp.where((lane >= inner) & (lane < inner + RANK), moved, got)
            upper[b][tile] = got
    per_tile = LANES // RANK

    def tile_value(i, j):
        rows = [upper[b][j] for b in range(per_tile * i, min(per_tile * i + per_tile, ny))]
        rows += [zero] * (per_tile - len(rows))
        return jnp.concatenate(rows, axis=0)

    up = [[tile_value(i, j) for j in range(tiles)] for i in range(tiles)]
    sym = [[up[i][j] + up[j][i].T for j in range(tiles)] for i in range(tiles)]

    if tiles == 2:
        half_own[c] = rounded(merge_pairs([jnp.where(c == 0, sym[0][0], sym[1][1])])[0])
        give(half_own.at[c])
        halves = [half_own[0], half_own[1]]

        def beside(a, b):
            return jnp.concatenate([a, b, zeros64], axis=0)

        pad = jnp.zeros((RANK, LANES), jnp.float32)
        first = beside(halves[0], pad)
        second = beside(pad, halves[1])
        upper_part = matmul_t(matmul(first, sym[0][1]), second)
        last = (
            matmul_t(matmul(first, sym[0][0]), first)
            + matmul_t(matmul(second, sym[1][1]), second)
            + upper_part
            + upper_part.T
        )
        sources = [first, second]
    elif ny == 4:
        tops = top_rows([(sym[0][0], 0), (sym[0][0], 1)])
        joined = jnp.concatenate(
            [rounded(tops[0]), rounded(tops[1]), jnp.zeros((64, LANES), jnp.float32)], axis=0
        )
        last = matmul_t(matmul(joined, sym[0][0]), joined)
        sources = [joined]
    else:
        last = sym[0][0]
        row = lax.broadcasted_iota(jnp.int32, (LANES, LANES), 0)
        col = lax.broadcasted_iota(jnp.int32, (LANES, LANES), 1)
        sources = [jnp.where(row == col, 1.0, 0.0).astype(jnp.float32)]
    top = rounded(top_rows([(last, 0)])[0])
    bent = matmul(top, last)
    place = jnp.concatenate(
        [jnp.zeros((64, LANES), jnp.float32), top, jnp.zeros((32, LANES), jnp.float32)], axis=0
    )
    final = factor_rows(top + matmul_t(bent, place), 64)
    final = jnp.where(half_mask(RANK, 0), final, 0.0)
    weights = jnp.concatenate([matmul(final, s) for s in sources], axis=1)[:, :big]
    weights = weights.astype(jnp.bfloat16)

    mine = half * c + per * y
    for r in range(per):
        tall_rows = jnp.concatenate([a_all[b, r] for b in range(ny)], axis=0)
        f_all[mine + r] = dot(weights, tall_rows, ((1,), (0,))).astype(jnp.bfloat16)
    here = f_all.at[pl.ds(mine, per)]
    copies = exchange(ny, y, dev_y, lambda q: here, here)
    stage = stage_count[0]
    stage_count[0] += 1

    def hand_over(d):
        owner = lax.rem(y + ny - d, ny)
        block = f_all.at[pl.ds(half * c + per * owner, per)]
        copy = pltpu.make_async_remote_copy(
            src_ref=block, dst_ref=block,
            send_sem=send.at[stage, d], recv_sem=recv.at[stage, d],
            device_id=partner, device_id_type=MESH,
        )
        copy.start()
        pending.append(copy)
        return copy

    handed = [hand_over(0)]
    for d in sorted(copies, key=lambda d: min(d, ny - d)):
        copies[d].wait_recv()
        handed.append(hand_over(d))
    for copy in handed:
        copy.wait_recv()

    coef = jnp.zeros((RANK, 64), jnp.float32)
    for r in range(0, 2 * half, 2):
        a = jnp.concatenate([f_all[r], f_all[r + 1]], axis=1)
        b = jnp.concatenate([y_ref[r], y_ref[r + 1]], axis=1)
        coef = coef + dot(a, b, ((1,), (1,)))
    coef_x[x] = jnp.concatenate([coef[:16], coef[16:]], axis=1).astype(jnp.bfloat16)
    copies = exchange(nx, x, dev_x, lambda q: coef_x.at[x], coef_x.at[x])
    arrive(copies)
    coef_z[z] = jnp.sum(coef_x[...].astype(jnp.float32), axis=0).astype(jnp.bfloat16)
    copies = exchange(nz, z, dev_z, lambda q: coef_z.at[z], coef_z.at[z])
    arrive(copies)
    packed = jnp.sum(coef_z[...].astype(jnp.float32), axis=0)
    solved = jnp.concatenate([packed[:, :64], packed[:, 64:]], axis=0).astype(jnp.bfloat16)

    solved_out[...] = solved
    f_out[...] = f_all[...]
    for copy in pending:
        copy.wait_send()


def merge_call(residuals, diffusivity, ny, nx, nz):
    height = residuals.shape[0]
    nxc = 2 * nx
    unit = 2 * ny
    padded = -(-height // unit) * unit
    while (padded // 2) % 2:
        padded += unit
    half = padded // 2
    per = half // ny
    piece2 = RANK * ny // nxc
    f32, bf16 = jnp.float32, jnp.bfloat16
    vm = pltpu.VMEM
    reach = -(-(ROW_BASE + height + PASSES) // 8) * 8
    last = -(-(ROW_BASE + height) // 8) * 8
    tall_h = -(-height // 16) * 16
    sems = max(8, nxc, ny, nz)
    return pl.pallas_call(
        functools.partial(merge_kernel, ny, nx, nz),
        out_shape=(
            jax.ShapeDtypeStruct((RANK, 64), bf16),
            jax.ShapeDtypeStruct((padded, RANK, LANES), bf16),
        ),
        in_specs=[pl.BlockSpec(memory_space=pl.ANY), pl.BlockSpec(memory_space=pltpu.VMEM)],
        out_specs=(pl.BlockSpec(memory_space=pltpu.VMEM),) * 2,
        scratch_shapes=[
            vm(residuals.shape, bf16),
            vm((64, reach + 8, LANES), f32),
            vm((64, reach + 8, LANES), f32),
            vm((4, reach + 8, LANES), f32),
            vm((4, reach + 8, LANES), f32),
            vm((4, reach + 8, LANES), f32),
            vm((4, reach + 8, LANES), f32),
            vm((5, reach + 8, LANES), f32),
            vm((16, 5, reach + 8, LANES), f32),
            vm((2, 5, reach + 8, LANES), f32),
            vm((max(last - 8, -(-height // 8) * 8) * 72, LANES), f32),
            vm((padded, 64, LANES), bf16),
            vm((4, tall_h, LANES), bf16),
            vm((2, 4, 8, LANES), bf16),
            vm((2, PASSES, 64, LANES), bf16),
            vm((2, 8, LANES), f32),
            vm((2, PASSES, 64, LANES), bf16),
            vm((2, 4, tall_h, LANES), bf16),
            vm((2, 3, 4, 8, LANES), bf16),
            vm((2, height, LANES), f32),
            vm((2, 3, 8, LANES), f32),
            vm((half, 2, 64, LANES), bf16),
            vm((ny, per, 2, 64, LANES), bf16),
            vm((ny, RANK, LANES), bf16),
            vm((ny, 8, LANES), f32),
            vm((nxc, LANES // nxc, LANES), f32),
            vm((nxc, LANES // nxc, LANES), f32),
            vm((nz, LANES // nxc, LANES), f32),
            vm((nxc, LANES // nxc, LANES), f32),
            vm((ny, per, RANK, LANES), bf16),
            vm((nxc, piece2, LANES), f32),
            vm((nxc, piece2, LANES), f32),
            vm((ny, piece2, LANES), f32),
            vm((nz, piece2, LANES), f32),
            vm((nxc, piece2, LANES), f32),
            vm((padded, RANK, LANES), bf16),
            vm((nx, 16, LANES), bf16),
            vm((nz, 16, LANES), bf16),
            vm((2, RANK, LANES), f32),
            vm((2, RANK, LANES), f32),
            pltpu.SemaphoreType.DMA((22, sems)),
            pltpu.SemaphoreType.DMA((22, sems)),
            pltpu.SemaphoreType.DMA,
        ],
        compiler_params=pltpu.CompilerParams(collective_id=0, has_side_effects=True),
        name="merge",
    )(residuals, diffusivity)


def project_kernel(solved_ref, modes_ref, out_ref):
    solved = solved_ref[...].T
    for r in range(out_ref.shape[0]):
        out_ref[r] = dot(solved, modes_ref[r], ((1,), (0,))).astype(jnp.bfloat16)


def project_call(solved, modes, height):
    block = max(n for n in range(1, 10) if height % n == 0)
    return pl.pallas_call(
        project_kernel,
        grid=(height // block,),
        out_shape=jax.ShapeDtypeStruct((height, 64, LANES), jnp.bfloat16),
        in_specs=[
            pl.BlockSpec((RANK, 64), lambda i: (0, 0)),
            pl.BlockSpec((block, RANK, LANES), lambda i: (i, 0, 0)),
        ],
        out_specs=pl.BlockSpec((block, 64, LANES), lambda i: (i, 0, 0)),
        name="project",
    )(solved, modes)


def shards(residuals, diffusivity):
    solved, modes = merge_call(
        residuals.transpose(1, 0, 2), diffusivity,
        lax.axis_size("tm") // 2, lax.axis_size("lat"), lax.axis_size("lon"),
    )
    projected = project_call(solved, modes, residuals.shape[1])
    return projected.transpose(1, 0, 2)


def solution(mesh):
    return jax.shard_map(
        shards,
        mesh=mesh,
        in_specs=(P("tm", "lat", "lon"), P("lat", "lon")),
        out_specs=P("tm", "lat", "lon"),
        check_vma=False,
    )
```

```python
import functools
import math

import jax
import jax.numpy as jnp
from jax import lax
from jax.experimental import pallas as pl
from jax.experimental.pallas import tpu as pltpu
from jax.sharding import PartitionSpec as P

RANK = 32
PASSES = 4
POWER = 3
LANES = 128
ROW_BASE = 11
HIGHEST = lax.Precision.HIGHEST
MESH = pl.DeviceIdType.MESH


def dot(a, b, dims, precision=None):
    return lax.dot_general(
        a, b, (dims, ((), ())), precision=precision, preferred_element_type=jnp.float32
    )


def matmul(a, b):
    return dot(a, b, ((1,), (0,)), HIGHEST)


def matmul_t(a, b):
    return dot(a, b, ((1,), (1,)), HIGHEST)


def rounded(a):
    return a.astype(jnp.bfloat16).astype(jnp.float32)


def factor_rows(m, start, block=8):
    count = RANK // 8
    v = [m[8 * i : 8 * i + 8] for i in range(count)]
    sub = lax.broadcasted_iota(jnp.int32, (8, LANES), 0)
    pivots = [None] * count

    def column(x, j):
        return jnp.broadcast_to(x[:, start + j : start + j + 1], (8, LANES))

    for k in range(0, RANK, block):
        b, s = k // 8, k % 8
        row = [jnp.broadcast_to(v[b][s + j : s + j + 1, :], (8, LANES)) for j in range(block)]
        diag = {(i, j): column(row[i], k + j) for i in range(block) for j in range(i, block)}
        cols = [[column(v[i], k + j) for j in range(block)] for i in range(b, count)]
        inverse = []
        for i in range(block):
            inverse.append(1.0 / diag[i, i])
            ratio = {j: diag[i, j] * inverse[i] for j in range(i + 1, block)}
            for j in range(i + 1, block):
                for n in range(j, block):
                    diag[j, n] = diag[j, n] - ratio[j] * diag[i, n]
                row[j] = row[j] - ratio[j] * row[i]
                for c in cols:
                    c[j] = c[j] - c[i] * ratio[j]
            kept = pivots[(k + i) // 8]
            pivots[(k + i) // 8] = (
                diag[i, i] if kept is None else jnp.where(sub == (k + i) % 8, diag[i, i], kept)
            )
        scaled = [row[i] * inverse[i] for i in range(block)]
        for i in range(b, count):
            total = None
            for j in range(block):
                if i == b and s + j == 7:
                    continue
                c = cols[i - b][j]
                if i == b:
                    c = jnp.where(sub > s + j, c, 0.0)
                term = c * scaled[j]
                total = term if total is None else total + term
            if total is not None:
                v[i] = v[i] - total
    return jnp.concatenate([v[i] * lax.rsqrt(pivots[i]) for i in range(count)], axis=0)


def half_mask(rows, side):
    lane = lax.broadcasted_iota(jnp.int32, (rows, LANES), 1)
    return (lane < 64) if side == 0 else (lane >= 64)


def inner_beside(p, side):
    start = 64 * (1 - side)
    parts = []
    if start:
        parts.append(jnp.zeros((start, LANES), jnp.float32))
    parts.append(p)
    parts.append(jnp.zeros((LANES - start - RANK, LANES), jnp.float32))
    return p + matmul_t(p, jnp.concatenate(parts, axis=0))


def top_rows(problems):
    def orthonormal(bases):
        keeps = [half_mask(RANK, side) for _, side in problems]
        bases = [jnp.where(keep, p, 0.0) for keep, p in zip(keeps, bases)]
        beside = [inner_beside(p, side) for (_, side), p in zip(problems, bases)]
        return tuple(
            jnp.where(keep, factor_rows(m, 64 * (1 - side)), 0.0)
            for keep, m, (_, side) in zip(keeps, beside, problems)
        )

    def body(_, bases):
        return orthonormal([matmul(p, gram) for (gram, _), p in zip(problems, bases)])

    start = orthonormal([gram[64 * side : 64 * side + RANK] for gram, side in problems])
    return lax.fori_loop(0, POWER, body, start)


def merge_pairs(grams):
    problems = [(g, side) for g in grams for side in (0, 1)]
    tops = top_rows(problems)
    zeros = jnp.zeros((64, LANES), jnp.float32)
    joined = [
        jnp.concatenate([rounded(tops[2 * i]), rounded(tops[2 * i + 1]), zeros], axis=0)
        for i in range(len(grams))
    ]
    merged = [matmul_t(matmul(j, g), j) for j, g in zip(joined, grams)]
    second = top_rows([(m, 0) for m in merged])
    return [matmul(rounded(p), j) for p, j in zip(second, joined)]


def order_of(n):
    return sorted(range(1, n), key=lambda d: -min(d, n - d))


def merge_kernel(
    ny, nx, nz, res_hbm, dif_ref, solved_out, f_out,
    res_ref, field_a, field_b, west_a, west_b, east_a, east_b, coef_0, coef_m, coef_s, grid, y_ref, pack, pack_edge, edge_rows, dif_edge,
    got_rows, got_pack, got_edge, got_dif, got_dif_edge,
    pair, y_all, basis_all, own_blocks, gram_part, gram_rs, gram_z, gram_ag,
    a_all, g2_part, g2_rs, g2_y, g2_z, g2_ag,
    f_all, coef_x, coef_z, top_own, half_own,
    send, recv, load_sem,
):
    t, x, z = lax.axis_index("tm"), lax.axis_index("lat"), lax.axis_index("lon")
    y, c = t // 2, lax.rem(t, 2)
    nxc = 2 * nx
    p = x * 2 + c
    half = y_ref.shape[0] // 2
    per = half // ny

    def dev_xc(q):
        return (y * 2 + lax.rem(q, 2), q // 2, z)

    def dev_x(q):
        return (t, q, z)

    def dev_z(q):
        return (t, x, q)

    def dev_y(q):
        return (q * 2 + c, x, z)

    partner = (y * 2 + (1 - c), x, z)
    def dev_around(dx, dz):
        return (t, lax.rem(x + dx + nx, nx), lax.rem(z + dz + nz, nz))

    load = pltpu.make_async_copy(res_hbm, res_ref, load_sem)
    load.start()
    corners = [(dx, dz) for dx in (-1, 1) for dz in (-1, 1)]
    barrier = pltpu.get_barrier_semaphore()
    groups = ((nxc, p, dev_xc), (nz, z, dev_z), (ny, y, dev_y))
    for n, me, dev in groups:
        for d in range(1, n):
            pl.semaphore_signal(
                barrier, inc=1, device_id=dev(lax.rem(me + d, n)), device_id_type=MESH
            )
    for dx, dz in corners:
        pl.semaphore_signal(barrier, inc=1, device_id=dev_around(dx, dz), device_id_type=MESH)

    pending = []
    stage_count = [0]

    def exchange(n, me, dev, source, target):
        stage = stage_count[0]
        stage_count[0] += 1
        copies = {}
        for d in order_of(n):
            q = lax.rem(me + d, n)
            copy = pltpu.make_async_remote_copy(
                src_ref=source(q), dst_ref=target,
                send_sem=send.at[stage, d], recv_sem=recv.at[stage, d],
                device_id=dev(q), device_id_type=MESH,
            )
            copy.start()
            copies[d] = copy
            pending.append(copy)
        return copies

    def arrive(copies):
        for d in sorted(copies, key=lambda d: min(d, len(copies) + 1 - d)):
            copies[d].wait_recv()

    height = res_ref.shape[0]
    base, edge = ROW_BASE, PASSES
    lane8 = lax.broadcasted_iota(jnp.int32, (8, LANES), 1)
    lane_h = lax.broadcasted_iota(jnp.int32, (height, LANES), 1)
    load.wait()
    for r in range(height):
        grid[pl.ds(r * 72, 64), :] = res_ref[r].astype(jnp.float32)

    def take_in(g, carry):
        def one(j, acc):
            s = 16 * g + j
            parts = [
                grid[pl.ds(8 * k * 72 + s, 8, stride=72), :] for k in range((height + 7) // 8)
            ]
            value = pltpu.roll(jnp.concatenate(parts, axis=0)[:height], 8 * j + 4, 1)
            field_a[s, pl.ds(base, height), :] = value
            return jnp.where(lane_h // 8 == j, value, acc)

        acc = lax.fori_loop(0, 16, one, jnp.zeros((height, LANES), jnp.float32), unroll=8)
        west_a[g, pl.ds(base, height), :] = acc
        east_a[g, pl.ds(base, height), :] = acc
        pack[g, pl.ds(0, height), :] = acc.astype(jnp.bfloat16)
        pack_edge[0, g, pl.ds(0, edge), :] = acc[:edge].astype(jnp.bfloat16)
        pack_edge[1, g, pl.ds(0, edge), :] = acc[height - edge :].astype(jnp.bfloat16)
        return carry

    lax.fori_loop(0, 4, take_in, 0)
    for side, first in ((0, 0), (1, height - edge)):
        for e in range(edge):
            edge_rows[side, e] = field_a[:, base + first + e, :].astype(jnp.bfloat16)
    dif_edge[0, pl.ds(0, edge), :] = dif_ref[pl.ds(0, edge), :]
    dif_edge[1, pl.ds(0, edge), :] = dif_ref[pl.ds(height - edge, edge), :]
    pl.semaphore_wait(barrier, sum(n - 1 for n, _, _ in groups) + len(corners))

    stage = stage_count[0]
    stage_count[0] += 3
    halo = []

    def pass_on(source, target, dx, dz):
        at = len(halo)
        copy = pltpu.make_async_remote_copy(
            src_ref=source, dst_ref=target,
            send_sem=send.at[stage + at // 8, at % 8], recv_sem=recv.at[stage + at // 8, at % 8],
            device_id=dev_around(dx, dz), device_id_type=MESH,
        )
        copy.start()
        halo.append(copy)
        pending.append(copy)

    for side, dx in ((0, -1), (1, 1)):
        for dz in (-1, 0, 1):
            pass_on(dif_edge.at[side], got_dif_edge.at[side, dz + 1], dx, dz)
    for dz in (-1, 1):
        pass_on(dif_ref, got_dif.at[(dz + 1) // 2], 0, dz)
    early = len(halo)
    for side, dx in ((0, -1), (1, 1)):
        for dz in (-1, 1):
            pass_on(pack_edge.at[side], got_edge.at[side, dz + 1], dx, dz)
        pass_on(edge_rows.at[side], got_rows.at[side], dx, 0)
        pass_on(pack_edge.at[side], got_edge.at[side, 1], dx, 0)
    for dz in (-1, 1):
        pass_on(pack, got_pack.at[(dz + 1) // 2], 0, dz)
    has_north, has_south = x > 0, x < nx - 1
    for copy in halo[:early]:
        copy.wait_recv()

    wide = height + 2 * edge

    def tall_of(middle, k):
        north = jnp.where(has_north, got_dif_edge[1, k, pl.ds(0, edge), :], 0.0)
        south = jnp.where(has_south, got_dif_edge[0, k, pl.ds(0, edge), :], 0.0)
        return jnp.concatenate([north, middle, south], axis=0)

    own_d = tall_of(dif_ref[...], 1)
    west_d = tall_of(got_dif[1], 2)
    east_d = tall_of(got_dif[0], 0)
    lane_w = lax.broadcasted_iota(jnp.int32, (wide, LANES), 1)
    row_w = lax.broadcasted_iota(jnp.int32, (wide, LANES), 0)
    inside = ((row_w >= edge) | has_north) & ((row_w < height + edge) | has_south)

    def five(center, left, right):
        zero_row = jnp.zeros((1, LANES), jnp.float32)
        up = jnp.concatenate([zero_row, center[:-1]], axis=0)
        down = jnp.concatenate([center[1:], zero_row], axis=0)
        ks = [jnp.where(inside, 0.5 * (center + v), 0.0) for v in (up, down, left, right)]
        return [1.0 - (ks[0] + ks[1] + ks[2] + ks[3])] + ks

    left = jnp.where(lane_w == 0, pltpu.roll(west_d, 1, 1), pltpu.roll(own_d, 1, 1))
    right = jnp.where(lane_w == LANES - 1, pltpu.roll(east_d, LANES - 1, 1), pltpu.roll(own_d, LANES - 1, 1))
    main = five(own_d, left, right)
    for k in range(5):
        coef_0[k, pl.ds(base - edge, wide), :] = main[k]

    def turn(j, carry):
        for k in range(5):
            coef_m[j, k, pl.ds(base - edge, wide), :] = pltpu.roll(
                coef_0[k, pl.ds(base - edge, wide), :], 8 * j + 4, 1
            )
        return carry

    lax.fori_loop(0, 16, turn, 0, unroll=2)
    for which, (first_d, second_d) in enumerate(((west_d, own_d), (own_d, east_d))):
        strip = jnp.where(
            lane_w < 4,
            pltpu.roll(first_d, 4, 1),
            jnp.where(lane_w < 8, pltpu.roll(second_d, 4, 1), 0.0),
        )
        for shift in (8, 16, 32, 64):
            strip = strip + pltpu.roll(strip, shift, 1)
        ks = five(strip, pltpu.roll(strip, 1, 1), pltpu.roll(strip, LANES - 1, 1))
        for k in range(5):
            coef_s[which, k, pl.ds(base - edge, wide), :] = ks[k]

    for copy in halo[early:]:
        copy.wait_recv()

    for side, first, there in ((1, base - edge, has_north), (0, base + height, has_south)):
        for e in range(edge):
            row = got_rows[side, e].astype(jnp.float32)
            row = jnp.where(there, row, 0.0)
            field_a[:, first + e, :] = row

    def seam(own, other, rows, own_first):
        t8 = lax.broadcasted_iota(jnp.int32, (rows, LANES), 1) % 8
        return jnp.where((t8 < 4) == own_first, own, other)

    for g in range(4):
        own = west_a[g, pl.ds(base, height), :]
        from_west = got_pack[1, g, pl.ds(0, height), :].astype(jnp.float32)
        from_east = got_pack[0, g, pl.ds(0, height), :].astype(jnp.float32)
        west_a[g, pl.ds(base, height), :] = seam(own, from_west, height, False)
        east_a[g, pl.ds(base, height), :] = seam(own, from_east, height, True)
        for side, first, there in ((1, base - edge, has_north), (0, base + height, has_south)):
            own, from_west, from_east = (
                jnp.where(
                    there, got_edge[side, k, g, pl.ds(0, edge), :].astype(jnp.float32), 0.0
                )
                for k in (1, 2, 0)
            )
            west_a[g, pl.ds(first, edge), :] = seam(own, from_west, edge, False)
            east_a[g, pl.ds(first, edge), :] = seam(own, from_east, edge, True)

    def weighted_sum(c, center, north, south, left, right):
        return center * c[0] + north * c[1] + south * c[2] + left * c[3] + right * c[4]

    tile_rows = [8 * k for k in range(1, (base + height + edge + 7) // 8)]

    def stencil_rows(field, west, east, j, tiles, finish):
        for r in tiles:
            here = pl.ds(r, 8)
            c = [coef_m[j, k, here, :] for k in range(5)]
            for g in range(4):
                s = 16 * g + j
                center = field[s, here, :]
                lft = jnp.where(lane8 == 8 * j + 3, west[g, here, :], center)
                rgt = jnp.where(lane8 == 8 * j + 4, east[g, here, :], center)
                finish(
                    s, r,
                    weighted_sum(
                        c, center, field[s, pl.ds(r - 1, 8), :],
                        field[s, pl.ds(r + 1, 8), :],
                        pltpu.roll(lft, 1, 1), pltpu.roll(rgt, LANES - 1, 1),
                    ),
                )

    def one_pass(field, west, east, field_to, west_to, east_to):
        def keep(s, r, value):
            field_to[s, pl.ds(r, 8), :] = value

        def each(j, carry):
            stencil_rows(field, west, east, j, tile_rows, keep)
            return carry

        lax.fori_loop(0, 16, each, 0, unroll=2)
        for which, (strip, strip_to) in enumerate(((west, west_to), (east, east_to))):
            for r in tile_rows:
                here = pl.ds(r, 8)
                c = [coef_s[which, k, here, :] for k in range(5)]
                for g in range(4):
                    center = strip[g, here, :]
                    strip_to[g, here, :] = weighted_sum(
                        c, center, strip[g, pl.ds(r - 1, 8), :], strip[g, pl.ds(r + 1, 8), :],
                        pltpu.roll(center, 1, 1), pltpu.roll(center, LANES - 1, 1),
                    )

    states = ((field_a, west_a, east_a), (field_b, west_b, east_b))
    for number in range(PASSES - 1):
        one_pass(*states[number % 2], *states[1 - number % 2])
    last_rows = [8 * k for k in range(1, (base + height + 7) // 8)]
    skip = base - 8
    sub8 = lax.broadcasted_iota(jnp.int32, (8, LANES), 0)

    def scale_of(r):
        row = (x * height + sub8 + (r - base)).astype(jnp.float32)
        latitude = (row + 0.5) * math.pi / (height * nx) - math.pi / 2
        return jnp.sqrt(jnp.maximum(jnp.cos(latitude), 0.0))

    scales = {r: scale_of(r) for r in last_rows}

    def last_pass(j, carry):
        def out(s, r, value):
            value = pltpu.roll(value * scales[r], LANES - 4 - 8 * j, 1)
            grid[pl.ds((r - 8) * 72 + s, 8, stride=72), :] = value

        stencil_rows(*states[(PASSES - 1) % 2], j, last_rows, out)
        return carry

    lax.fori_loop(0, 16, last_pass, 0, unroll=2)
    for i in range(height):
        y_ref[i] = grid[pl.ds((i + skip) * 72, 64), :].astype(jnp.bfloat16)
    for i in range(height, y_ref.shape[0]):
        y_ref[i] = jnp.zeros((64, LANES), jnp.bfloat16)

    def give(block):
        at = stage_count[0]
        stage_count[0] += 1
        copy = pltpu.make_async_remote_copy(
            src_ref=block, dst_ref=block,
            send_sem=send.at[at, 0], recv_sem=recv.at[at, 0],
            device_id=partner, device_id_type=MESH,
        )
        copy.start()
        pending.append(copy)
        copy.wait_recv()

    stage = stage_count[0]
    stage_count[0] += 1
    swap = pltpu.make_async_remote_copy(
        src_ref=y_ref.at[pl.ds(half * (1 - c), half)], dst_ref=pair.at[:, c],
        send_sem=send.at[stage, 0], recv_sem=recv.at[stage, 0],
        device_id=partner, device_id_type=MESH,
    )
    swap.start()
    pending.append(swap)
    pair[:, c] = y_ref[pl.ds(half * c, half)]
    swap.wait_recv()

    def rows_of(r):
        return jnp.concatenate([pair[r, 0], pair[r, 1]], axis=0)

    spread = exchange(ny, y, dev_y, lambda q: pair.at[pl.ds(per * q, per)], y_all.at[y])
    y_all[y] = pair[pl.ds(per * y, per)]

    total = jnp.zeros((LANES, LANES), jnp.float32)
    for r in range(0, half, 2):
        wide = jnp.concatenate([rows_of(r), rows_of(r + 1)], axis=1)
        total = total + dot(wide, wide, ((1,), (1,)))
    piece = LANES // nxc
    gram_part[...] = total.reshape(nxc, piece, LANES)
    copies = exchange(nxc, p, dev_xc, lambda q: gram_part.at[q], gram_rs.at[p])
    gram_rs[p] = gram_part[p]
    arrive(copies)
    gram_z[z] = jnp.sum(gram_rs[...], axis=0)
    copies = exchange(nz, z, dev_z, lambda q: gram_z.at[z], gram_z.at[z])
    arrive(copies)
    gram_ag[p] = jnp.sum(gram_z[...], axis=0)
    copies = exchange(nxc, p, dev_xc, lambda q: gram_ag.at[p], gram_ag.at[p])
    arrive(copies)
    gram = gram_ag[...].reshape(LANES, LANES)

    own_gram = jnp.where(c == 0, gram[:64], pltpu.roll(gram[64:], 64, 1))
    zeros64 = jnp.zeros((64, LANES), jnp.float32)
    top_own[c] = rounded(top_rows([(jnp.concatenate([own_gram, zeros64], axis=0), 0)])[0])
    give(top_own.at[c])
    joined = jnp.concatenate([top_own[0], pltpu.roll(top_own[1], 64, 1), zeros64], axis=0)
    merged = matmul_t(matmul(joined, gram), joined)
    basis = matmul(rounded(top_rows([(merged, 0)])[0]), joined).astype(jnp.bfloat16)

    basis_all[y] = basis
    copies = exchange(ny, y, dev_y, lambda q: basis_all.at[y], basis_all.at[y])
    used = basis.astype(jnp.float32)
    below = jnp.zeros((LANES - RANK, LANES), jnp.float32)
    block = matmul_t(matmul(used, gram), jnp.concatenate([used, below], axis=0))
    folded = block[:8]
    for i in range(1, RANK // 8):
        folded = folded + pltpu.roll(block[8 * i : 8 * i + 8], RANK * i, 1)
    own_blocks[y] = folded
    block_copies = exchange(ny, y, dev_y, lambda q: own_blocks.at[y], own_blocks.at[y])
    arrive(copies)
    arrive(spread)
    for b in range(ny):
        weights = basis_all[b]
        for r in range(per):
            snaps = jnp.concatenate([y_all[b, r, 0], y_all[b, r, 1]], axis=0)
            a_all[b, r] = dot(weights, snaps, ((1,), (0,))).astype(jnp.bfloat16)

    stacked = jnp.concatenate(
        [
            jnp.concatenate([a_all[b, r] for b in range(ny)], axis=0)
            for r in range(per)
        ],
        axis=1,
    )
    big = ny * RANK
    full = dot(stacked, stacked, ((1,), (1,)))
    width = full.shape[1]
    near = ny // 2
    if width % LANES:
        full = jnp.concatenate(
            [full, jnp.zeros((big, LANES - width % LANES), jnp.float32)], axis=1
        )
    tiles = full.shape[1] // LANES
    lane = lax.broadcasted_iota(jnp.int32, (RANK, LANES), 1)

    def lane_window(block, shift):
        if width < LANES:
            rolled = block if shift == 0 else jnp.where(
                lane < width - shift, pltpu.roll(block, LANES - shift, 1),
                pltpu.roll(block, (width - shift) % LANES, 1),
            )
            return rolled
        first, inner = shift // LANES, shift % LANES
        a = block[:, LANES * first : LANES * first + LANES]
        if inner == 0:
            return a
        nxt = (first + 1) % tiles
        bb = block[:, LANES * nxt : LANES * nxt + LANES]
        return jnp.where(
            lane < LANES - inner, pltpu.roll(a, LANES - inner, 1), pltpu.roll(bb, LANES - inner, 1)
        )

    pieces = []
    for b in range(ny):
        window = lane_window(full[RANK * b : RANK * b + RANK], RANK * (b + 1) % width)
        valid = RANK * (near if b < near else near - 1)
        pieces.append(jnp.where(lane < valid, window, 0.0))
    g2_part[...] = jnp.concatenate(pieces, axis=0).reshape(g2_part.shape)
    copies = exchange(nxc, p, dev_xc, lambda q: g2_part.at[q], g2_rs.at[p])
    g2_rs[p] = g2_part[p]
    arrive(copies)
    deep = g2_part.shape[1]
    cut = -(-deep // 16) * 8
    low, high = pl.ds(0, cut), pl.ds(cut, deep - cut)
    share = jnp.sum(g2_rs[...], axis=0)
    g2_y[y, low, :] = share[:cut]
    if deep > cut:
        g2_z[z, high, :] = share[cut:]
    for order in range(2):
        along_y, along_z = (low, high) if order == 0 else (high, low)
        rows_y, rows_z = (cut, deep - cut) if order == 0 else (deep - cut, cut)
        copies_y, copies_z = {}, {}
        if rows_y:
            copies_y = exchange(
                ny, y, dev_y, lambda q: g2_y.at[y, along_y], g2_y.at[y, along_y]
            )
        if rows_z:
            copies_z = exchange(
                nz, z, dev_z, lambda q: g2_z.at[z, along_z], g2_z.at[z, along_z]
            )
        arrive(copies_y)
        arrive(copies_z)
        if order == 0:
            g2_z[z, low, :] = jnp.sum(g2_y[:, low, :], axis=0)
            if deep > cut:
                g2_y[y, high, :] = jnp.sum(g2_z[:, high, :], axis=0)
    g2_ag[p, low, :] = jnp.sum(g2_z[:, low, :], axis=0)
    if deep > cut:
        g2_ag[p, high, :] = jnp.sum(g2_y[:, high, :], axis=0)
    copies = exchange(nxc, p, dev_xc, lambda q: g2_ag.at[p], g2_ag.at[p])
    arrive(copies)
    flat = g2_ag[...].reshape(g2_ag.shape[0] * g2_ag.shape[1], LANES)

    zero = jnp.zeros((RANK, LANES), jnp.float32)
    upper = [[None] * tiles for _ in range(ny)]
    arrive(block_copies)
    for b in range(ny):
        block = flat[RANK * b : RANK * b + RANK]
        folded = own_blocks[b]
        for tile in range(tiles):
            got = zero
            for off in range(near + 1 if b < near else near):
                col = (RANK * (b + off)) % width
                if col // LANES != tile:
                    continue
                inner = col % LANES
                if off == 0:
                    moved = 0.5 * jnp.concatenate(
                        [
                            pltpu.roll(folded, (inner - RANK * i) % LANES, 1)
                            if (inner - RANK * i) % LANES else folded
                            for i in range(RANK // 8)
                        ],
                        axis=0,
                    )
                else:
                    shift = (inner - RANK * (off - 1)) % LANES
                    moved = pltpu.roll(block, shift, 1) if shift else block
                got = jnp.where((lane >= inner) & (lane < inner + RANK), moved, got)
            upper[b][tile] = got
    per_tile = LANES // RANK

    def tile_value(i, j):
        rows = [upper[b][j] for b in range(per_tile * i, min(per_tile * i + per_tile, ny))]
        rows += [zero] * (per_tile - len(rows))
        return jnp.concatenate(rows, axis=0)

    up = [[tile_value(i, j) for j in range(tiles)] for i in range(tiles)]
    sym = [[up[i][j] + up[j][i].T for j in range(tiles)] for i in range(tiles)]

    if tiles == 2:
        half_own[c] = rounded(merge_pairs([jnp.where(c == 0, sym[0][0], sym[1][1])])[0])
        give(half_own.at[c])
        halves = [half_own[0], half_own[1]]

        def beside(a, b):
            return jnp.concatenate([a, b, zeros64], axis=0)

        pad = jnp.zeros((RANK, LANES), jnp.float32)
        first = beside(halves[0], pad)
        second = beside(pad, halves[1])
        upper_part = matmul_t(matmul(first, sym[0][1]), second)
        last = (
            matmul_t(matmul(first, sym[0][0]), first)
            + matmul_t(matmul(second, sym[1][1]), second)
            + upper_part
            + upper_part.T
        )
        sources = [first, second]
    elif ny == 4:
        tops = top_rows([(sym[0][0], 0), (sym[0][0], 1)])
        joined = jnp.concatenate(
            [rounded(tops[0]), rounded(tops[1]), jnp.zeros((64, LANES), jnp.float32)], axis=0
        )
        last = matmul_t(matmul(joined, sym[0][0]), joined)
        sources = [joined]
    else:
        last = sym[0][0]
        row = lax.broadcasted_iota(jnp.int32, (LANES, LANES), 0)
        col = lax.broadcasted_iota(jnp.int32, (LANES, LANES), 1)
        sources = [jnp.where(row == col, 1.0, 0.0).astype(jnp.float32)]
    top = rounded(top_rows([(last, 0)])[0])
    bent = matmul(top, last)
    place = jnp.concatenate(
        [jnp.zeros((64, LANES), jnp.float32), top, jnp.zeros((32, LANES), jnp.float32)], axis=0
    )
    final = factor_rows(top + matmul_t(bent, place), 64)
    final = jnp.where(half_mask(RANK, 0), final, 0.0)
    weights = jnp.concatenate([matmul(final, s) for s in sources], axis=1)[:, :big]
    weights = weights.astype(jnp.bfloat16)

    mine = half * c + per * y
    for r in range(per):
        tall_rows = jnp.concatenate([a_all[b, r] for b in range(ny)], axis=0)
        f_all[mine + r] = dot(weights, tall_rows, ((1,), (0,))).astype(jnp.bfloat16)
    here = f_all.at[pl.ds(mine, per)]
    copies = exchange(ny, y, dev_y, lambda q: here, here)
    stage = stage_count[0]
    stage_count[0] += 1

    def hand_over(d):
        owner = lax.rem(y + ny - d, ny)
        block = f_all.at[pl.ds(half * c + per * owner, per)]
        copy = pltpu.make_async_remote_copy(
            src_ref=block, dst_ref=block,
            send_sem=send.at[stage, d], recv_sem=recv.at[stage, d],
            device_id=partner, device_id_type=MESH,
        )
        copy.start()
        pending.append(copy)
        return copy

    handed = [hand_over(0)]
    for d in sorted(copies, key=lambda d: min(d, ny - d)):
        copies[d].wait_recv()
        handed.append(hand_over(d))
    for copy in handed:
        copy.wait_recv()

    coef = jnp.zeros((RANK, 64), jnp.float32)
    for r in range(0, 2 * half, 2):
        a = jnp.concatenate([f_all[r], f_all[r + 1]], axis=1)
        b = jnp.concatenate([y_ref[r], y_ref[r + 1]], axis=1)
        coef = coef + dot(a, b, ((1,), (1,)))
    coef_x[x] = jnp.concatenate([coef[:16], coef[16:]], axis=1).astype(jnp.bfloat16)
    copies = exchange(nx, x, dev_x, lambda q: coef_x.at[x], coef_x.at[x])
    arrive(copies)
    coef_z[z] = jnp.sum(coef_x[...].astype(jnp.float32), axis=0).astype(jnp.bfloat16)
    copies = exchange(nz, z, dev_z, lambda q: coef_z.at[z], coef_z.at[z])
    arrive(copies)
    packed = jnp.sum(coef_z[...].astype(jnp.float32), axis=0)
    solved = jnp.concatenate([packed[:, :64], packed[:, 64:]], axis=0).astype(jnp.bfloat16)

    solved_out[...] = solved
    f_out[...] = f_all[...]
    for copy in pending:
        copy.wait_send()


def merge_call(residuals, diffusivity, ny, nx, nz):
    height = residuals.shape[0]
    nxc = 2 * nx
    unit = 2 * ny
    padded = -(-height // unit) * unit
    while (padded // 2) % 2:
        padded += unit
    half = padded // 2
    per = half // ny
    piece2 = RANK * ny // nxc
    f32, bf16 = jnp.float32, jnp.bfloat16
    vm = pltpu.VMEM
    reach = -(-(ROW_BASE + height + PASSES) // 8) * 8
    last = -(-(ROW_BASE + height) // 8) * 8
    tall_h = -(-height // 16) * 16
    sems = max(8, nxc, ny, nz)
    return pl.pallas_call(
        functools.partial(merge_kernel, ny, nx, nz),
        out_shape=(
            jax.ShapeDtypeStruct((RANK, 64), bf16),
            jax.ShapeDtypeStruct((padded, RANK, LANES), bf16),
        ),
        in_specs=[pl.BlockSpec(memory_space=pl.ANY), pl.BlockSpec(memory_space=pltpu.VMEM)],
        out_specs=(pl.BlockSpec(memory_space=pltpu.VMEM),) * 2,
        scratch_shapes=[
            vm(residuals.shape, bf16),
            vm((64, reach + 8, LANES), f32),
            vm((64, reach + 8, LANES), f32),
            vm((4, reach + 8, LANES), f32),
            vm((4, reach + 8, LANES), f32),
            vm((4, reach + 8, LANES), f32),
            vm((4, reach + 8, LANES), f32),
            vm((5, reach + 8, LANES), f32),
            vm((16, 5, reach + 8, LANES), f32),
            vm((2, 5, reach + 8, LANES), f32),
            vm((max(last - 8, -(-height // 8) * 8) * 72, LANES), f32),
            vm((padded, 64, LANES), bf16),
            vm((4, tall_h, LANES), bf16),
            vm((2, 4, 8, LANES), bf16),
            vm((2, PASSES, 64, LANES), bf16),
            vm((2, 8, LANES), f32),
            vm((2, PASSES, 64, LANES), bf16),
            vm((2, 4, tall_h, LANES), bf16),
            vm((2, 3, 4, 8, LANES), bf16),
            vm((2, height, LANES), f32),
            vm((2, 3, 8, LANES), f32),
            vm((half, 2, 64, LANES), bf16),
            vm((ny, per, 2, 64, LANES), bf16),
            vm((ny, RANK, LANES), bf16),
            vm((ny, 8, LANES), f32),
            vm((nxc, LANES // nxc, LANES), f32),
            vm((nxc, LANES // nxc, LANES), f32),
            vm((nz, LANES // nxc, LANES), f32),
            vm((nxc, LANES // nxc, LANES), f32),
            vm((ny, per, RANK, LANES), bf16),
            vm((nxc, piece2, LANES), f32),
            vm((nxc, piece2, LANES), f32),
            vm((ny, piece2, LANES), f32),
            vm((nz, piece2, LANES), f32),
            vm((nxc, piece2, LANES), f32),
            vm((padded, RANK, LANES), bf16),
            vm((nx, 16, LANES), bf16),
            vm((nz, 16, LANES), bf16),
            vm((2, RANK, LANES), f32),
            vm((2, RANK, LANES), f32),
            pltpu.SemaphoreType.DMA((22, sems)),
            pltpu.SemaphoreType.DMA((22, sems)),
            pltpu.SemaphoreType.DMA,
        ],
        compiler_params=pltpu.CompilerParams(collective_id=0, has_side_effects=True),
        name="merge",
    )(residuals, diffusivity)


def project_kernel(solved_ref, modes_ref, out_ref):
    solved = solved_ref[...].T
    for r in range(out_ref.shape[0]):
        out_ref[r] = dot(solved, modes_ref[r], ((1,), (0,))).astype(jnp.bfloat16)


def project_call(solved, modes, height):
    return pl.pallas_call(
        project_kernel,
        out_shape=jax.ShapeDtypeStruct((height, 64, LANES), jnp.bfloat16),
        in_specs=[pl.BlockSpec(memory_space=pltpu.VMEM)] * 2,
        out_specs=pl.BlockSpec(memory_space=pltpu.VMEM),
        name="project",
    )(solved, modes)


def shards(residuals, diffusivity):
    solved, modes = merge_call(
        residuals.transpose(1, 0, 2), diffusivity,
        lax.axis_size("tm") // 2, lax.axis_size("lat"), lax.axis_size("lon"),
    )
    projected = project_call(solved, modes, residuals.shape[1])
    return projected.transpose(1, 0, 2)


def solution(mesh):
    return jax.shard_map(
        shards,
        mesh=mesh,
        in_specs=(P("tm", "lat", "lon"), P("lat", "lon")),
        out_specs=P("tm", "lat", "lon"),
        check_vma=False,
    )
```

```python
import functools
import math

import jax
import jax.numpy as jnp
from jax import lax
from jax.experimental import pallas as pl
from jax.experimental.pallas import tpu as pltpu
from jax.sharding import PartitionSpec as P

RANK = 32
PASSES = 4
POWER = 3
LANES = 128
ROW_BASE = 11
HIGHEST = lax.Precision.HIGHEST
MESH = pl.DeviceIdType.MESH


def dot(a, b, dims, precision=None):
    return lax.dot_general(
        a, b, (dims, ((), ())), precision=precision, preferred_element_type=jnp.float32
    )


def matmul(a, b):
    return dot(a, b, ((1,), (0,)), HIGHEST)


def matmul_t(a, b):
    return dot(a, b, ((1,), (1,)), HIGHEST)


def rounded(a):
    return a.astype(jnp.bfloat16).astype(jnp.float32)


def factor_rows(m, start, block=8):
    count = RANK // 8
    v = [m[8 * i : 8 * i + 8] for i in range(count)]
    sub = lax.broadcasted_iota(jnp.int32, (8, LANES), 0)
    pivots = [None] * count

    def column(x, j):
        return jnp.broadcast_to(x[:, start + j : start + j + 1], (8, LANES))

    for k in range(0, RANK, block):
        b, s = k // 8, k % 8
        row = [jnp.broadcast_to(v[b][s + j : s + j + 1, :], (8, LANES)) for j in range(block)]
        diag = {(i, j): column(row[i], k + j) for i in range(block) for j in range(i, block)}
        cols = [[column(v[i], k + j) for j in range(block)] for i in range(b, count)]
        inverse = []
        for i in range(block):
            inverse.append(1.0 / diag[i, i])
            ratio = {j: diag[i, j] * inverse[i] for j in range(i + 1, block)}
            for j in range(i + 1, block):
                for n in range(j, block):
                    diag[j, n] = diag[j, n] - ratio[j] * diag[i, n]
                row[j] = row[j] - ratio[j] * row[i]
                for c in cols:
                    c[j] = c[j] - c[i] * ratio[j]
            kept = pivots[(k + i) // 8]
            pivots[(k + i) // 8] = (
                diag[i, i] if kept is None else jnp.where(sub == (k + i) % 8, diag[i, i], kept)
            )
        scaled = [row[i] * inverse[i] for i in range(block)]
        for i in range(b, count):
            total = None
            for j in range(block):
                if i == b and s + j == 7:
                    continue
                c = cols[i - b][j]
                if i == b:
                    c = jnp.where(sub > s + j, c, 0.0)
                term = c * scaled[j]
                total = term if total is None else total + term
            if total is not None:
                v[i] = v[i] - total
    return jnp.concatenate([v[i] * lax.rsqrt(pivots[i]) for i in range(count)], axis=0)


def half_mask(rows, side):
    lane = lax.broadcasted_iota(jnp.int32, (rows, LANES), 1)
    return (lane < 64) if side == 0 else (lane >= 64)


def inner_beside(p, side):
    start = 64 * (1 - side)
    parts = []
    if start:
        parts.append(jnp.zeros((start, LANES), jnp.float32))
    parts.append(p)
    parts.append(jnp.zeros((LANES - start - RANK, LANES), jnp.float32))
    return p + matmul_t(p, jnp.concatenate(parts, axis=0))


def top_rows(problems):
    def orthonormal(bases):
        keeps = [half_mask(RANK, side) for _, side in problems]
        bases = [jnp.where(keep, p, 0.0) for keep, p in zip(keeps, bases)]
        beside = [inner_beside(p, side) for (_, side), p in zip(problems, bases)]
        return tuple(
            jnp.where(keep, factor_rows(m, 64 * (1 - side)), 0.0)
            for keep, m, (_, side) in zip(keeps, beside, problems)
        )

    def body(_, bases):
        return orthonormal([matmul(p, gram) for (gram, _), p in zip(problems, bases)])

    start = orthonormal([gram[64 * side : 64 * side + RANK] for gram, side in problems])
    return lax.fori_loop(0, POWER, body, start)


def order_of(n):
    return sorted(range(1, n), key=lambda d: -min(d, n - d))


def merge_kernel(
    ny, nx, nz, res_hbm, dif_ref, solved_out, f_out,
    res_ref, field_a, field_b, west_a, west_b, east_a, east_b, coef_0, coef_m, coef_s, grid, y_ref, pack, pack_edge, edge_rows, dif_edge,
    got_rows, got_pack, got_edge, got_dif, got_dif_edge,
    pair, y_all, basis_all, own_blocks, gram_part, gram_rs, gram_z, gram_ag,
    a_all, g2_part, g2_rs, g2_y, g2_z, g2_ag,
    f_all, coef_x, coef_z, top_own, half_own, pair_own,
    send, recv, load_sem,
):
    t, x, z = lax.axis_index("tm"), lax.axis_index("lat"), lax.axis_index("lon")
    y, c = t // 2, lax.rem(t, 2)
    nxc = 2 * nx
    p = x * 2 + c
    half = y_ref.shape[0] // 2
    per = half // ny

    def dev_xc(q):
        return (y * 2 + lax.rem(q, 2), q // 2, z)

    def dev_x(q):
        return (t, q, z)

    def dev_z(q):
        return (t, x, q)

    def dev_y(q):
        return (q * 2 + c, x, z)

    partner = (y * 2 + (1 - c), x, z)
    def dev_around(dx, dz):
        return (t, lax.rem(x + dx + nx, nx), lax.rem(z + dz + nz, nz))

    load = pltpu.make_async_copy(res_hbm, res_ref, load_sem)
    load.start()
    corners = [(dx, dz) for dx in (-1, 1) for dz in (-1, 1)]
    barrier = pltpu.get_barrier_semaphore()
    groups = ((nxc, p, dev_xc), (nz, z, dev_z), (ny, y, dev_y))
    for n, me, dev in groups:
        for d in range(1, n):
            pl.semaphore_signal(
                barrier, inc=1, device_id=dev(lax.rem(me + d, n)), device_id_type=MESH
            )
    for dx, dz in corners:
        pl.semaphore_signal(barrier, inc=1, device_id=dev_around(dx, dz), device_id_type=MESH)

    pending = []
    stage_count = [0]

    def exchange(n, me, dev, source, target):
        stage = stage_count[0]
        stage_count[0] += 1
        copies = {}
        for d in order_of(n):
            q = lax.rem(me + d, n)
            copy = pltpu.make_async_remote_copy(
                src_ref=source(q), dst_ref=target,
                send_sem=send.at[stage, d], recv_sem=recv.at[stage, d],
                device_id=dev(q), device_id_type=MESH,
            )
            copy.start()
            copies[d] = copy
            pending.append(copy)
        return copies

    def arrive(copies):
        for d in sorted(copies, key=lambda d: min(d, len(copies) + 1 - d)):
            copies[d].wait_recv()

    height = res_ref.shape[0]
    base, edge = ROW_BASE, PASSES
    lane8 = lax.broadcasted_iota(jnp.int32, (8, LANES), 1)
    lane_h = lax.broadcasted_iota(jnp.int32, (height, LANES), 1)
    load.wait()
    for r in range(height):
        grid[pl.ds(r * 72, 64), :] = res_ref[r].astype(jnp.float32)

    def take_in(g, carry):
        def one(j, acc):
            s = 16 * g + j
            parts = [
                grid[pl.ds(8 * k * 72 + s, 8, stride=72), :] for k in range((height + 7) // 8)
            ]
            value = pltpu.roll(jnp.concatenate(parts, axis=0)[:height], 8 * j + 4, 1)
            field_a[s, pl.ds(base, height), :] = value
            return jnp.where(lane_h // 8 == j, value, acc)

        acc = lax.fori_loop(0, 16, one, jnp.zeros((height, LANES), jnp.float32), unroll=8)
        west_a[g, pl.ds(base, height), :] = acc
        east_a[g, pl.ds(base, height), :] = acc
        pack[g, pl.ds(0, height), :] = acc.astype(jnp.bfloat16)
        pack_edge[0, g, pl.ds(0, edge), :] = acc[:edge].astype(jnp.bfloat16)
        pack_edge[1, g, pl.ds(0, edge), :] = acc[height - edge :].astype(jnp.bfloat16)
        return carry

    lax.fori_loop(0, 4, take_in, 0)
    for side, first in ((0, 0), (1, height - edge)):
        for e in range(edge):
            edge_rows[side, e] = field_a[:, base + first + e, :].astype(jnp.bfloat16)
    dif_edge[0, pl.ds(0, edge), :] = dif_ref[pl.ds(0, edge), :]
    dif_edge[1, pl.ds(0, edge), :] = dif_ref[pl.ds(height - edge, edge), :]
    pl.semaphore_wait(barrier, sum(n - 1 for n, _, _ in groups) + len(corners))

    stage = stage_count[0]
    stage_count[0] += 3
    halo = []

    def pass_on(source, target, dx, dz):
        at = len(halo)
        copy = pltpu.make_async_remote_copy(
            src_ref=source, dst_ref=target,
            send_sem=send.at[stage + at // 8, at % 8], recv_sem=recv.at[stage + at // 8, at % 8],
            device_id=dev_around(dx, dz), device_id_type=MESH,
        )
        copy.start()
        halo.append(copy)
        pending.append(copy)

    for side, dx in ((0, -1), (1, 1)):
        for dz in (-1, 0, 1):
            pass_on(dif_edge.at[side], got_dif_edge.at[side, dz + 1], dx, dz)
    for dz in (-1, 1):
        pass_on(dif_ref, got_dif.at[(dz + 1) // 2], 0, dz)
    early = len(halo)
    for side, dx in ((0, -1), (1, 1)):
        for dz in (-1, 1):
            pass_on(pack_edge.at[side], got_edge.at[side, dz + 1], dx, dz)
        pass_on(edge_rows.at[side], got_rows.at[side], dx, 0)
        pass_on(pack_edge.at[side], got_edge.at[side, 1], dx, 0)
    for dz in (-1, 1):
        pass_on(pack, got_pack.at[(dz + 1) // 2], 0, dz)
    has_north, has_south = x > 0, x < nx - 1
    for copy in halo[:early]:
        copy.wait_recv()

    wide = height + 2 * edge

    def tall_of(middle, k):
        north = jnp.where(has_north, got_dif_edge[1, k, pl.ds(0, edge), :], 0.0)
        south = jnp.where(has_south, got_dif_edge[0, k, pl.ds(0, edge), :], 0.0)
        return jnp.concatenate([north, middle, south], axis=0)

    own_d = tall_of(dif_ref[...], 1)
    west_d = tall_of(got_dif[1], 2)
    east_d = tall_of(got_dif[0], 0)
    lane_w = lax.broadcasted_iota(jnp.int32, (wide, LANES), 1)
    row_w = lax.broadcasted_iota(jnp.int32, (wide, LANES), 0)
    inside = ((row_w >= edge) | has_north) & ((row_w < height + edge) | has_south)

    def five(center, left, right):
        zero_row = jnp.zeros((1, LANES), jnp.float32)
        up = jnp.concatenate([zero_row, center[:-1]], axis=0)
        down = jnp.concatenate([center[1:], zero_row], axis=0)
        ks = [jnp.where(inside, 0.5 * (center + v), 0.0) for v in (up, down, left, right)]
        return [1.0 - (ks[0] + ks[1] + ks[2] + ks[3])] + ks

    left = jnp.where(lane_w == 0, pltpu.roll(west_d, 1, 1), pltpu.roll(own_d, 1, 1))
    right = jnp.where(lane_w == LANES - 1, pltpu.roll(east_d, LANES - 1, 1), pltpu.roll(own_d, LANES - 1, 1))
    main = five(own_d, left, right)
    for k in range(5):
        coef_0[k, pl.ds(base - edge, wide), :] = main[k]

    def turn(j, carry):
        for k in range(5):
            coef_m[j, k, pl.ds(base - edge, wide), :] = pltpu.roll(
                coef_0[k, pl.ds(base - edge, wide), :], 8 * j + 4, 1
            )
        return carry

    lax.fori_loop(0, 16, turn, 0, unroll=2)
    for which, (first_d, second_d) in enumerate(((west_d, own_d), (own_d, east_d))):
        strip = jnp.where(
            lane_w < 4,
            pltpu.roll(first_d, 4, 1),
            jnp.where(lane_w < 8, pltpu.roll(second_d, 4, 1), 0.0),
        )
        for shift in (8, 16, 32, 64):
            strip = strip + pltpu.roll(strip, shift, 1)
        ks = five(strip, pltpu.roll(strip, 1, 1), pltpu.roll(strip, LANES - 1, 1))
        for k in range(5):
            coef_s[which, k, pl.ds(base - edge, wide), :] = ks[k]

    for copy in halo[early:]:
        copy.wait_recv()

    for side, first, there in ((1, base - edge, has_north), (0, base + height, has_south)):
        for e in range(edge):
            row = got_rows[side, e].astype(jnp.float32)
            row = jnp.where(there, row, 0.0)
            field_a[:, first + e, :] = row

    def seam(own, other, rows, own_first):
        t8 = lax.broadcasted_iota(jnp.int32, (rows, LANES), 1) % 8
        return jnp.where((t8 < 4) == own_first, own, other)

    for g in range(4):
        own = west_a[g, pl.ds(base, height), :]
        from_west = got_pack[1, g, pl.ds(0, height), :].astype(jnp.float32)
        from_east = got_pack[0, g, pl.ds(0, height), :].astype(jnp.float32)
        west_a[g, pl.ds(base, height), :] = seam(own, from_west, height, False)
        east_a[g, pl.ds(base, height), :] = seam(own, from_east, height, True)
        for side, first, there in ((1, base - edge, has_north), (0, base + height, has_south)):
            own, from_west, from_east = (
                jnp.where(
                    there, got_edge[side, k, g, pl.ds(0, edge), :].astype(jnp.float32), 0.0
                )
                for k in (1, 2, 0)
            )
            west_a[g, pl.ds(first, edge), :] = seam(own, from_west, edge, False)
            east_a[g, pl.ds(first, edge), :] = seam(own, from_east, edge, True)

    def weighted_sum(c, center, north, south, left, right):
        return center * c[0] + north * c[1] + south * c[2] + left * c[3] + right * c[4]

    tile_rows = [8 * k for k in range(1, (base + height + edge + 7) // 8)]

    def stencil_rows(field, west, east, j, tiles, finish):
        for r in tiles:
            here = pl.ds(r, 8)
            c = [coef_m[j, k, here, :] for k in range(5)]
            for g in range(4):
                s = 16 * g + j
                center = field[s, here, :]
                lft = jnp.where(lane8 == 8 * j + 3, west[g, here, :], center)
                rgt = jnp.where(lane8 == 8 * j + 4, east[g, here, :], center)
                finish(
                    s, r,
                    weighted_sum(
                        c, center, field[s, pl.ds(r - 1, 8), :],
                        field[s, pl.ds(r + 1, 8), :],
                        pltpu.roll(lft, 1, 1), pltpu.roll(rgt, LANES - 1, 1),
                    ),
                )

    def one_pass(field, west, east, field_to, west_to, east_to):
        def keep(s, r, value):
            field_to[s, pl.ds(r, 8), :] = value

        def each(j, carry):
            stencil_rows(field, west, east, j, tile_rows, keep)
            return carry

        lax.fori_loop(0, 16, each, 0, unroll=2)
        for which, (strip, strip_to) in enumerate(((west, west_to), (east, east_to))):
            for r in tile_rows:
                here = pl.ds(r, 8)
                c = [coef_s[which, k, here, :] for k in range(5)]
                for g in range(4):
                    center = strip[g, here, :]
                    strip_to[g, here, :] = weighted_sum(
                        c, center, strip[g, pl.ds(r - 1, 8), :], strip[g, pl.ds(r + 1, 8), :],
                        pltpu.roll(center, 1, 1), pltpu.roll(center, LANES - 1, 1),
                    )

    states = ((field_a, west_a, east_a), (field_b, west_b, east_b))
    for number in range(PASSES - 1):
        one_pass(*states[number % 2], *states[1 - number % 2])
    last_rows = [8 * k for k in range(1, (base + height + 7) // 8)]
    skip = base - 8
    sub8 = lax.broadcasted_iota(jnp.int32, (8, LANES), 0)

    def scale_of(r):
        row = (x * height + sub8 + (r - base)).astype(jnp.float32)
        latitude = (row + 0.5) * math.pi / (height * nx) - math.pi / 2
        return jnp.sqrt(jnp.maximum(jnp.cos(latitude), 0.0))

    scales = {r: scale_of(r) for r in last_rows}

    def last_pass(j, carry):
        def out(s, r, value):
            value = pltpu.roll(value * scales[r], LANES - 4 - 8 * j, 1)
            grid[pl.ds((r - 8) * 72 + s, 8, stride=72), :] = value

        stencil_rows(*states[(PASSES - 1) % 2], j, last_rows, out)
        return carry

    lax.fori_loop(0, 16, last_pass, 0, unroll=2)
    for i in range(height):
        y_ref[i] = grid[pl.ds((i + skip) * 72, 64), :].astype(jnp.bfloat16)
    for i in range(height, y_ref.shape[0]):
        y_ref[i] = jnp.zeros((64, LANES), jnp.bfloat16)

    def give(block, peer):
        at = stage_count[0]
        stage_count[0] += 1
        copy = pltpu.make_async_remote_copy(
            src_ref=block, dst_ref=block,
            send_sem=send.at[at, 0], recv_sem=recv.at[at, 0],
            device_id=peer, device_id_type=MESH,
        )
        copy.start()
        pending.append(copy)
        copy.wait_recv()

    stage = stage_count[0]
    stage_count[0] += 1
    swap = pltpu.make_async_remote_copy(
        src_ref=y_ref.at[pl.ds(half * (1 - c), half)], dst_ref=pair.at[:, c],
        send_sem=send.at[stage, 0], recv_sem=recv.at[stage, 0],
        device_id=partner, device_id_type=MESH,
    )
    swap.start()
    pending.append(swap)
    pair[:, c] = y_ref[pl.ds(half * c, half)]
    swap.wait_recv()

    def rows_of(r):
        return jnp.concatenate([pair[r, 0], pair[r, 1]], axis=0)

    spread = exchange(ny, y, dev_y, lambda q: pair.at[pl.ds(per * q, per)], y_all.at[y])
    y_all[y] = pair[pl.ds(per * y, per)]

    total = jnp.zeros((LANES, LANES), jnp.float32)
    for r in range(0, half, 2):
        wide = jnp.concatenate([rows_of(r), rows_of(r + 1)], axis=1)
        total = total + dot(wide, wide, ((1,), (1,)))
    piece = LANES // nxc
    gram_part[...] = total.reshape(nxc, piece, LANES)
    copies = exchange(nxc, p, dev_xc, lambda q: gram_part.at[q], gram_rs.at[p])
    gram_rs[p] = gram_part[p]
    arrive(copies)
    gram_z[z] = jnp.sum(gram_rs[...], axis=0)
    copies = exchange(nz, z, dev_z, lambda q: gram_z.at[z], gram_z.at[z])
    arrive(copies)
    gram_ag[p] = jnp.sum(gram_z[...], axis=0)
    copies = exchange(nxc, p, dev_xc, lambda q: gram_ag.at[p], gram_ag.at[p])
    arrive(copies)
    gram = gram_ag[...].reshape(LANES, LANES)

    zeros64 = jnp.zeros((64, LANES), jnp.float32)

    def merge_shared(both, side, tops, peer):
        own = jnp.where(side == 0, both[:64], pltpu.roll(both[64:], 64, 1))
        tops[side] = rounded(top_rows([(jnp.concatenate([own, zeros64], axis=0), 0)])[0])
        give(tops.at[side], peer)
        joined = jnp.concatenate([tops[0], pltpu.roll(tops[1], 64, 1), zeros64], axis=0)
        merged = matmul_t(matmul(joined, both), joined)
        return matmul(rounded(top_rows([(merged, 0)])[0]), joined)

    basis = merge_shared(gram, c, top_own, partner).astype(jnp.bfloat16)

    basis_all[y] = basis
    copies = exchange(ny, y, dev_y, lambda q: basis_all.at[y], basis_all.at[y])
    used = basis.astype(jnp.float32)
    below = jnp.zeros((LANES - RANK, LANES), jnp.float32)
    block = matmul_t(matmul(used, gram), jnp.concatenate([used, below], axis=0))
    folded = block[:8]
    for i in range(1, RANK // 8):
        folded = folded + pltpu.roll(block[8 * i : 8 * i + 8], RANK * i, 1)
    own_blocks[y] = folded
    block_copies = exchange(ny, y, dev_y, lambda q: own_blocks.at[y], own_blocks.at[y])
    arrive(copies)
    arrive(spread)
    for b in range(ny):
        weights = basis_all[b]
        for r in range(per):
            snaps = jnp.concatenate([y_all[b, r, 0], y_all[b, r, 1]], axis=0)
            a_all[b, r] = dot(weights, snaps, ((1,), (0,))).astype(jnp.bfloat16)

    stacked = jnp.concatenate(
        [
            jnp.concatenate([a_all[b, r] for b in range(ny)], axis=0)
            for r in range(per)
        ],
        axis=1,
    )
    big = ny * RANK
    full = dot(stacked, stacked, ((1,), (1,)))
    width = full.shape[1]
    near = ny // 2
    if width % LANES:
        full = jnp.concatenate(
            [full, jnp.zeros((big, LANES - width % LANES), jnp.float32)], axis=1
        )
    tiles = full.shape[1] // LANES
    lane = lax.broadcasted_iota(jnp.int32, (RANK, LANES), 1)

    def lane_window(block, shift):
        if width < LANES:
            rolled = block if shift == 0 else jnp.where(
                lane < width - shift, pltpu.roll(block, LANES - shift, 1),
                pltpu.roll(block, (width - shift) % LANES, 1),
            )
            return rolled
        first, inner = shift // LANES, shift % LANES
        a = block[:, LANES * first : LANES * first + LANES]
        if inner == 0:
            return a
        nxt = (first + 1) % tiles
        bb = block[:, LANES * nxt : LANES * nxt + LANES]
        return jnp.where(
            lane < LANES - inner, pltpu.roll(a, LANES - inner, 1), pltpu.roll(bb, LANES - inner, 1)
        )

    pieces = []
    for b in range(ny):
        window = lane_window(full[RANK * b : RANK * b + RANK], RANK * (b + 1) % width)
        valid = RANK * (near if b < near else near - 1)
        pieces.append(jnp.where(lane < valid, window, 0.0))
    g2_part[...] = jnp.concatenate(pieces, axis=0).reshape(g2_part.shape)
    copies = exchange(nxc, p, dev_xc, lambda q: g2_part.at[q], g2_rs.at[p])
    g2_rs[p] = g2_part[p]
    arrive(copies)
    deep = g2_part.shape[1]
    cut = -(-deep // 16) * 8
    low, high = pl.ds(0, cut), pl.ds(cut, deep - cut)
    share = jnp.sum(g2_rs[...], axis=0)
    g2_y[y, low, :] = share[:cut]
    if deep > cut:
        g2_z[z, high, :] = share[cut:]
    for order in range(2):
        along_y, along_z = (low, high) if order == 0 else (high, low)
        rows_y, rows_z = (cut, deep - cut) if order == 0 else (deep - cut, cut)
        copies_y, copies_z = {}, {}
        if rows_y:
            copies_y = exchange(
                ny, y, dev_y, lambda q: g2_y.at[y, along_y], g2_y.at[y, along_y]
            )
        if rows_z:
            copies_z = exchange(
                nz, z, dev_z, lambda q: g2_z.at[z, along_z], g2_z.at[z, along_z]
            )
        arrive(copies_y)
        arrive(copies_z)
        if order == 0:
            g2_z[z, low, :] = jnp.sum(g2_y[:, low, :], axis=0)
            if deep > cut:
                g2_y[y, high, :] = jnp.sum(g2_z[:, high, :], axis=0)
    g2_ag[p, low, :] = jnp.sum(g2_z[:, low, :], axis=0)
    if deep > cut:
        g2_ag[p, high, :] = jnp.sum(g2_y[:, high, :], axis=0)
    copies = exchange(nxc, p, dev_xc, lambda q: g2_ag.at[p], g2_ag.at[p])
    arrive(copies)
    flat = g2_ag[...].reshape(g2_ag.shape[0] * g2_ag.shape[1], LANES)

    zero = jnp.zeros((RANK, LANES), jnp.float32)
    upper = [[None] * tiles for _ in range(ny)]
    arrive(block_copies)
    for b in range(ny):
        block = flat[RANK * b : RANK * b + RANK]
        folded = own_blocks[b]
        for tile in range(tiles):
            got = zero
            for off in range(near + 1 if b < near else near):
                col = (RANK * (b + off)) % width
                if col // LANES != tile:
                    continue
                inner = col % LANES
                if off == 0:
                    moved = 0.5 * jnp.concatenate(
                        [
                            pltpu.roll(folded, (inner - RANK * i) % LANES, 1)
                            if (inner - RANK * i) % LANES else folded
                            for i in range(RANK // 8)
                        ],
                        axis=0,
                    )
                else:
                    shift = (inner - RANK * (off - 1)) % LANES
                    moved = pltpu.roll(block, shift, 1) if shift else block
                got = jnp.where((lane >= inner) & (lane < inner + RANK), moved, got)
            upper[b][tile] = got
    per_tile = LANES // RANK

    def tile_value(i, j):
        rows = [upper[b][j] for b in range(per_tile * i, min(per_tile * i + per_tile, ny))]
        rows += [zero] * (per_tile - len(rows))
        return jnp.concatenate(rows, axis=0)

    up = [[tile_value(i, j) for j in range(tiles)] for i in range(tiles)]
    sym = [[up[i][j] + up[j][i].T for j in range(tiles)] for i in range(tiles)]

    if tiles == 2:
        side = lax.rem(x, 2)
        along = (t, x + 1 - 2 * side, z)
        tile = jnp.where(c == 0, sym[0][0], sym[1][1])
        half_own[c] = rounded(merge_shared(tile, side, pair_own, along))
        give(half_own.at[c], partner)
        halves = [half_own[0], half_own[1]]

        def beside(a, b):
            return jnp.concatenate([a, b, zeros64], axis=0)

        pad = jnp.zeros((RANK, LANES), jnp.float32)
        first = beside(halves[0], pad)
        second = beside(pad, halves[1])
        upper_part = matmul_t(matmul(first, sym[0][1]), second)
        last = (
            matmul_t(matmul(first, sym[0][0]), first)
            + matmul_t(matmul(second, sym[1][1]), second)
            + upper_part
            + upper_part.T
        )
        sources = [first, second]
    elif ny == 4:
        tops = top_rows([(sym[0][0], 0), (sym[0][0], 1)])
        joined = jnp.concatenate(
            [rounded(tops[0]), rounded(tops[1]), jnp.zeros((64, LANES), jnp.float32)], axis=0
        )
        last = matmul_t(matmul(joined, sym[0][0]), joined)
        sources = [joined]
    else:
        last = sym[0][0]
        row = lax.broadcasted_iota(jnp.int32, (LANES, LANES), 0)
        col = lax.broadcasted_iota(jnp.int32, (LANES, LANES), 1)
        sources = [jnp.where(row == col, 1.0, 0.0).astype(jnp.float32)]
    top = rounded(top_rows([(last, 0)])[0])
    bent = matmul(top, last)
    place = jnp.concatenate(
        [jnp.zeros((64, LANES), jnp.float32), top, jnp.zeros((32, LANES), jnp.float32)], axis=0
    )
    final = factor_rows(top + matmul_t(bent, place), 64)
    final = jnp.where(half_mask(RANK, 0), final, 0.0)
    weights = jnp.concatenate([matmul(final, s) for s in sources], axis=1)[:, :big]
    weights = weights.astype(jnp.bfloat16)

    mine = half * c + per * y
    for r in range(per):
        tall_rows = jnp.concatenate([a_all[b, r] for b in range(ny)], axis=0)
        f_all[mine + r] = dot(weights, tall_rows, ((1,), (0,))).astype(jnp.bfloat16)
    here = f_all.at[pl.ds(mine, per)]
    copies = exchange(ny, y, dev_y, lambda q: here, here)
    stage = stage_count[0]
    stage_count[0] += 1

    def hand_over(d):
        owner = lax.rem(y + ny - d, ny)
        block = f_all.at[pl.ds(half * c + per * owner, per)]
        copy = pltpu.make_async_remote_copy(
            src_ref=block, dst_ref=block,
            send_sem=send.at[stage, d], recv_sem=recv.at[stage, d],
            device_id=partner, device_id_type=MESH,
        )
        copy.start()
        pending.append(copy)
        return copy

    handed = [hand_over(0)]
    for d in sorted(copies, key=lambda d: min(d, ny - d)):
        copies[d].wait_recv()
        handed.append(hand_over(d))
    for copy in handed:
        copy.wait_recv()

    coef = jnp.zeros((RANK, 64), jnp.float32)
    for r in range(0, 2 * half, 2):
        a = jnp.concatenate([f_all[r], f_all[r + 1]], axis=1)
        b = jnp.concatenate([y_ref[r], y_ref[r + 1]], axis=1)
        coef = coef + dot(a, b, ((1,), (1,)))
    coef_x[x] = jnp.concatenate([coef[:16], coef[16:]], axis=1).astype(jnp.bfloat16)
    copies = exchange(nx, x, dev_x, lambda q: coef_x.at[x], coef_x.at[x])
    arrive(copies)
    coef_z[z] = jnp.sum(coef_x[...].astype(jnp.float32), axis=0).astype(jnp.bfloat16)
    copies = exchange(nz, z, dev_z, lambda q: coef_z.at[z], coef_z.at[z])
    arrive(copies)
    packed = jnp.sum(coef_z[...].astype(jnp.float32), axis=0)
    solved = jnp.concatenate([packed[:, :64], packed[:, 64:]], axis=0).astype(jnp.bfloat16)

    solved_out[...] = solved
    f_out[...] = f_all[...]
    for copy in pending:
        copy.wait_send()


def merge_call(residuals, diffusivity, ny, nx, nz):
    height = residuals.shape[0]
    nxc = 2 * nx
    unit = 2 * ny
    padded = -(-height // unit) * unit
    while (padded // 2) % 2:
        padded += unit
    half = padded // 2
    per = half // ny
    piece2 = RANK * ny // nxc
    f32, bf16 = jnp.float32, jnp.bfloat16
    vm = pltpu.VMEM
    reach = -(-(ROW_BASE + height + PASSES) // 8) * 8
    last = -(-(ROW_BASE + height) // 8) * 8
    tall_h = -(-height // 16) * 16
    sems = max(8, nxc, ny, nz)
    return pl.pallas_call(
        functools.partial(merge_kernel, ny, nx, nz),
        out_shape=(
            jax.ShapeDtypeStruct((RANK, 64), bf16),
            jax.ShapeDtypeStruct((padded, RANK, LANES), bf16),
        ),
        in_specs=[pl.BlockSpec(memory_space=pl.ANY), pl.BlockSpec(memory_space=pltpu.VMEM)],
        out_specs=(pl.BlockSpec(memory_space=pltpu.VMEM),) * 2,
        scratch_shapes=[
            vm(residuals.shape, bf16),
            vm((64, reach + 8, LANES), f32),
            vm((64, reach + 8, LANES), f32),
            vm((4, reach + 8, LANES), f32),
            vm((4, reach + 8, LANES), f32),
            vm((4, reach + 8, LANES), f32),
            vm((4, reach + 8, LANES), f32),
            vm((5, reach + 8, LANES), f32),
            vm((16, 5, reach + 8, LANES), f32),
            vm((2, 5, reach + 8, LANES), f32),
            vm((max(last - 8, -(-height // 8) * 8) * 72, LANES), f32),
            vm((padded, 64, LANES), bf16),
            vm((4, tall_h, LANES), bf16),
            vm((2, 4, 8, LANES), bf16),
            vm((2, PASSES, 64, LANES), bf16),
            vm((2, 8, LANES), f32),
            vm((2, PASSES, 64, LANES), bf16),
            vm((2, 4, tall_h, LANES), bf16),
            vm((2, 3, 4, 8, LANES), bf16),
            vm((2, height, LANES), f32),
            vm((2, 3, 8, LANES), f32),
            vm((half, 2, 64, LANES), bf16),
            vm((ny, per, 2, 64, LANES), bf16),
            vm((ny, RANK, LANES), bf16),
            vm((ny, 8, LANES), f32),
            vm((nxc, LANES // nxc, LANES), f32),
            vm((nxc, LANES // nxc, LANES), f32),
            vm((nz, LANES // nxc, LANES), f32),
            vm((nxc, LANES // nxc, LANES), f32),
            vm((ny, per, RANK, LANES), bf16),
            vm((nxc, piece2, LANES), f32),
            vm((nxc, piece2, LANES), f32),
            vm((ny, piece2, LANES), f32),
            vm((nz, piece2, LANES), f32),
            vm((nxc, piece2, LANES), f32),
            vm((padded, RANK, LANES), bf16),
            vm((nx, 16, LANES), bf16),
            vm((nz, 16, LANES), bf16),
            vm((2, RANK, LANES), f32),
            vm((2, RANK, LANES), f32),
            vm((2, RANK, LANES), f32),
            pltpu.SemaphoreType.DMA((23, sems)),
            pltpu.SemaphoreType.DMA((23, sems)),
            pltpu.SemaphoreType.DMA,
        ],
        compiler_params=pltpu.CompilerParams(collective_id=0, has_side_effects=True),
        name="merge",
    )(residuals, diffusivity)


def project_kernel(solved_ref, modes_ref, out_ref):
    solved = solved_ref[...].T
    for r in range(out_ref.shape[0]):
        out_ref[r] = dot(solved, modes_ref[r], ((1,), (0,))).astype(jnp.bfloat16)


def project_call(solved, modes, height):
    return pl.pallas_call(
        project_kernel,
        out_shape=jax.ShapeDtypeStruct((height, 64, LANES), jnp.bfloat16),
        in_specs=[pl.BlockSpec(memory_space=pltpu.VMEM)] * 2,
        out_specs=pl.BlockSpec(memory_space=pltpu.VMEM),
        name="project",
    )(solved, modes)


def shards(residuals, diffusivity):
    solved, modes = merge_call(
        residuals.transpose(1, 0, 2), diffusivity,
        lax.axis_size("tm") // 2, lax.axis_size("lat"), lax.axis_size("lon"),
    )
    projected = project_call(solved, modes, residuals.shape[1])
    return projected.transpose(1, 0, 2)


def solution(mesh):
    return jax.shard_map(
        shards,
        mesh=mesh,
        in_specs=(P("tm", "lat", "lon"), P("lat", "lon")),
        out_specs=P("tm", "lat", "lon"),
        check_vma=False,
    )
```
